128 devices in a mesh: img: 16 (over z_lo, x, core), head: 2 (over z_hi), txt: 4 (over y).
Axes of the slice: x: 4, y: 4, z: 4 (z_hi: 2, z_lo: 2; z = z_hi * 2 + z_lo), core: 2. Of those that a mesh axis runs over, the one named last changes fastest.
Arguments:
- image_feats: bfloat16 [16384, 7680], P(('img', 'txt'), 'head'), may hold values from -6 to 6
- key_weight: bfloat16 [7680, 512], P('head'), may hold values from -0.0625 to 0.0625
- value_weight: bfloat16 [7680, 512], P('head'), may hold values from -0.0625 to 0.0625
- queries: bfloat16 [1024, 4096], P('txt', 'head'), may hold values from -21 to 21
- grad_out: bfloat16 [1024, 4096], P('txt', 'head'), may hold values from -768 to 768
- tile_image: int32 [128], P('img'), may hold values from 0 to 7, never falling along the last dimension, each value on 1 to 32 neighbouring positions
- text_sees: int32 [8, 8], replicated, may hold values from 0 to 1, as said below
Outputs:
- attn_out: bfloat16 [1024, 4096], P('txt', 'head')
- grad_feats: bfloat16 [16384, 7680], P(('img', 'txt'), 'head')
The draws below stay inside these ranges and needn't reach their ends.
Inputs may be any that keep to these rules, and one draw needn't show every extreme that they name: `text_sees`: every row holds at least one 1.
All inputs are finite; a program needn't handle non-finite values.
Results may differ from the reference program's by a relative error of at most 0.012.
The reference program's roundings to bfloat16 on the way (of `weights`) count: a program that leaves them out, or rounds other values in their place, can miss the bound.
Values may be sent and summed in bfloat16 or wider, within the bound.
No kernel may reach another device: no remote copies, remote signals or barrier semaphores. Data moves between devices by JAX's collectives and lax.ppermute only.
A program may use at most 128 MiB of HBM per device.

```python
import math
import jax
import jax.numpy as jnp
import numpy as np
from jax import lax

DV = 7680
HD = 128
KVH = 4
QH = 32
TILE = 128
TBLK = 128
IMAGES = 8
IMG = 16384
TXT = 1024
TILES = 128
TBLKS = 8
MOST = 32


def draw_queries(key, part):
    key_base, key_scale = jax.random.split(key, 2)
    shape = (TXT, QH * HD)
    row_scale = jnp.exp(jax.random.uniform(key_scale, (TXT, 1), jnp.float32, math.log(0.5), math.log(4.0)))
    base_values = jnp.clip(jax.random.normal(key_base, shape, jnp.float32), -4.0, 4.0)
    return (base_values * row_scale).astype(jnp.bfloat16)


def draw_text_sees(key, part):
    random_bits = jax.random.randint(key, (TBLKS, IMAGES), 0, 2)
    forced = jax.random.randint(jax.random.fold_in(key, 1), (TBLKS, 1), 0, IMAGES)
    forced_hit = (jnp.arange(IMAGES)[None, :] == forced).astype(jnp.int32)
    return jnp.maximum(random_bits, forced_hit).astype(jnp.int32)


def block_scale(own_key, dims, pieces, low, high):
    def one(axis_at, parts):
        steps = jax.random.uniform(jax.random.fold_in(jax.random.fold_in(own_key, 6), axis_at), (parts,), jnp.float32, low / len(pieces), high / len(pieces))
        return jnp.repeat(jnp.exp(steps), dims[axis_at] // parts).reshape((-1,) + (1,) * (len(dims) - axis_at - 1))

    loudness = one(*pieces[0])
    for cut in pieces[1:]:
        loudness = loudness * one(*cut)
    return loudness


def profile(count, total, limit, lean):
    weights = [(1 << 20) // math.isqrt(rank ** lean) + 1 for rank in range(2, count + 1)]
    surplus, counts = total - limit - (count - 1), [1] * (count - 1)
    while surplus > 0:
        movable = [i for i in range(count - 1) if counts[i] < limit]
        pool, remaining = sum([weights[i] for i in movable]), surplus
        for i in movable:
            more = min(limit - counts[i], max(1, remaining * weights[i] // pool), surplus)
            counts[i] = counts[i] + more
            surplus = surplus - more
    return np.array([limit] + counts)


def ragged_sizes(key, number_of, total, most, slope):
    if number_of == 2:
        one = jax.random.randint(key, (), max(1, total - most), min(most, total - 1) + 1)
        return jnp.stack([one, total - one])
    lengths = jnp.asarray(profile(number_of, total, most, slope), jnp.int32)
    pairs = (number_of - 1) // 2
    giver, sink = lengths[1:1 + 2 * pairs:2], lengths[2:2 + 2 * pairs:2]
    slack = jnp.minimum(giver - 1, most - sink)
    moved = jax.random.randint(jax.random.fold_in(key, 1), (pairs,), 0, 1 << 20) % (slack + 1)
    lengths = lengths.at[1:1 + 2 * pairs:2].set(giver - moved).at[2:2 + 2 * pairs:2].set(sink + moved)
    return lengths[jax.random.permutation(jax.random.fold_in(key, 2), number_of)]


def scatter_about(key, dims, deviation, limit, shards=(), kind=jnp.bfloat16):
    loudness = block_scale(key, dims, shards, -0.22, 0.18) if shards else 1.0
    values = jax.random.normal(key, dims, jnp.float32) * deviation * loudness
    return jnp.minimum(jnp.maximum(values, -limit), limit).astype(kind)


def setup_inputs(seed: int = 0) -> dict:
    splits = jax.random.split(jax.random.key(seed), 8)
    image_feats = scatter_about(splits[0], (IMG, DV), 1.0, 6.0, ((0, 64), (1, 2)))
    key_weight = scatter_about(splits[1], (DV, KVH * HD), DV ** -0.5, 0.0625, ((0, 2),))
    value_weight = scatter_about(splits[2], (DV, KVH * HD), DV ** -0.5, 0.0625, ((0, 2),))
    queries = draw_queries(jax.random.fold_in(splits[7], 71), 0)
    grad_out = scatter_about(splits[4], (TXT, QH * HD), 128.0, 768.0, ((0, 4), (1, 2)))
    tile_image = jnp.searchsorted(jnp.cumsum(ragged_sizes(splits[5], IMAGES, TILES, MOST, 2)), jnp.arange(TILES), side="right").astype(jnp.int32)
    text_sees = draw_text_sees(jax.random.fold_in(splits[7], 71), 0)
    return dict(image_feats=image_feats, key_weight=key_weight, value_weight=value_weight, queries=queries, grad_out=grad_out, tile_image=tile_image, text_sees=text_sees)


def attend_one(query, grad_head, key_head, value_head, allowed, scale_factor):
    scores = jnp.dot(query, key_head.T, preferred_element_type=jnp.float32) * scale_factor
    masked = jnp.where(allowed, scores, -1e+30)
    row_max = lax.optimization_barrier(jnp.max(masked, axis=1))
    weights = jnp.exp(masked - row_max[:, None]).astype(jnp.bfloat16)
    totals = lax.optimization_barrier(jnp.sum(weights, axis=1, dtype=jnp.float32))
    numerator = jnp.dot(weights, value_head, preferred_element_type=jnp.float32)
    output = (numerator / totals[:, None]).astype(jnp.bfloat16)
    log_total = row_max + jnp.log(totals)
    row_delta = lax.optimization_barrier(jnp.sum(grad_head.astype(jnp.float32) * output.astype(jnp.float32), axis=1))
    probabilities = jnp.exp(masked - log_total[:, None])
    grad_probs = jnp.dot(grad_head, value_head.T, preferred_element_type=jnp.float32)
    grad_scores = (probabilities * (grad_probs - row_delta[:, None]) * scale_factor).astype(jnp.bfloat16)
    value_grad = jnp.dot(probabilities.astype(jnp.bfloat16).T, grad_head, preferred_element_type=jnp.float32)
    key_grad = jnp.dot(grad_scores.T, query, preferred_element_type=jnp.float32)
    return (output, key_grad, value_grad)

def reference(image_feats, key_weight, value_weight, queries, grad_out, tile_image, text_sees):
    scale_factor = 1.0 / math.sqrt(HD)
    keys = jnp.dot(image_feats, key_weight, preferred_element_type=jnp.float32).astype(jnp.bfloat16)
    values = jnp.dot(image_feats, value_weight, preferred_element_type=jnp.float32).astype(jnp.bfloat16)
    block_allowed = text_sees[:, tile_image]
    allowed = jnp.repeat(jnp.repeat(block_allowed, TBLK, axis=0), TILE, axis=1) > 0
    repeats = QH // KVH
    query_heads = queries.reshape(TXT, KVH, repeats, HD).transpose(1, 2, 0, 3)
    grad_heads = grad_out.reshape(TXT, KVH, repeats, HD).transpose(1, 2, 0, 3)
    key_heads = keys.reshape(IMG, KVH, HD).transpose(1, 0, 2)
    value_heads = values.reshape(IMG, KVH, HD).transpose(1, 0, 2)

    def per_group(operands):
        group_queries, group_grads, key_head, value_head = operands

        def per_query(carry, pair):
            output, key_grad, value_grad = attend_one(pair[0], pair[1], key_head, value_head, allowed, scale_factor)
            return ((carry[0] + key_grad, carry[1] + value_grad), output)
        start = (jnp.zeros((IMG, HD), jnp.float32), jnp.zeros((IMG, HD), jnp.float32))
        summed, outputs = lax.scan(per_query, start, (group_queries, group_grads))
        return (outputs, summed[0], summed[1])
    outputs, key_grad, value_grad = lax.map(per_group, (query_heads, grad_heads, key_heads, value_heads))
    attn_out = outputs.transpose(2, 0, 1, 3).reshape(TXT, QH * HD)
    key_grad = key_grad.transpose(1, 0, 2).reshape(IMG, KVH * HD).astype(jnp.bfloat16)
    value_grad = value_grad.transpose(1, 0, 2).reshape(IMG, KVH * HD).astype(jnp.bfloat16)
    grad_feats = jnp.dot(key_grad, key_weight.T, preferred_element_type=jnp.float32)
    grad_feats = grad_feats + jnp.dot(value_grad, value_weight.T, preferred_element_type=jnp.float32)
    return (attn_out, grad_feats.astype(jnp.bfloat16))
```

```python
import math

import jax
import jax.numpy as jnp
from jax import lax
from jax.experimental import pallas as pl
from jax.experimental.pallas import tpu as pltpu
from jax.sharding import PartitionSpec as P

HD = 128
TILE = 128
TBLK = 128
BF = jnp.bfloat16
F32 = jnp.float32
SCALE = 1.0 / math.sqrt(HD)
C2 = SCALE * math.log2(math.e)
NEG = -1e30
TOP = 3e38
AXES = ("img", "head", "txt")
NT = (((1,), (1,)), ((), ()))


def dot_nt(a, b):
    return lax.dot_general(a, b, NT, preferred_element_type=F32)


def dot_nn(a, b):
    return jnp.dot(a, b, preferred_element_type=F32)


def moved(sizes, where):
    ni, nh, nt = sizes
    pairs = []
    for i in range(ni):
        for h in range(nh):
            for t in range(nt):
                a, b, c = where(i, h, t)
                pairs.append(((i * nh + h) * nt + t, (a * nh + b) * nt + c))
    return lambda x: lax.ppermute(x, AXES, pairs)


def spec(shape):
    zeros = (0,) * len(shape)
    return pl.BlockSpec(shape, lambda *_: zeros)


def project(idx, feats, weight, own_dtype, sent_dtype, name):
    rows, feat = feats.shape
    cols = weight.shape[1]
    steps = 5
    chunk = feat // steps

    def body(ix, x, w, own, oc, oh, ohc, acc):
        k = pl.program_id(0)
        part = dot_nn(x[...], w[...])

        @pl.when(k == 0)
        def _():
            acc[...] = part

        @pl.when(k > 0)
        def _():
            acc[...] += part

        @pl.when(k == steps - 1)
        def _():
            h = ix[0]
            c = ix[1]

            def piece(hh, cc):
                at = pl.multiple_of((hh * 2 + cc) * HD, HD)
                return acc[:, pl.ds(at, HD)]

            own[...] = piece(h, c).astype(own.dtype)
            oc[...] = piece(h, 1 - c).astype(oc.dtype)
            oh[...] = piece(1 - h, c).astype(oh.dtype)
            ohc[...] = piece(1 - h, 1 - c).astype(ohc.dtype)

    out = lambda dt: jax.ShapeDtypeStruct((rows, HD), dt)
    return pl.pallas_call(
        body,
        out_shape=(out(own_dtype), out(sent_dtype), out(sent_dtype), out(sent_dtype)),
        grid_spec=pltpu.PrefetchScalarGridSpec(
            num_scalar_prefetch=1,
            grid=(steps,),
            in_specs=[
                pl.BlockSpec((rows, chunk), lambda k, ix: (0, k)),
                pl.BlockSpec((chunk, cols), lambda k, ix: (k, 0)),
            ],
            out_specs=[spec((rows, HD))] * 4,
            scratch_shapes=[pltpu.VMEM((rows, cols), F32)],
        ),
        compiler_params=pltpu.CompilerParams(vmem_limit_bytes=24 << 20),
        name=name,
    )(idx, feats, weight)


def tile_cap(ix, tiles, sees, block, chunk, tile):
    half, j = divmod(tile, 2)
    shard = jnp.bitwise_xor(ix[2], chunk)
    image = tiles[half, shard * 2 + j]
    row = ix[2] * 2 + block
    return jnp.where(sees[row, image] > 0, jnp.float32(TOP), jnp.float32(NEG))


def forward(idx, tiles, sees, queries, grad_out, keys, values):
    rows = queries.shape[0]
    heads = 8
    width = heads * HD
    span = keys[0].shape[0]
    n = len(keys)
    total = span * n
    per = span // TILE

    def body(ix, tl, se, q, g, k0, k1, k2, k3, v0, v1, v2, v3, o_out, st_out, y_scr, va, stat):
        ks = (k0, k1, k2, k3)
        vs = (v0, v1, v2, v3)
        for j in range(n):
            va[j * span : (j + 1) * span, :HD] = vs[j][...]
        va[:, HD:] = jnp.ones((total, HD), BF)
        caps = [
            [tile_cap(ix, tl, se, b, j, e) for j in range(n) for e in range(per)]
            for b in range(2)
        ]
        lane = lax.broadcasted_iota(jnp.int32, (rows, HD), 1)
        st = jnp.zeros((rows, HD), F32)
        for h in range(heads):
            cols = slice(h * HD, (h + 1) * HD)
            slot = h % 2
            qh = q[:, cols]
            best = [None, None]
            for j in range(n):
                s = dot_nt(qh, ks[j][...]) * C2
                for b in range(2):
                    for e in range(per):
                        y = jnp.minimum(
                            s[b * TBLK : (b + 1) * TBLK, e * TILE : (e + 1) * TILE],
                            caps[b][j * per + e],
                        )
                        at = j * span + e * TILE
                        y_scr[slot, b * TBLK : (b + 1) * TBLK, at : at + TILE] = y
                        best[b] = y if best[b] is None else jnp.maximum(best[b], y)
            m = jnp.max(jnp.concatenate(best, axis=0), axis=1, keepdims=True)
            p = jnp.exp2(y_scr[slot] - m).astype(BF)
            r = dot_nn(p, va[...])
            den = r[:, HD:]
            o = r[:, :HD] / den
            o_out[:, :, cols] = o.astype(BF).reshape(8, rows // 8, HD)
            lse = m + jnp.log2(den)
            delta = jnp.sum(o * g[:, cols].astype(F32), axis=1, keepdims=True)
            st = jnp.where(lane == h, lse, st)
            st = jnp.where(lane == heads + h, delta, st)
        flat = st.T[: 2 * heads, :]
        for i in range(8):
            st_out[i] = flat

    own = lambda i, ix, tl, se: (0, ix[1])
    return pl.pallas_call(
        body,
        out_shape=(
            jax.ShapeDtypeStruct((8, rows // 8, width), BF),
            jax.ShapeDtypeStruct((8, 2 * heads, rows), F32),
        ),
        grid_spec=pltpu.PrefetchScalarGridSpec(
            num_scalar_prefetch=3,
            grid=(1,),
            in_specs=[pl.BlockSpec((rows, width), own)] * 2 + [spec((span, HD))] * 8,
            out_specs=[spec((8, rows // 8, width)), spec((8, 2 * heads, rows))],
            scratch_shapes=[
                pltpu.VMEM((2, rows, total), F32),
                pltpu.VMEM((total, 2 * HD), BF),
                pltpu.VMEM((rows, HD), F32),
            ],
        ),
        compiler_params=pltpu.CompilerParams(vmem_limit_bytes=40 << 20),
        name="fwd",
    )(idx, tiles, sees, queries, grad_out, *keys, *values)


def merge_weights(stats, heads):
    lses = [stats[i, :heads, :] for i in range(8)]
    top = lses[0]
    for x in lses[1:]:
        top = jnp.maximum(top, x)
    ws = [jnp.exp2(x - top) for x in lses]
    total = ws[0]
    for w in ws[1:]:
        total = total + w
    return top, ws, total


def combine(idx, parts, stats):
    _, share, width = parts.shape
    heads = width // HD
    rows = stats.shape[2]

    def body(ix, x, st, out, w_scr):
        _, ws, total = merge_weights(st, heads)
        inv = 1.0 / total
        stacked = jnp.concatenate([w * inv for w in ws] + [jnp.zeros((HD - 8 * heads, rows), F32)], axis=0)
        w_scr[...] = stacked.T
        w = w_scr[pl.ds(pl.multiple_of(ix[3] * share, share), share), :]
        for h in range(heads):
            cols = slice(h * HD, (h + 1) * HD)
            acc = jnp.zeros((share, HD), F32)
            for i in range(8):
                acc += x[i, :, cols].astype(F32) * w[:, i * heads + h : i * heads + h + 1]
            v = acc.astype(BF)
            for i in range(8):
                out[i, :, cols] = v

    return pl.pallas_call(
        body,
        out_shape=jax.ShapeDtypeStruct((8, share, width), BF),
        grid_spec=pltpu.PrefetchScalarGridSpec(
            num_scalar_prefetch=1,
            grid=(1,),
            in_specs=[spec(parts.shape), spec(stats.shape)],
            out_specs=spec((8, share, width)),
            scratch_shapes=[pltpu.VMEM((rows, HD), F32)],
        ),
        name="combine",
    )(idx, parts, stats)


def backward(idx, tiles, sees, queries, grad_out, key, value, stats, chunk, dtype):
    rows = queries.shape[0]
    heads = 8
    width = heads * HD
    span = key.shape[0]
    per = span // TILE

    def body(ix, tl, se, q, g, k, v, st, out, dk, dv):
        top, ws, total = merge_weights(st, heads)
        inv = 1.0 / total
        lse = top + jnp.log2(total)
        delta = ws[0] * st[0, heads:, :]
        for i in range(1, 8):
            delta += ws[i] * st[i, heads:, :]
        delta = delta * inv
        lane = lax.broadcasted_iota(jnp.int32, (1, rows), 1)
        caps = [
            jnp.where(
                lane < TBLK,
                tile_cap(ix, tl, se, 0, chunk, e),
                tile_cap(ix, tl, se, 1, chunk, e),
            )
            for e in range(per)
        ]
        kk = k[...]
        vv = v[...]
        for h in range(heads):
            cols = slice(h * HD, (h + 1) * HD)
            qh = q[:, cols]
            gh = g[:, cols]
            s = dot_nt(kk, qh) * C2
            d = dot_nt(vv, gh)
            lh = lse[h : h + 1, :]
            dh = delta[h : h + 1, :]
            ps = []
            ds = []
            for e in range(per):
                at = slice(e * TILE, (e + 1) * TILE)
                p = jnp.exp2(jnp.minimum(s[at, :], caps[e]) - lh)
                ps.append(p.astype(BF))
                ds.append((p * (d[at, :] - dh) * SCALE).astype(BF))
            pv = dot_nn(jnp.concatenate(ps, axis=0), gh)
            pk = dot_nn(jnp.concatenate(ds, axis=0), qh)
            if h == 0:
                dv[...] = pv
                dk[...] = pk
            else:
                dv[...] += pv
                dk[...] += pk
        out[:, :HD] = dk[...].astype(out.dtype)
        out[:, HD:] = dv[...].astype(out.dtype)

    own = lambda i, ix, tl, se: (0, ix[1])
    return pl.pallas_call(
        body,
        out_shape=jax.ShapeDtypeStruct((span, 2 * HD), dtype),
        grid_spec=pltpu.PrefetchScalarGridSpec(
            num_scalar_prefetch=3,
            grid=(1,),
            in_specs=[pl.BlockSpec((rows, width), own)] * 2
            + [spec((span, HD))] * 2
            + [spec(stats.shape)],
            out_specs=spec((span, 2 * HD)),
            scratch_shapes=[pltpu.VMEM((span, HD), F32)] * 2,
        ),
        compiler_params=pltpu.CompilerParams(vmem_limit_bytes=32 << 20),
        name=f"grads{chunk}",
    )(idx, tiles, sees, queries, grad_out, key, value, stats)


def feature_grad(idx, own, oc, oh, ohc, key_weight, value_weight):
    rows = own.shape[0]
    feat, cols = key_weight.shape
    steps = 5
    chunk = feat // steps

    def body(ix, a, b, c_, d_, wk, wv, out, both):
        @pl.when(pl.program_id(0) == 0)
        def _():
            h = ix[0]
            c = ix[1]

            def put(hh, cc, x):
                at = pl.multiple_of((hh * 2 + cc) * HD, HD)
                both[0, :, pl.ds(at, HD)] = x[:, :HD]
                both[1, :, pl.ds(at, HD)] = x[:, HD:]

            put(h, c, a)
            put(h, 1 - c, b)
            put(1 - h, c, c_)
            put(1 - h, 1 - c, d_)

        out[...] = (dot_nt(both[0], wk[...]) + dot_nt(both[1], wv[...])).astype(BF)

    piece = spec((rows, 2 * HD))
    return pl.pallas_call(
        body,
        out_shape=jax.ShapeDtypeStruct((rows, feat), BF),
        grid_spec=pltpu.PrefetchScalarGridSpec(
            num_scalar_prefetch=1,
            grid=(steps,),
            in_specs=[piece] * 4 + [pl.BlockSpec((chunk, cols), lambda k, ix: (k, 0))] * 2,
            out_specs=pl.BlockSpec((rows, chunk), lambda k, ix: (0, k)),
            scratch_shapes=[pltpu.VMEM((2, rows, cols), BF)],
        ),
        compiler_params=pltpu.CompilerParams(vmem_limit_bytes=24 << 20),
        name="feats",
    )(idx, own, oc, oh, ohc, key_weight, value_weight)


def solution(mesh):
    sizes = tuple(mesh.shape[a] for a in AXES)
    to_c = moved(sizes, lambda i, h, t: (i ^ 1, h, t))
    to_h = moved(sizes, lambda i, h, t: (i, 1 - h, t))
    to_hc = moved(sizes, lambda i, h, t: (i ^ 1, 1 - h, t))
    to_t = {k: moved(sizes, lambda i, h, t, k=k: (i, h, t ^ k)) for k in (1, 2, 3)}
    chips = [[m * 2 + c for m in range(8)] for c in range(2)]

    def swap8(x):
        return lax.all_to_all(x, "img", 0, 0, axis_index_groups=chips, tiled=True)

    def gathered(own):
        return [own] + [to_t[k](own) for k in (1, 2, 3)]

    def shards(image_feats, key_weight, value_weight, queries, grad_out, tile_image, text_sees):
        img = lax.axis_index("img")
        core = img % 2
        idx = jnp.stack([lax.axis_index("head"), core, lax.axis_index("txt"), img // 2]).astype(jnp.int32)
        tiles = jnp.stack([tile_image, to_c(tile_image)])

        def owned(weight, sent, name):
            own, c, h, hc = project(idx, image_feats, weight, F32, sent, name)
            h, c, hc = to_h(h), to_c(c), to_hc(hc)
            near = own + h.astype(F32)
            far = c.astype(F32) + hc.astype(F32)
            return jnp.concatenate([near.astype(BF), far.astype(BF)], axis=0)

        keys = gathered(owned(key_weight, F32, "keys"))
        values = gathered(owned(value_weight, BF, "values"))
        parts, stats = forward(idx, tiles, text_sees, queries, grad_out, keys, values)
        stats = swap8(stats)

        def grads(k, dtype):
            return backward(idx, tiles, text_sees, queries, grad_out, keys[k], values[k], stats, k, dtype)

        far = [to_t[k](grads(k, BF)) for k in (2, 1, 3)]
        total = grads(0, F32)
        for x in far:
            total = total + x.astype(F32)
        total = total.astype(BF)
        rows = total.shape[0] // 2
        near, other = total[:rows], total[rows:]
        grad_feats = feature_grad(
            idx, near, to_c(other), to_h(near), to_hc(other), key_weight, value_weight
        )

        merged = combine(idx, swap8(parts), stats)
        mine = swap8(merged).reshape(queries.shape[0], -1)
        theirs = to_c(mine)
        attn_out = jnp.where(
            core == 0,
            jnp.concatenate([mine, theirs], axis=1),
            jnp.concatenate([theirs, mine], axis=1),
        )
        return attn_out, grad_feats

    placed = (
        P(("img", "txt"), "head"),
        P("head", None),
        P("head", None),
        P("txt", "head"),
        P("txt", "head"),
        P("img"),
        P(),
    )
    return jax.shard_map(
        shards,
        mesh=mesh,
        in_specs=placed,
        out_specs=(P("txt", "head"), P(("img", "txt"), "head")),
        check_vma=False,
    )
```

```python
import math

import jax
import jax.numpy as jnp
from jax import lax
from jax.experimental import pallas as pl
from jax.experimental.pallas import tpu as pltpu
from jax.sharding import PartitionSpec as P

HD = 128
TILE = 128
TBLK = 128
BF = jnp.bfloat16
F32 = jnp.float32
SCALE = 1.0 / math.sqrt(HD)
C2 = SCALE * math.log2(math.e)
NEG = -1e30
TOP = 3e38
AXES = ("img", "head", "txt")
NT = (((1,), (1,)), ((), ()))


def dot_nt(a, b):
    return lax.dot_general(a, b, NT, preferred_element_type=F32)


def dot_nn(a, b):
    return jnp.dot(a, b, preferred_element_type=F32)


def moved(sizes, where):
    ni, nh, nt = sizes
    pairs = []
    for i in range(ni):
        for h in range(nh):
            for t in range(nt):
                a, b, c = where(i, h, t)
                pairs.append(((i * nh + h) * nt + t, (a * nh + b) * nt + c))
    return lambda x: lax.ppermute(x, AXES, pairs)


def cost(us):
    return pl.CostEstimate(flops=int(us * 1.1e9), transcendentals=0, bytes_accessed=1 << 16)


def spec(shape):
    zeros = (0,) * len(shape)
    return pl.BlockSpec(shape, lambda *_: zeros)


def in_hbm(x):
    return pltpu.with_memory_space_constraint(x, pltpu.HBM)


def project(idx, feats, key_weight, value_weight):
    rows, feat = feats.shape
    cols = key_weight.shape[1]
    steps = 5
    chunk = feat // steps

    def body(ix, x, wk, wv, own, oc, oh, ohc, acc):
        k = pl.program_id(0)
        key = dot_nn(x[...], wk[...])
        value = dot_nn(x[...], wv[...])

        @pl.when(k == 0)
        def _():
            acc[0] = key
            acc[1] = value

        @pl.when(k > 0)
        def _():
            acc[0] += key
            acc[1] += value

        @pl.when(k == steps - 1)
        def _():
            h = ix[0]
            c = ix[1]

            def piece(which, hh, cc):
                at = pl.multiple_of((hh * 2 + cc) * HD, HD)
                return acc[which, :, pl.ds(at, HD)]

            own[:, :HD] = piece(0, h, c)
            own[:, HD:] = piece(1, h, c)
            for ref, hh, cc in ((oh, 1 - h, c), (ohc, 1 - h, 1 - c), (oc, h, 1 - c)):
                kp = piece(0, hh, cc)
                high = kp.astype(BF)
                ref[:, :HD] = high
                ref[:, HD : 2 * HD] = (kp - high.astype(F32)).astype(BF)
                ref[:, 2 * HD :] = piece(1, hh, cc).astype(BF)

    sent = jax.ShapeDtypeStruct((rows, 3 * HD), BF)
    return pl.pallas_call(
        body,
        out_shape=(jax.ShapeDtypeStruct((rows, 2 * HD), F32), sent, sent, sent),
        grid_spec=pltpu.PrefetchScalarGridSpec(
            num_scalar_prefetch=1,
            grid=(steps,),
            in_specs=[
                pl.BlockSpec((rows, chunk), lambda k, ix: (0, k)),
                pl.BlockSpec((chunk, cols), lambda k, ix: (k, 0)),
                pl.BlockSpec((chunk, cols), lambda k, ix: (k, 0)),
            ],
            out_specs=[spec((rows, 2 * HD))] + [spec((rows, 3 * HD))] * 3,
            scratch_shapes=[pltpu.VMEM((2, rows, cols), F32)],
        ),
        compiler_params=pltpu.CompilerParams(vmem_limit_bytes=24 << 20),
        name="project",
        cost_estimate=cost(4),
    )(idx, in_hbm(feats), in_hbm(key_weight), in_hbm(value_weight))


def tile_cap(ix, tiles, sees, block, chunk, tile):
    half, j = divmod(tile, 2)
    shard = jnp.bitwise_xor(ix[2], chunk)
    image = tiles[half, shard * 2 + j]
    row = ix[2] * 2 + block
    return jnp.where(sees[row, image] > 0, jnp.float32(TOP), jnp.float32(NEG))


def forward(idx, tiles, sees, queries, grad_out, kvs):
    rows = queries.shape[0]
    heads = 8
    width = heads * HD
    span = kvs[0].shape[0]
    n = len(kvs)
    total = span * n
    share = rows // 8
    per = span // TILE

    def body(ix, tl, se, q, g, k0, k1, k2, k3, out, y_scr, va):
        ks = (k0, k1, k2, k3)
        for j in range(n):
            va[j * span : (j + 1) * span, :HD] = ks[j][:, HD:]
        va[:, HD:] = jnp.ones((total, HD), BF)
        caps = [
            [tile_cap(ix, tl, se, b, j, e) for j in range(n) for e in range(per)]
            for b in range(2)
        ]
        lane = lax.broadcasted_iota(jnp.int32, (rows, HD), 1)
        st = jnp.zeros((rows, HD), F32)
        for h in range(heads):
            cols = slice(h * HD, (h + 1) * HD)
            slot = h % 2
            qh = q[:, cols]
            best = [None, None]
            for j in range(n):
                s = dot_nt(qh, ks[j][:, :HD]) * C2
                for b in range(2):
                    for e in range(per):
                        y = jnp.minimum(
                            s[b * TBLK : (b + 1) * TBLK, e * TILE : (e + 1) * TILE],
                            caps[b][j * per + e],
                        )
                        at = j * span + e * TILE
                        y_scr[slot, b * TBLK : (b + 1) * TBLK, at : at + TILE] = y
                        best[b] = y if best[b] is None else jnp.maximum(best[b], y)
            m = jnp.max(jnp.concatenate(best, axis=0), axis=1, keepdims=True)
            p = jnp.exp2(y_scr[slot] - m).astype(BF)
            r = dot_nn(p, va[...])
            den = r[:, HD:]
            o = r[:, :HD] / den
            out[:, :share, cols] = o.astype(BF).reshape(8, share, HD)
            lse = m + jnp.log2(den)
            delta = jnp.sum(o * g[:, cols].astype(F32), axis=1, keepdims=True)
            st = jnp.where(lane == h, lse, st)
            st = jnp.where(lane == heads + h, delta, st)
        left = st.T[: 2 * heads, :]
        terms = []
        for _ in range(3):
            terms.append(left.astype(BF))
            left = left - terms[-1].astype(F32)
        note = jnp.concatenate(terms + [jnp.zeros((2 * heads, width - 3 * rows), BF)], axis=1)
        for i in range(8):
            out[i, share:, :] = note

    own = lambda i, ix, tl, se: (0, ix[1])
    return pl.pallas_call(
        body,
        out_shape=jax.ShapeDtypeStruct((8, share + 2 * heads, width), BF),
        grid_spec=pltpu.PrefetchScalarGridSpec(
            num_scalar_prefetch=3,
            grid=(1,),
            in_specs=[pl.BlockSpec((rows, width), own)] * 2 + [spec((span, 2 * HD))] * 4,
            out_specs=spec((8, share + 2 * heads, width)),
            scratch_shapes=[
                pltpu.VMEM((2, rows, total), F32),
                pltpu.VMEM((total, 2 * HD), BF),
            ],
        ),
        compiler_params=pltpu.CompilerParams(vmem_limit_bytes=40 << 20),
        name="fwd",
        cost_estimate=cost(7),
    )(idx, tiles, sees, queries, grad_out, *kvs)


def merge_weights(note, heads, rows):
    stats = []
    for i in range(8):
        x = note[i].astype(F32)
        stats.append(x[:, :rows] + x[:, rows : 2 * rows] + x[:, 2 * rows : 3 * rows])
    top = stats[0][:heads]
    for x in stats[1:]:
        top = jnp.maximum(top, x[:heads])
    ws = [jnp.exp2(x[:heads] - top) for x in stats]
    total = ws[0]
    delta = ws[0] * stats[0][heads:]
    for w, x in zip(ws[1:], stats[1:]):
        total = total + w
        delta = delta + w * x[heads:]
    inv = 1.0 / total
    return top + jnp.log2(total), delta * inv, [w * inv for w in ws]


def merge_parts(ix, x, ws, out, w_scr):
    _, share, width = x.shape
    heads = width // HD
    rows = w_scr.shape[0]
    pad = [jnp.zeros((HD - 8 * heads, rows), F32)]
    w_scr[...] = jnp.concatenate(ws + pad, axis=0).T
    w = w_scr[pl.ds(pl.multiple_of(ix[3] * share, share), share), :]
    for h in range(heads):
        cols = slice(h * HD, (h + 1) * HD)
        acc = jnp.zeros((share, HD), F32)
        for i in range(8):
            acc += x[i, :, cols].astype(F32) * w[:, i * heads + h : i * heads + h + 1]
        out[:, cols] = acc.astype(BF)


def backward(idx, tiles, sees, queries, grad_out, kv, notes, chunk, dtype, merging=False):
    rows = queries.shape[0]
    heads = 8
    width = heads * HD
    span = kv.shape[0]
    per = span // TILE

    def body(ix, tl, se, q, g, kv_ref, st, *refs):
        lse, delta, ws = merge_weights(st, heads, rows)
        if merging:
            x, out, merged, dk, dv, w_scr = refs
            merge_parts(ix, x, ws, merged, w_scr)
        else:
            out, dk, dv = refs
        lane = lax.broadcasted_iota(jnp.int32, (1, rows), 1)
        caps = [
            jnp.where(
                lane < TBLK,
                tile_cap(ix, tl, se, 0, chunk, e),
                tile_cap(ix, tl, se, 1, chunk, e),
            )
            for e in range(per)
        ]
        kk = kv_ref[:, :HD]
        vv = kv_ref[:, HD:]
        for h in range(heads):
            cols = slice(h * HD, (h + 1) * HD)
            qh = q[:, cols]
            gh = g[:, cols]
            s = dot_nt(kk, qh) * C2
            d = dot_nt(vv, gh)
            lh = lse[h : h + 1, :]
            dh = delta[h : h + 1, :]
            ps = []
            ds = []
            for e in range(per):
                at = slice(e * TILE, (e + 1) * TILE)
                p = jnp.exp2(jnp.minimum(s[at, :], caps[e]) - lh)
                ps.append(p.astype(BF))
                ds.append((p * (d[at, :] - dh) * SCALE).astype(BF))
            pv = dot_nn(jnp.concatenate(ps, axis=0), gh)
            pk = dot_nn(jnp.concatenate(ds, axis=0), qh)
            if h == 0:
                dv[...] = pv
                dk[...] = pk
            else:
                dv[...] += pv
                dk[...] += pk
        out[:, :HD] = dk[...].astype(out.dtype)
        out[:, HD:] = dv[...].astype(out.dtype)

    own = lambda i, ix, tl, se: (0, ix[1])
    out_shape = [jax.ShapeDtypeStruct((span, 2 * HD), dtype)]
    share = rows // 8
    in_specs = [pl.BlockSpec((rows, width), own)] * 2 + [
        spec((span, 2 * HD)),
        pl.BlockSpec((8, 2 * heads, width), lambda *_: (0, share // (2 * heads), 0)),
    ]
    out_specs = [spec((span, 2 * HD))]
    scratch = [pltpu.VMEM((span, HD), F32)] * 2
    more = []
    if merging:
        more = [notes]
        in_specs.append(spec((8, share, width)))
        out_shape.append(jax.ShapeDtypeStruct((share, width), BF))
        out_specs.append(spec((share, width)))
        scratch.append(pltpu.VMEM((rows, HD), F32))
    return pl.pallas_call(
        body,
        out_shape=out_shape,
        grid_spec=pltpu.PrefetchScalarGridSpec(
            num_scalar_prefetch=3,
            grid=(1,),
            in_specs=in_specs,
            out_specs=out_specs,
            scratch_shapes=scratch,
        ),
        compiler_params=pltpu.CompilerParams(vmem_limit_bytes=32 << 20),
        name=f"grads{chunk}",
        cost_estimate=cost(3),
    )(idx, tiles, sees, queries, grad_out, kv, notes, *more)


def feature_grad(idx, own, oc, oh, ohc, key_weight, value_weight, gathered):
    rows = own.shape[0]
    feat, cols = key_weight.shape
    steps = 5
    chunk = feat // steps
    chips, cores, share, half = gathered.shape

    def body(ix, a, b, c_, d_, wk, wv, all_ref, out, attn, both, sems):
        h = ix[0]
        c = ix[1]
        step = pl.program_id(0)

        def place(cc):
            return pltpu.make_async_copy(
                all_ref.at[:, cc], attn.at[:, :, cc * half : (cc + 1) * half], sems.at[cc]
            )

        @pl.when(step == 0)
        def _():
            for cc in range(cores):
                place(cc).start()

            def put(hh, cc, x):
                at = pl.multiple_of((hh * 2 + cc) * HD, HD)
                both[0, :, pl.ds(at, HD)] = x[:, :HD]
                both[1, :, pl.ds(at, HD)] = x[:, HD:]

            put(h, c, a)
            put(h, 1 - c, b)
            put(1 - h, c, c_)
            put(1 - h, 1 - c, d_)

        out[...] = (dot_nt(both[0], wk[...]) + dot_nt(both[1], wv[...])).astype(BF)

        @pl.when(step == steps - 1)
        def _():
            for cc in range(cores):
                place(cc).wait()

    piece = spec((rows, 2 * HD))
    whole = pl.BlockSpec(memory_space=pltpu.HBM)
    return pl.pallas_call(
        body,
        out_shape=(
            jax.ShapeDtypeStruct((rows, feat), BF),
            jax.ShapeDtypeStruct((chips, share, cores * half), BF),
        ),
        grid_spec=pltpu.PrefetchScalarGridSpec(
            num_scalar_prefetch=1,
            grid=(steps,),
            in_specs=[piece] * 4
            + [pl.BlockSpec((chunk, cols), lambda k, ix: (k, 0))] * 2
            + [whole],
            out_specs=[pl.BlockSpec((rows, chunk), lambda k, ix: (0, k)), whole],
            scratch_shapes=[pltpu.VMEM((2, rows, cols), BF), pltpu.SemaphoreType.DMA((2,))],
        ),
        compiler_params=pltpu.CompilerParams(vmem_limit_bytes=24 << 20),
        name="feats",
        cost_estimate=cost(4),
    )(idx, own, oc, oh, ohc, in_hbm(key_weight), in_hbm(value_weight), gathered)


def solution(mesh):
    sizes = tuple(mesh.shape[a] for a in AXES)
    to_c = moved(sizes, lambda i, h, t: (i ^ 1, h, t))
    to_h = moved(sizes, lambda i, h, t: (i, 1 - h, t))
    to_hc = moved(sizes, lambda i, h, t: (i ^ 1, 1 - h, t))
    to_t = {k: moved(sizes, lambda i, h, t, k=k: (i, h, t ^ k)) for k in (1, 2, 3)}
    chips = [[m * 2 + c for m in range(8)] for c in range(2)]

    def swap8(x):
        return lax.all_to_all(x, "img", 0, 0, axis_index_groups=chips, tiled=True)

    def gathered(own):
        return [own] + [to_t[k](own) for k in (1, 2, 3)]

    def shards(image_feats, key_weight, value_weight, queries, grad_out, tile_image, text_sees):
        img = lax.axis_index("img")
        core = img % 2
        idx = jnp.stack([lax.axis_index("head"), core, lax.axis_index("txt"), img // 2]).astype(jnp.int32)
        tiles = jnp.stack([tile_image, to_c(tile_image)])

        own, c, h, hc = project(idx, image_feats, key_weight, value_weight)
        h, hc, c = to_h(h), to_hc(hc), to_c(c)

        def wide(x):
            x = x.astype(F32)
            return x[:, :HD] + x[:, HD : 2 * HD], x[:, 2 * HD :]

        hk, hv = wide(h)
        ck, cv = wide(c)
        hck, hcv = wide(hc)
        near = jnp.concatenate([own[:, :HD] + hk, own[:, HD:] + hv], axis=1).astype(BF)
        far = jnp.concatenate([ck + hck, cv + hcv], axis=1).astype(BF)
        kvs = gathered(jnp.concatenate([near, far], axis=0))
        notes = swap8(forward(idx, tiles, text_sees, queries, grad_out, kvs))

        def grads(k, dtype, merging=False):
            return backward(idx, tiles, text_sees, queries, grad_out, kvs[k], notes, k, dtype, merging)

        far = []
        for k in (2, 1, 3):
            if k == 2:
                sent, merged = grads(k, BF, True)
                every = lax.all_gather(merged, "img").reshape(8, 2, *merged.shape)
            else:
                (sent,) = grads(k, BF)
            far.append(to_t[k](sent))
        (total,) = grads(0, F32)
        for x in far:
            total = total + x.astype(F32)
        total = total.astype(BF)
        rows = total.shape[0] // 2
        near, other = total[:rows], total[rows:]
        grad_feats, attn_out = feature_grad(
            idx, near, to_c(other), to_h(near), to_hc(other), key_weight, value_weight, every
        )
        return attn_out.reshape(queries.shape), grad_feats

    placed = (
        P(("img", "txt"), "head"),
        P("head", None),
        P("head", None),
        P("txt", "head"),
        P("txt", "head"),
        P("img"),
        P(),
    )
    return jax.shard_map(
        shards,
        mesh=mesh,
        in_specs=placed,
        out_specs=(P("txt", "head"), P(("img", "txt"), "head")),
        check_vma=False,
    )
```

```python
import math

import jax
import jax.numpy as jnp
from jax import lax
from jax.experimental import pallas as pl
from jax.experimental.pallas import tpu as pltpu
from jax.sharding import PartitionSpec as P

HD = 128
TILE = 128
TBLK = 128
BF = jnp.bfloat16
F32 = jnp.float32
SCALE = 1.0 / math.sqrt(HD)
C2 = SCALE * math.log2(math.e)
NEG = -1e30
TOP = 3e38
AXES = ("img", "head", "txt")
NT = (((1,), (1,)), ((), ()))


def dot_nt(a, b):
    return lax.dot_general(a, b, NT, preferred_element_type=F32)


def dot_nn(a, b):
    return jnp.dot(a, b, preferred_element_type=F32)


def moved(sizes, where):
    ni, nh, nt = sizes
    pairs = []
    for i in range(ni):
        for h in range(nh):
            for t in range(nt):
                a, b, c = where(i, h, t)
                pairs.append(((i * nh + h) * nt + t, (a * nh + b) * nt + c))
    return lambda x: lax.ppermute(x, AXES, pairs)


def cost(us):
    return pl.CostEstimate(flops=int(us * 1.1e9), transcendentals=0, bytes_accessed=1 << 16)


def spec(shape):
    zeros = (0,) * len(shape)
    return pl.BlockSpec(shape, lambda *_: zeros)


def in_hbm(x):
    return pltpu.with_memory_space_constraint(x, pltpu.HBM)


def project(idx, feats, key_weight, value_weight):
    rows, feat = feats.shape
    cols = key_weight.shape[1]
    steps = 5
    chunk = feat // steps

    def body(ix, x_hbm, wk_hbm, wv_hbm, own, oc, oh, ohc, x, wk, wv, acc, sems):
        copies = []
        for s in range(steps):
            at = slice(s * chunk, (s + 1) * chunk)
            copies.append(
                (
                    pltpu.make_async_copy(x_hbm.at[:, at], x.at[s], sems.at[0, s]),
                    pltpu.make_async_copy(wk_hbm.at[at, :], wk.at[s], sems.at[1, s]),
                    pltpu.make_async_copy(wv_hbm.at[at, :], wv.at[s], sems.at[2, s]),
                )
            )
            for copy in copies[s]:
                copy.start()
        for s in range(steps):
            for copy in copies[s]:
                copy.wait()
            key = dot_nn(x[s], wk[s])
            value = dot_nn(x[s], wv[s])
            if s == 0:
                acc[0] = key
                acc[1] = value
            else:
                acc[0] += key
                acc[1] += value
        h = ix[0]
        c = ix[1]

        def piece(which, hh, cc):
            at = pl.multiple_of((hh * 2 + cc) * HD, HD)
            return acc[which, :, pl.ds(at, HD)]

        own[:, :HD] = piece(0, h, c)
        own[:, HD:] = piece(1, h, c)
        for ref, hh, cc in ((oh, 1 - h, c), (ohc, 1 - h, 1 - c), (oc, h, 1 - c)):
            kp = piece(0, hh, cc)
            high = kp.astype(BF)
            ref[:, :HD] = high
            ref[:, HD : 2 * HD] = (kp - high.astype(F32)).astype(BF)
            ref[:, 2 * HD :] = piece(1, hh, cc).astype(BF)

    sent = jax.ShapeDtypeStruct((rows, 3 * HD), BF)
    return pl.pallas_call(
        body,
        out_shape=(jax.ShapeDtypeStruct((rows, 2 * HD), F32), sent, sent, sent),
        grid_spec=pltpu.PrefetchScalarGridSpec(
            num_scalar_prefetch=1,
            grid=(1,),
            in_specs=[pl.BlockSpec(memory_space=pltpu.HBM)] * 3,
            out_specs=[spec((rows, 2 * HD))] + [spec((rows, 3 * HD))] * 3,
            scratch_shapes=[
                pltpu.VMEM((steps, rows, chunk), BF),
                pltpu.VMEM((steps, chunk, cols), BF),
                pltpu.VMEM((steps, chunk, cols), BF),
                pltpu.VMEM((2, rows, cols), F32),
                pltpu.SemaphoreType.DMA((3, steps)),
            ],
        ),
        compiler_params=pltpu.CompilerParams(vmem_limit_bytes=24 << 20),
        name="project",
        cost_estimate=cost(4),
    )(idx, in_hbm(feats), in_hbm(key_weight), in_hbm(value_weight))


def tile_cap(ix, tiles, sees, block, chunk, tile):
    half, j = divmod(tile, 2)
    shard = jnp.bitwise_xor(ix[2], chunk)
    image = tiles[half, shard * 2 + j]
    row = ix[2] * 2 + block
    return jnp.where(sees[row, image] > 0, jnp.float32(TOP), jnp.float32(NEG))


def forward(idx, tiles, sees, queries, grad_out, kvs):
    rows = queries.shape[0]
    heads = 8
    width = heads * HD
    span = kvs[0].shape[0]
    n = len(kvs)
    total = span * n
    share = rows // 8
    per = span // TILE

    def body(ix, tl, se, q, g, k0, k1, k2, k3, out, st_out, y_scr, va):
        ks = (k0, k1, k2, k3)
        for j in range(n):
            va[j * span : (j + 1) * span, :HD] = ks[j][:, HD:]
        va[:, HD:] = jnp.ones((total, HD), BF)
        caps = [
            [tile_cap(ix, tl, se, b, j, e) for j in range(n) for e in range(per)]
            for b in range(2)
        ]
        lane = lax.broadcasted_iota(jnp.int32, (rows, HD), 1)
        st = jnp.zeros((rows, HD), F32)
        for h in range(heads):
            cols = slice(h * HD, (h + 1) * HD)
            slot = h % 2
            qh = q[:, cols]
            best = [None, None]
            for j in range(n):
                s = dot_nt(qh, ks[j][:, :HD]) * C2
                for b in range(2):
                    for e in range(per):
                        y = jnp.minimum(
                            s[b * TBLK : (b + 1) * TBLK, e * TILE : (e + 1) * TILE],
                            caps[b][j * per + e],
                        )
                        at = j * span + e * TILE
                        y_scr[slot, b * TBLK : (b + 1) * TBLK, at : at + TILE] = y
                        best[b] = y if best[b] is None else jnp.maximum(best[b], y)
            m = jnp.max(jnp.concatenate(best, axis=0), axis=1, keepdims=True)
            p = jnp.exp2(y_scr[slot] - m).astype(BF)
            r = dot_nn(p, va[...])
            den = r[:, HD:]
            o = r[:, :HD] / den
            out[:, :, cols] = o.astype(BF).reshape(8, share, HD)
            lse = m + jnp.log2(den)
            delta = jnp.sum(o * g[:, cols].astype(F32), axis=1, keepdims=True)
            st = jnp.where(lane == h, lse, st)
            st = jnp.where(lane == heads + h, delta, st)
        flat = st.T[: 2 * heads, :]
        for i in range(8):
            st_out[i] = flat

    own = lambda i, ix, tl, se: (0, ix[1])
    return pl.pallas_call(
        body,
        out_shape=(
            jax.ShapeDtypeStruct((8, share, width), BF),
            jax.ShapeDtypeStruct((8, 2 * heads, rows), F32),
        ),
        grid_spec=pltpu.PrefetchScalarGridSpec(
            num_scalar_prefetch=3,
            grid=(1,),
            in_specs=[pl.BlockSpec((rows, width), own)] * 2 + [spec((span, 2 * HD))] * 4,
            out_specs=[spec((8, share, width)), spec((8, 2 * heads, rows))],
            scratch_shapes=[
                pltpu.VMEM((2, rows, total), F32),
                pltpu.VMEM((total, 2 * HD), BF),
            ],
        ),
        compiler_params=pltpu.CompilerParams(vmem_limit_bytes=40 << 20),
        name="fwd",
        cost_estimate=cost(7),
    )(idx, tiles, sees, queries, grad_out, *kvs)


def merge_weights(st, heads):
    stats = [st[i] for i in range(8)]
    top = stats[0][:heads]
    for x in stats[1:]:
        top = jnp.maximum(top, x[:heads])
    ws = [jnp.exp2(x[:heads] - top) for x in stats]
    total = ws[0]
    delta = ws[0] * stats[0][heads:]
    for w, x in zip(ws[1:], stats[1:]):
        total = total + w
        delta = delta + w * x[heads:]
    inv = 1.0 / total
    return top + jnp.log2(total), delta * inv, [w * inv for w in ws]


def merge_parts(ix, x, ws, out, w_scr):
    _, share, width = x.shape
    heads = width // HD
    rows = w_scr.shape[0]
    pad = [jnp.zeros((HD - 8 * heads, rows), F32)]
    w_scr[...] = jnp.concatenate(ws + pad, axis=0).T
    w = w_scr[pl.ds(pl.multiple_of(ix[3] * share, share), share), :]
    for h in range(heads):
        cols = slice(h * HD, (h + 1) * HD)
        acc = jnp.zeros((share, HD), F32)
        for i in range(8):
            acc += x[i, :, cols].astype(F32) * w[:, i * heads + h : i * heads + h + 1]
        v = acc.astype(BF)
        for i in range(8):
            out[i, :, cols] = v


def backward(idx, tiles, sees, queries, grad_out, kv, stats, chunk, dtype, parts=None):
    rows = queries.shape[0]
    heads = 8
    width = heads * HD
    span = kv.shape[0]
    per = span // TILE

    def body(ix, tl, se, q, g, kv_ref, st, *refs):
        lse, delta, ws = merge_weights(st, heads)
        if parts is None:
            out, dk, dv = refs
        else:
            x, out, merged, dk, dv, w_scr = refs
            merge_parts(ix, x, ws, merged, w_scr)
        lane = lax.broadcasted_iota(jnp.int32, (1, rows), 1)
        caps = [
            jnp.where(
                lane < TBLK,
                tile_cap(ix, tl, se, 0, chunk, e),
                tile_cap(ix, tl, se, 1, chunk, e),
            )
            for e in range(per)
        ]
        kk = kv_ref[:, :HD]
        vv = kv_ref[:, HD:]
        for h in range(heads):
            cols = slice(h * HD, (h + 1) * HD)
            qh = q[:, cols]
            gh = g[:, cols]
            s = dot_nt(kk, qh) * C2
            d = dot_nt(vv, gh)
            lh = lse[h : h + 1, :]
            dh = delta[h : h + 1, :]
            ps = []
            ds = []
            for e in range(per):
                at = slice(e * TILE, (e + 1) * TILE)
                p = jnp.exp2(jnp.minimum(s[at, :], caps[e]) - lh)
                ps.append(p.astype(BF))
                ds.append((p * (d[at, :] - dh) * SCALE).astype(BF))
            pv = dot_nn(jnp.concatenate(ps, axis=0), gh)
            pk = dot_nn(jnp.concatenate(ds, axis=0), qh)
            if h == 0:
                dv[...] = pv
                dk[...] = pk
            else:
                dv[...] += pv
                dk[...] += pk
        out[:, :HD] = dk[...].astype(out.dtype)
        out[:, HD:] = dv[...].astype(out.dtype)

    own = lambda i, ix, tl, se: (0, ix[1])
    out_shape = [jax.ShapeDtypeStruct((span, 2 * HD), dtype)]
    in_specs = [pl.BlockSpec((rows, width), own)] * 2 + [spec((span, 2 * HD)), spec(stats.shape)]
    out_specs = [spec((span, 2 * HD))]
    scratch = [pltpu.VMEM((span, HD), F32)] * 2
    more = []
    if parts is not None:
        more = [parts]
        in_specs.append(spec(parts.shape))
        out_shape.append(jax.ShapeDtypeStruct(parts.shape, BF))
        out_specs.append(spec(parts.shape))
        scratch.append(pltpu.VMEM((rows, HD), F32))
    return pl.pallas_call(
        body,
        out_shape=out_shape,
        grid_spec=pltpu.PrefetchScalarGridSpec(
            num_scalar_prefetch=3,
            grid=(1,),
            in_specs=in_specs,
            out_specs=out_specs,
            scratch_shapes=scratch,
        ),
        compiler_params=pltpu.CompilerParams(vmem_limit_bytes=32 << 20),
        name=f"grads{chunk}",
        cost_estimate=cost(3),
    )(idx, tiles, sees, queries, grad_out, kv, stats, *more)


def feature_grad(idx, own, oc, oh, ohc, key_weight, value_weight, mine, theirs):
    rows = own.shape[0]
    feat, cols = key_weight.shape
    steps = 5
    chunk = feat // steps
    half = mine.shape[1]

    def body(ix, a, b, c_, d_, wk_hbm, wv_hbm, m_ref, t_ref, out_hbm, attn, wk, wv, both, out, sems):
        h = ix[0]
        c = ix[1]

        def load(s):
            at = slice(s * chunk, (s + 1) * chunk)
            return (
                pltpu.make_async_copy(wk_hbm.at[at, :], wk.at[s], sems.at[0, s]),
                pltpu.make_async_copy(wv_hbm.at[at, :], wv.at[s], sems.at[1, s]),
            )

        def place(src, cc, s):
            at = pl.multiple_of(cc * half, half)
            return pltpu.make_async_copy(src, attn.at[:, pl.ds(at, half)], sems.at[3, s])

        def store(s):
            at = slice(s * chunk, (s + 1) * chunk)
            return pltpu.make_async_copy(out.at[s], out_hbm.at[:, at], sems.at[2, s])

        for s in range(steps):
            for copy in load(s):
                copy.start()
        place(m_ref, c, 0).start()
        place(t_ref, 1 - c, 1).start()

        def put(hh, cc, x):
            at = pl.multiple_of((hh * 2 + cc) * HD, HD)
            both[0, :, pl.ds(at, HD)] = x[:, :HD]
            both[1, :, pl.ds(at, HD)] = x[:, HD:]

        put(h, c, a)
        put(h, 1 - c, b)
        put(1 - h, c, c_)
        put(1 - h, 1 - c, d_)
        for s in range(steps):
            for copy in load(s):
                copy.wait()
            out[s] = (dot_nt(both[0], wk[s]) + dot_nt(both[1], wv[s])).astype(BF)
            store(s).start()
        for s in range(steps):
            store(s).wait()
        place(m_ref, c, 0).wait()
        place(t_ref, 1 - c, 1).wait()

    piece = spec((rows, 2 * HD))
    hbm = pl.BlockSpec(memory_space=pltpu.HBM)
    anywhere = pl.BlockSpec(memory_space=pl.ANY)
    return pl.pallas_call(
        body,
        out_shape=(
            jax.ShapeDtypeStruct((rows, feat), BF),
            jax.ShapeDtypeStruct((rows, 2 * half), BF),
        ),
        grid_spec=pltpu.PrefetchScalarGridSpec(
            num_scalar_prefetch=1,
            grid=(1,),
            in_specs=[piece] * 4 + [hbm] * 2 + [anywhere] * 2,
            out_specs=[hbm, hbm],
            scratch_shapes=[
                pltpu.VMEM((steps, chunk, cols), BF),
                pltpu.VMEM((steps, chunk, cols), BF),
                pltpu.VMEM((2, rows, cols), BF),
                pltpu.VMEM((steps, rows, chunk), BF),
                pltpu.SemaphoreType.DMA((4, steps)),
            ],
        ),
        compiler_params=pltpu.CompilerParams(vmem_limit_bytes=24 << 20),
        name="feats",
        cost_estimate=cost(4),
    )(idx, own, oc, oh, ohc, in_hbm(key_weight), in_hbm(value_weight), mine, theirs)


def solution(mesh):
    sizes = tuple(mesh.shape[a] for a in AXES)
    to_c = moved(sizes, lambda i, h, t: (i ^ 1, h, t))
    to_h = moved(sizes, lambda i, h, t: (i, 1 - h, t))
    to_hc = moved(sizes, lambda i, h, t: (i ^ 1, 1 - h, t))
    to_t = {k: moved(sizes, lambda i, h, t, k=k: (i, h, t ^ k)) for k in (1, 2, 3)}
    chips = [[m * 2 + c for m in range(8)] for c in range(2)]

    def swap8(x):
        return lax.all_to_all(x, "img", 0, 0, axis_index_groups=chips, tiled=True)

    def gathered(own):
        return [own] + [to_t[k](own) for k in (1, 2, 3)]

    def shards(image_feats, key_weight, value_weight, queries, grad_out, tile_image, text_sees):
        img = lax.axis_index("img")
        core = img % 2
        idx = jnp.stack([lax.axis_index("head"), core, lax.axis_index("txt"), img // 2]).astype(jnp.int32)
        tiles = jnp.stack([tile_image, to_c(tile_image)])

        own, c, h, hc = project(idx, image_feats, key_weight, value_weight)
        h, hc, c = to_h(h), to_hc(hc), to_c(c)

        def wide(x):
            x = x.astype(F32)
            return x[:, :HD] + x[:, HD : 2 * HD], x[:, 2 * HD :]

        hk, hv = wide(h)
        ck, cv = wide(c)
        hck, hcv = wide(hc)
        near = jnp.concatenate([own[:, :HD] + hk, own[:, HD:] + hv], axis=1).astype(BF)
        far = jnp.concatenate([ck + hck, cv + hcv], axis=1).astype(BF)
        kvs = gathered(jnp.concatenate([near, far], axis=0))
        parts, stats = forward(idx, tiles, text_sees, queries, grad_out, kvs)
        stats = swap8(stats)
        parts = swap8(parts)

        def grads(k, dtype, *more):
            return backward(idx, tiles, text_sees, queries, grad_out, kvs[k], stats, k, dtype, *more)

        far = []
        for k in (2, 1, 3):
            (sent,) = grads(k, BF)
            far.append(to_t[k](sent))
        total, merged = grads(0, F32, parts)
        mine = swap8(merged).reshape(queries.shape[0], -1)
        for x in far:
            total = total + x.astype(F32)
        total = total.astype(BF)
        rows = total.shape[0] // 2
        near, other = total[:rows], total[rows:]
        grad_feats, attn_out = feature_grad(
            idx, near, to_c(other), to_h(near), to_hc(other), key_weight, value_weight, mine, to_c(mine)
        )
        return attn_out, grad_feats

    placed = (
        P(("img", "txt"), "head"),
        P("head", None),
        P("head", None),
        P("txt", "head"),
        P("txt", "head"),
        P("img"),
        P(),
    )
    return jax.shard_map(
        shards,
        mesh=mesh,
        in_specs=placed,
        out_specs=(P("txt", "head"), P(("img", "txt"), "head")),
        check_vma=False,
    )
```

```python
import math

import jax
import jax.numpy as jnp
from jax import lax
from jax.experimental import pallas as pl
from jax.experimental.pallas import tpu as pltpu
from jax.sharding import PartitionSpec as P

HD = 128
TILE = 128
TBLK = 128
BF = jnp.bfloat16
F32 = jnp.float32
SCALE = 1.0 / math.sqrt(HD)
C2 = SCALE * math.log2(math.e)
NEG = -1e30
TOP = 3e38
AXES = ("img", "head", "txt")
NT = (((1,), (1,)), ((), ()))


def dot_nt(a, b):
    return lax.dot_general(a, b, NT, preferred_element_type=F32)


def dot_nn(a, b):
    return jnp.dot(a, b, preferred_element_type=F32)


def moved(sizes, where):
    ni, nh, nt = sizes
    pairs = []
    for i in range(ni):
        for h in range(nh):
            for t in range(nt):
                a, b, c = where(i, h, t)
                pairs.append(((i * nh + h) * nt + t, (a * nh + b) * nt + c))
    return lambda x: lax.ppermute(x, AXES, pairs)


def cost(us):
    return pl.CostEstimate(flops=int(us * 1.1e9), transcendentals=0, bytes_accessed=1 << 16)


def spec(shape):
    zeros = (0,) * len(shape)
    return pl.BlockSpec(shape, lambda *_: zeros)


def in_hbm(x):
    return pltpu.with_memory_space_constraint(x, pltpu.HBM)


def project(idx, feats, key_weight, value_weight):
    rows, feat = feats.shape
    cols = key_weight.shape[1]
    steps = 5
    chunk = feat // steps

    def body(ix, x_hbm, wk_hbm, wv_hbm, own, oc, oh, ohc, x, wk, wv, acc, sems):
        copies = []
        for s in range(steps):
            at = slice(s * chunk, (s + 1) * chunk)
            copies.append(
                (
                    pltpu.make_async_copy(x_hbm.at[:, at], x.at[s], sems.at[0, s]),
                    pltpu.make_async_copy(wk_hbm.at[at, :], wk.at[s], sems.at[1, s]),
                    pltpu.make_async_copy(wv_hbm.at[at, :], wv.at[s], sems.at[2, s]),
                )
            )
            for copy in copies[s]:
                copy.start()
        for s in range(steps):
            for copy in copies[s]:
                copy.wait()
            key = dot_nn(x[s], wk[s])
            value = dot_nn(x[s], wv[s])
            if s == 0:
                acc[0] = key
                acc[1] = value
            else:
                acc[0] += key
                acc[1] += value
        h = ix[0]
        c = ix[1]

        def piece(which, hh, cc):
            at = pl.multiple_of((hh * 2 + cc) * HD, HD)
            return acc[which, :, pl.ds(at, HD)]

        own[:, :HD] = piece(0, h, c)
        own[:, HD:] = piece(1, h, c)
        for ref, hh, cc in ((oh, 1 - h, c), (ohc, 1 - h, 1 - c), (oc, h, 1 - c)):
            kp = piece(0, hh, cc)
            high = kp.astype(BF)
            ref[:, :HD] = high
            ref[:, HD : 2 * HD] = (kp - high.astype(F32)).astype(BF)
            ref[:, 2 * HD :] = piece(1, hh, cc).astype(BF)

    sent = jax.ShapeDtypeStruct((rows, 3 * HD), BF)
    return pl.pallas_call(
        body,
        out_shape=(jax.ShapeDtypeStruct((rows, 2 * HD), F32), sent, sent, sent),
        grid_spec=pltpu.PrefetchScalarGridSpec(
            num_scalar_prefetch=1,
            grid=(1,),
            in_specs=[pl.BlockSpec(memory_space=pltpu.HBM)] * 3,
            out_specs=[spec((rows, 2 * HD))] + [spec((rows, 3 * HD))] * 3,
            scratch_shapes=[
                pltpu.VMEM((steps, rows, chunk), BF),
                pltpu.VMEM((steps, chunk, cols), BF),
                pltpu.VMEM((steps, chunk, cols), BF),
                pltpu.VMEM((2, rows, cols), F32),
                pltpu.SemaphoreType.DMA((3, steps)),
            ],
        ),
        compiler_params=pltpu.CompilerParams(vmem_limit_bytes=24 << 20),
        name="project",
        cost_estimate=cost(4),
    )(idx, in_hbm(feats), in_hbm(key_weight), in_hbm(value_weight))


def tile_cap(ix, tiles, sees, block, chunk, tile):
    half, j = divmod(tile, 2)
    shard = jnp.bitwise_xor(ix[2], chunk)
    image = tiles[half, shard * 2 + j]
    row = ix[2] * 2 + block
    return jnp.where(sees[row, image] > 0, jnp.float32(TOP), jnp.float32(NEG))


def forward(idx, tiles, sees, queries, grad_out, kvs):
    rows = queries.shape[0]
    heads = 8
    width = heads * HD
    span = kvs[0].shape[0]
    n = len(kvs)
    total = span * n
    share = rows // 8
    per = span // TILE

    def body(ix, tl, se, q, g, k0, k1, k2, k3, out, st_out, y_scr, va):
        ks = (k0, k1, k2, k3)
        for j in range(n):
            va[j * span : (j + 1) * span, :HD] = ks[j][:, HD:]
        va[:, HD:] = jnp.ones((total, HD), BF)
        caps = [
            [tile_cap(ix, tl, se, b, j, e) for j in range(n) for e in range(per)]
            for b in range(2)
        ]
        lane = lax.broadcasted_iota(jnp.int32, (rows, HD), 1)
        st = jnp.zeros((rows, HD), F32)
        for h in range(heads):
            cols = slice(h * HD, (h + 1) * HD)
            slot = h % 2
            qh = q[:, cols]
            best = [None, None]
            for j in range(n):
                s = dot_nt(qh, ks[j][:, :HD]) * C2
                for b in range(2):
                    for e in range(per):
                        y = jnp.minimum(
                            s[b * TBLK : (b + 1) * TBLK, e * TILE : (e + 1) * TILE],
                            caps[b][j * per + e],
                        )
                        at = j * span + e * TILE
                        y_scr[slot, b * TBLK : (b + 1) * TBLK, at : at + TILE] = y
                        best[b] = y if best[b] is None else jnp.maximum(best[b], y)
            m = jnp.max(jnp.concatenate(best, axis=0), axis=1, keepdims=True)
            p = jnp.exp2(y_scr[slot] - m).astype(BF)
            r = dot_nn(p, va[...])
            den = r[:, HD:]
            o = r[:, :HD] / den
            out[:, :, cols] = o.astype(BF).reshape(8, share, HD)
            lse = m + jnp.log2(den)
            delta = jnp.sum(o * g[:, cols].astype(F32), axis=1, keepdims=True)
            st = jnp.where(lane == h, lse, st)
            st = jnp.where(lane == heads + h, delta, st)
        flat = st.T[: 2 * heads, :]
        for i in range(8):
            st_out[i] = flat

    own = lambda i, ix, tl, se: (0, ix[1])
    return pl.pallas_call(
        body,
        out_shape=(
            jax.ShapeDtypeStruct((8, share, width), BF),
            jax.ShapeDtypeStruct((8, 2 * heads, rows), F32),
        ),
        grid_spec=pltpu.PrefetchScalarGridSpec(
            num_scalar_prefetch=3,
            grid=(1,),
            in_specs=[pl.BlockSpec((rows, width), own)] * 2 + [spec((span, 2 * HD))] * 4,
            out_specs=[spec((8, share, width)), spec((8, 2 * heads, rows))],
            scratch_shapes=[
                pltpu.VMEM((2, rows, total), F32),
                pltpu.VMEM((total, 2 * HD), BF),
            ],
        ),
        compiler_params=pltpu.CompilerParams(vmem_limit_bytes=24 << 20),
        name="fwd",
        cost_estimate=cost(7),
    )(idx, tiles, sees, queries, grad_out, *kvs)


def merge_weights(st, heads):
    stats = [st[i] for i in range(8)]
    top = stats[0][:heads]
    for x in stats[1:]:
        top = jnp.maximum(top, x[:heads])
    ws = [jnp.exp2(x[:heads] - top) for x in stats]
    total = ws[0]
    delta = ws[0] * stats[0][heads:]
    for w, x in zip(ws[1:], stats[1:]):
        total = total + w
        delta = delta + w * x[heads:]
    inv = 1.0 / total
    return top + jnp.log2(total), delta * inv, [w * inv for w in ws]


def merge_parts(ix, x, ws, out, w_scr):
    _, share, width = x.shape
    heads = width // HD
    rows = w_scr.shape[0]
    pad = [jnp.zeros((HD - 8 * heads, rows), F32)]
    w_scr[...] = jnp.concatenate(ws + pad, axis=0).T
    w = w_scr[pl.ds(pl.multiple_of(ix[3] * share, share), share), :]
    for h in range(heads):
        cols = slice(h * HD, (h + 1) * HD)
        acc = jnp.zeros((share, HD), F32)
        for i in range(8):
            acc += x[i, :, cols].astype(F32) * w[:, i * heads + h : i * heads + h + 1]
        v = acc.astype(BF)
        for i in range(8):
            out[i, :, cols] = v


def backward(idx, tiles, sees, queries, grad_out, kvs, stats, chunks, parts=None):
    rows = queries.shape[0]
    heads = 8
    width = heads * HD
    span = kvs[0].shape[0]
    per = span // TILE
    n = len(chunks)

    def body(ix, tl, se, q, g, st, *refs):
        kv_refs, refs = refs[:n], refs[n:]
        lse, delta, ws = merge_weights(st, heads)
        if parts is None:
            outs, (dk, dv) = refs[:n], refs[n:]
        else:
            x, outs, (merged, dk, dv, w_scr) = refs[0], refs[1 : n + 1], refs[n + 1 :]
        lane = lax.broadcasted_iota(jnp.int32, (1, rows), 1)
        for chunk, kv_ref, out in zip(chunks, kv_refs, outs):
            caps = [
                jnp.where(
                    lane < TBLK,
                    tile_cap(ix, tl, se, 0, chunk, e),
                    tile_cap(ix, tl, se, 1, chunk, e),
                )
                for e in range(per)
            ]
            kk = kv_ref[:, :HD]
            vv = kv_ref[:, HD:]
            for h in range(heads):
                cols = slice(h * HD, (h + 1) * HD)
                qh = q[:, cols]
                gh = g[:, cols]
                s = dot_nt(kk, qh) * C2
                d = dot_nt(vv, gh)
                lh = lse[h : h + 1, :]
                dh = delta[h : h + 1, :]
                ps = []
                ds = []
                for e in range(per):
                    at = slice(e * TILE, (e + 1) * TILE)
                    p = jnp.exp2(jnp.minimum(s[at, :], caps[e]) - lh)
                    ps.append(p.astype(BF))
                    ds.append((p * (d[at, :] - dh) * SCALE).astype(BF))
                pv = dot_nn(jnp.concatenate(ps, axis=0), gh)
                pk = dot_nn(jnp.concatenate(ds, axis=0), qh)
                if h == 0:
                    dv[...] = pv
                    dk[...] = pk
                else:
                    dv[...] += pv
                    dk[...] += pk
            out[:, :HD] = dk[...].astype(out.dtype)
            out[:, HD:] = dv[...].astype(out.dtype)
        if parts is not None:
            merge_parts(ix, x, ws, merged, w_scr)

    own = lambda i, ix, tl, se: (0, ix[1])
    out_shape = [jax.ShapeDtypeStruct((span, 2 * HD), BF if k else F32) for k in chunks]
    in_specs = [pl.BlockSpec((rows, width), own)] * 2 + [spec(stats.shape)] + [spec((span, 2 * HD))] * n
    out_specs = [spec((span, 2 * HD))] * n
    scratch = [pltpu.VMEM((span, HD), F32)] * 2
    more = []
    if parts is not None:
        more.append(parts)
        in_specs.append(spec(parts.shape))
        out_shape.append(jax.ShapeDtypeStruct(parts.shape, BF))
        out_specs.append(spec(parts.shape))
        scratch.append(pltpu.VMEM((rows, HD), F32))
    return pl.pallas_call(
        body,
        out_shape=out_shape,
        grid_spec=pltpu.PrefetchScalarGridSpec(
            num_scalar_prefetch=3,
            grid=(1,),
            in_specs=in_specs,
            out_specs=out_specs,
            scratch_shapes=scratch,
        ),
        compiler_params=pltpu.CompilerParams(vmem_limit_bytes=20 << 20),
        name="grads" + "".join(map(str, chunks)),
        cost_estimate=cost(3 * n),
    )(idx, tiles, sees, queries, grad_out, stats, *[kvs[k] for k in chunks], *more)


def fetch_weights(key_weight, value_weight, token):
    rows = key_weight.shape[0]
    steps = 4
    chunk = rows // steps

    def body(k_hbm, v_hbm, _, k_out, v_out, sems):
        copies = []
        for s in range(steps):
            at = slice(s * chunk, (s + 1) * chunk)
            copies.append(pltpu.make_async_copy(k_hbm.at[at, :], k_out.at[at, :], sems.at[0, s]))
            copies.append(pltpu.make_async_copy(v_hbm.at[at, :], v_out.at[at, :], sems.at[1, s]))
        for copy in copies:
            copy.start()
        for copy in copies:
            copy.wait()

    hbm = pl.BlockSpec(memory_space=pltpu.HBM)
    vmem = pl.BlockSpec(memory_space=pltpu.VMEM)
    return pl.pallas_call(
        body,
        out_shape=(
            pltpu.VMEM(key_weight.shape, BF),
            pltpu.VMEM(value_weight.shape, BF),
        ),
        in_specs=[hbm, hbm, pl.BlockSpec(memory_space=pl.ANY)],
        out_specs=[vmem, vmem],
        scratch_shapes=[pltpu.SemaphoreType.DMA((2, steps))],
        compiler_params=pltpu.CompilerParams(vmem_limit_bytes=2 << 20),
        name="fetch",
        cost_estimate=cost(4),
    )(in_hbm(key_weight), in_hbm(value_weight), token)


def feature_grad(idx, own, oc, oh, ohc, key_weight, value_weight, mine, theirs):
    rows = own.shape[0]
    feat, cols = key_weight.shape
    steps = 5
    chunk = feat // steps
    half = mine.shape[1]

    def body(ix, a, b, c_, d_, wk, wv, m_ref, t_ref, out_hbm, attn, both, out, sems):
        h = ix[0]
        c = ix[1]

        def place(src, cc, s):
            at = pl.multiple_of(cc * half, half)
            return pltpu.make_async_copy(src, attn.at[:, pl.ds(at, half)], sems.at[1, s])

        def store(s):
            at = slice(s * chunk, (s + 1) * chunk)
            return pltpu.make_async_copy(out.at[s], out_hbm.at[:, at], sems.at[0, s])

        place(m_ref, c, 0).start()
        place(t_ref, 1 - c, 1).start()

        def put(hh, cc, x):
            at = pl.multiple_of((hh * 2 + cc) * HD, HD)
            both[0, :, pl.ds(at, HD)] = x[:, :HD]
            both[1, :, pl.ds(at, HD)] = x[:, HD:]

        put(h, c, a)
        put(h, 1 - c, b)
        put(1 - h, c, c_)
        put(1 - h, 1 - c, d_)
        for s in range(steps):
            at = slice(s * chunk, (s + 1) * chunk)
            out[s] = (dot_nt(both[0], wk[at, :]) + dot_nt(both[1], wv[at, :])).astype(BF)
            store(s).start()
        for s in range(steps):
            store(s).wait()
        place(m_ref, c, 0).wait()
        place(t_ref, 1 - c, 1).wait()

    piece = spec((rows, 2 * HD))
    hbm = pl.BlockSpec(memory_space=pltpu.HBM)
    vmem = pl.BlockSpec(memory_space=pltpu.VMEM)
    anywhere = pl.BlockSpec(memory_space=pl.ANY)
    return pl.pallas_call(
        body,
        out_shape=(
            jax.ShapeDtypeStruct((rows, feat), BF),
            jax.ShapeDtypeStruct((rows, 2 * half), BF),
        ),
        grid_spec=pltpu.PrefetchScalarGridSpec(
            num_scalar_prefetch=1,
            grid=(1,),
            in_specs=[piece] * 4 + [vmem] * 2 + [anywhere] * 2,
            out_specs=[hbm, hbm],
            scratch_shapes=[
                pltpu.VMEM((2, rows, cols), BF),
                pltpu.VMEM((steps, rows, chunk), BF),
                pltpu.SemaphoreType.DMA((2, steps)),
            ],
        ),
        compiler_params=pltpu.CompilerParams(vmem_limit_bytes=8 << 20),
        name="feats",
        cost_estimate=cost(4),
    )(idx, own, oc, oh, ohc, key_weight, value_weight, mine, theirs)


def solution(mesh):
    sizes = tuple(mesh.shape[a] for a in AXES)
    to_c = moved(sizes, lambda i, h, t: (i ^ 1, h, t))
    to_h = moved(sizes, lambda i, h, t: (i, 1 - h, t))
    to_hc = moved(sizes, lambda i, h, t: (i ^ 1, 1 - h, t))
    to_t = {k: moved(sizes, lambda i, h, t, k=k: (i, h, t ^ k)) for k in (1, 2, 3)}
    chips = [[m * 2 + c for m in range(8)] for c in range(2)]

    def swap8(x):
        return lax.all_to_all(x, "img", 0, 0, axis_index_groups=chips, tiled=True)

    def gathered(own):
        return [own] + [to_t[k](own) for k in (1, 2, 3)]

    def shards(image_feats, key_weight, value_weight, queries, grad_out, tile_image, text_sees):
        img = lax.axis_index("img")
        core = img % 2
        idx = jnp.stack([lax.axis_index("head"), core, lax.axis_index("txt"), img // 2]).astype(jnp.int32)
        tiles = jnp.stack([tile_image, to_c(tile_image)])

        own, c, h, hc = project(idx, image_feats, key_weight, value_weight)
        h, hc, c = to_h(h), to_hc(hc), to_c(c)

        def wide(x):
            x = x.astype(F32)
            return x[:, :HD] + x[:, HD : 2 * HD], x[:, 2 * HD :]

        hk, hv = wide(h)
        ck, cv = wide(c)
        hck, hcv = wide(hc)
        near = jnp.concatenate([own[:, :HD] + hk, own[:, HD:] + hv], axis=1).astype(BF)
        far = jnp.concatenate([ck + hck, cv + hcv], axis=1).astype(BF)
        kvs = gathered(jnp.concatenate([near, far], axis=0))
        parts, stats = forward(idx, tiles, text_sees, queries, grad_out, kvs)
        stats = swap8(stats)
        parts = swap8(parts)

        def grads(chunks, *more):
            return backward(idx, tiles, text_sees, queries, grad_out, kvs, stats, chunks, *more)

        (second,) = grads((2,))
        (first,) = grads((1,))
        third, total, merged = grads((3, 0), parts)
        far = [to_t[2](second), to_t[1](first), to_t[3](third)]
        mine = swap8(merged).reshape(queries.shape[0], -1)
        for x in far:
            total = total + x.astype(F32)
        total = total.astype(BF)
        rows = total.shape[0] // 2
        near, other = total[:rows], total[rows:]
        pieces = near, to_c(other), to_h(near), to_hc(other)
        key_near, value_near = fetch_weights(key_weight, value_weight, total)
        grad_feats, attn_out = feature_grad(idx, *pieces, key_near, value_near, mine, to_c(mine))
        return attn_out, grad_feats

    placed = (
        P(("img", "txt"), "head"),
        P("head", None),
        P("head", None),
        P("txt", "head"),
        P("txt", "head"),
        P("img"),
        P(),
    )
    return jax.shard_map(
        shards,
        mesh=mesh,
        in_specs=placed,
        out_specs=(P("txt", "head"), P(("img", "txt"), "head")),
        check_vma=False,
    )
```

```python
import math

import jax
import jax.numpy as jnp
from jax import lax
from jax.experimental import pallas as pl
from jax.experimental.pallas import tpu as pltpu
from jax.sharding import PartitionSpec as P

HD = 128
TILE = 128
TBLK = 128
BF = jnp.bfloat16
F32 = jnp.float32
SCALE = 1.0 / math.sqrt(HD)
C2 = SCALE * math.log2(math.e)
NEG = -1e30
TOP = 3e38
AXES = ("img", "head", "txt")
NT = (((1,), (1,)), ((), ()))


def dot_nt(a, b):
    return lax.dot_general(a, b, NT, preferred_element_type=F32)


def dot_nn(a, b):
    return jnp.dot(a, b, preferred_element_type=F32)


def moved(sizes, where):
    ni, nh, nt = sizes
    pairs = []
    for i in range(ni):
        for h in range(nh):
            for t in range(nt):
                a, b, c = where(i, h, t)
                pairs.append(((i * nh + h) * nt + t, (a * nh + b) * nt + c))
    return lambda x: lax.ppermute(x, AXES, pairs)


def cost(us):
    return pl.CostEstimate(flops=int(us * 1.1e9), transcendentals=0, bytes_accessed=1 << 16)


def spec(shape):
    zeros = (0,) * len(shape)
    return pl.BlockSpec(shape, lambda *_: zeros)


def in_hbm(x):
    return pltpu.with_memory_space_constraint(x, pltpu.HBM)


def project(idx, tiles, feats, key_weight, value_weight):
    rows, feat = feats.shape
    cols = key_weight.shape[1]
    steps = 5
    chunk = feat // steps

    def body(ix, tl, x_hbm, wk_hbm, wv_hbm, k0, kc, kh, khc, v0, vc, vh, vhc, x, wk, wv, acc, sems):
        copies = []
        for s in range(steps):
            at = slice(s * chunk, (s + 1) * chunk)
            copies.append(
                (
                    pltpu.make_async_copy(x_hbm.at[:, at], x.at[s], sems.at[0, s]),
                    pltpu.make_async_copy(wk_hbm.at[at, :], wk.at[s], sems.at[1, s]),
                    pltpu.make_async_copy(wv_hbm.at[at, :], wv.at[s], sems.at[2, s]),
                )
            )
            for copy in copies[s]:
                copy.start()
        for s in range(steps):
            for copy in copies[s]:
                copy.wait()
            key = dot_nn(x[s], wk[s])
            value = dot_nn(x[s], wv[s])
            if s == 0:
                acc[0] = key
                acc[1] = value
            else:
                acc[0] += key
                acc[1] += value
        h = ix[0]
        c = ix[1]

        def piece(which, hh, cc):
            at = pl.multiple_of((hh * 2 + cc) * HD, HD)
            return acc[which, :, pl.ds(at, HD)]

        for which, refs in ((1, (v0, vh, vhc, vc)), (0, (k0, kh, khc, kc))):
            for ref, (hh, cc) in zip(refs, ((h, c), (1 - h, c), (1 - h, 1 - c), (h, 1 - c))):
                ref[:rows, :] = piece(which, hh, cc).astype(ref.dtype)
        lane = lax.broadcasted_iota(jnp.int32, (extra, HD), 1)
        ids = jnp.zeros((extra, HD), F32)
        for e in range(tiles.shape[0]):
            ids = jnp.where(lane == e, tl[e].astype(F32), ids)
        vc[rows:, :] = ids.astype(BF)

    extra = 16
    key = jax.ShapeDtypeStruct((rows, HD), F32)
    value = jax.ShapeDtypeStruct((rows, HD), BF)
    marked = jax.ShapeDtypeStruct((rows + extra, HD), BF)
    outs = (key, key, key, key, key, marked, value, value)
    return pl.pallas_call(
        body,
        out_shape=outs,
        grid_spec=pltpu.PrefetchScalarGridSpec(
            num_scalar_prefetch=2,
            grid=(1,),
            in_specs=[pl.BlockSpec(memory_space=pltpu.HBM)] * 3,
            out_specs=[spec(o.shape) for o in outs],
            scratch_shapes=[
                pltpu.VMEM((steps, rows, chunk), BF),
                pltpu.VMEM((steps, chunk, cols), BF),
                pltpu.VMEM((steps, chunk, cols), BF),
                pltpu.VMEM((2, rows, cols), F32),
                pltpu.SemaphoreType.DMA((3, steps)),
            ],
        ),
        compiler_params=pltpu.CompilerParams(vmem_limit_bytes=24 << 20),
        name="project",
        cost_estimate=cost(4),
    )(idx, tiles, in_hbm(feats), in_hbm(key_weight), in_hbm(value_weight))


def tile_cap(ix, tiles, sees, block, chunk, tile):
    half, j = divmod(tile, 2)
    shard = jnp.bitwise_xor(ix[2], chunk)
    image = tiles[half, shard * 2 + j]
    row = ix[2] * 2 + block
    return jnp.where(sees[row, image] > 0, jnp.float32(TOP), jnp.float32(NEG))


def forward(idx, tiles, sees, queries, grad_out, keys, values):
    rows = queries.shape[0]
    heads = 8
    width = heads * HD
    span = keys[0].shape[0]
    n = len(keys)
    total = span * n
    share = rows // 8
    per = span // TILE

    def body(ix, tl, se, q, g, k0, k1, k2, k3, v0, v1, v2, v3, out, st_out, y_scr, va):
        ks = (k0, k1, k2, k3)
        vs = (v0, v1, v2, v3)
        for j in range(n):
            va[j * span : (j + 1) * span, :HD] = vs[j][...]
        va[:, HD:] = jnp.ones((total, HD), BF)
        caps = [
            [tile_cap(ix, tl, se, b, j, e) for j in range(n) for e in range(per)]
            for b in range(2)
        ]
        lane = lax.broadcasted_iota(jnp.int32, (rows, HD), 1)
        st = jnp.zeros((rows, HD), F32)
        for h in range(heads):
            cols = slice(h * HD, (h + 1) * HD)
            slot = h % 2
            qh = q[:, cols]
            best = [None, None]
            for j in range(n):
                s = dot_nt(qh, ks[j][...]) * C2
                for b in range(2):
                    for e in range(per):
                        y = jnp.minimum(
                            s[b * TBLK : (b + 1) * TBLK, e * TILE : (e + 1) * TILE],
                            caps[b][j * per + e],
                        )
                        at = j * span + e * TILE
                        y_scr[slot, b * TBLK : (b + 1) * TBLK, at : at + TILE] = y
                        best[b] = y if best[b] is None else jnp.maximum(best[b], y)
            m = jnp.max(jnp.concatenate(best, axis=0), axis=1, keepdims=True)
            p = jnp.exp2(y_scr[slot] - m).astype(BF)
            r = dot_nn(p, va[...])
            den = r[:, HD:]
            o = r[:, :HD] / den
            out[:, :, cols] = o.astype(BF).reshape(8, share, HD)
            lse = m + jnp.log2(den)
            delta = jnp.sum(o * g[:, cols].astype(F32), axis=1, keepdims=True)
            st = jnp.where(lane == h, lse, st)
            st = jnp.where(lane == heads + h, delta, st)
        flat = st.T[: 2 * heads, :]
        for i in range(8):
            st_out[i] = flat

    own = lambda i, ix, tl, se: (0, ix[1])
    return pl.pallas_call(
        body,
        out_shape=(
            jax.ShapeDtypeStruct((8, share, width), BF),
            jax.ShapeDtypeStruct((8, 2 * heads, rows), F32),
        ),
        grid_spec=pltpu.PrefetchScalarGridSpec(
            num_scalar_prefetch=3,
            grid=(1,),
            in_specs=[pl.BlockSpec((rows, width), own)] * 2 + [spec((span, HD))] * 8,
            out_specs=[spec((8, share, width)), spec((8, 2 * heads, rows))],
            scratch_shapes=[
                pltpu.VMEM((2, rows, total), F32),
                pltpu.VMEM((total, 2 * HD), BF),
            ],
        ),
        compiler_params=pltpu.CompilerParams(vmem_limit_bytes=24 << 20),
        name="fwd",
        cost_estimate=cost(7),
    )(idx, tiles, sees, queries, grad_out, *keys, *values)


def merge_weights(st, heads):
    stats = [st[i] for i in range(8)]
    top = stats[0][:heads]
    for x in stats[1:]:
        top = jnp.maximum(top, x[:heads])
    ws = [jnp.exp2(x[:heads] - top) for x in stats]
    total = ws[0]
    delta = ws[0] * stats[0][heads:]
    for w, x in zip(ws[1:], stats[1:]):
        total = total + w
        delta = delta + w * x[heads:]
    inv = 1.0 / total
    return top + jnp.log2(total), delta * inv, [w * inv for w in ws]


def merge_parts(ix, x, ws, out, w_scr):
    _, share, width = x.shape
    heads = width // HD
    rows = w_scr.shape[0]
    pad = [jnp.zeros((HD - 8 * heads, rows), F32)]
    w_scr[...] = jnp.concatenate(ws + pad, axis=0).T
    w = w_scr[pl.ds(pl.multiple_of(ix[3] * share, share), share), :]
    for h in range(heads):
        cols = slice(h * HD, (h + 1) * HD)
        acc = jnp.zeros((share, HD), F32)
        for i in range(8):
            acc += x[i, :, cols].astype(F32) * w[:, i * heads + h : i * heads + h + 1]
        v = acc.astype(BF)
        for i in range(8):
            out[i, :, cols] = v


def backward(idx, tiles, sees, queries, grad_out, keys, values, stats, chunks, parts=None):
    rows = queries.shape[0]
    heads = 8
    width = heads * HD
    span = keys[0].shape[0]
    per = span // TILE
    n = len(chunks)

    def body(ix, tl, se, q, g, st, *refs):
        k_refs, v_refs, refs = refs[:n], refs[n : 2 * n], refs[2 * n :]
        lse, delta, ws = merge_weights(st, heads)
        if parts is None:
            outs, (dk, dv) = refs[:n], refs[n:]
        else:
            x, outs, (merged, dk, dv, w_scr) = refs[0], refs[1 : n + 1], refs[n + 1 :]
        lane = lax.broadcasted_iota(jnp.int32, (1, rows), 1)
        for chunk, k_ref, v_ref, out in zip(chunks, k_refs, v_refs, outs):
            caps = [
                jnp.where(
                    lane < TBLK,
                    tile_cap(ix, tl, se, 0, chunk, e),
                    tile_cap(ix, tl, se, 1, chunk, e),
                )
                for e in range(per)
            ]
            kk = k_ref[...]
            vv = v_ref[...]
            for h in range(heads):
                cols = slice(h * HD, (h + 1) * HD)
                qh = q[:, cols]
                gh = g[:, cols]
                s = dot_nt(kk, qh) * C2
                d = dot_nt(vv, gh)
                lh = lse[h : h + 1, :]
                dh = delta[h : h + 1, :]
                ps = []
                ds = []
                for e in range(per):
                    at = slice(e * TILE, (e + 1) * TILE)
                    p = jnp.exp2(jnp.minimum(s[at, :], caps[e]) - lh)
                    ps.append(p.astype(BF))
                    ds.append((p * (d[at, :] - dh) * SCALE).astype(BF))
                pv = dot_nn(jnp.concatenate(ps, axis=0), gh)
                pk = dot_nn(jnp.concatenate(ds, axis=0), qh)
                if h == 0:
                    dv[...] = pv
                    dk[...] = pk
                else:
                    dv[...] += pv
                    dk[...] += pk
            out[:, :HD] = dk[...].astype(out.dtype)
            out[:, HD:] = dv[...].astype(out.dtype)
        if parts is not None:
            merge_parts(ix, x, ws, merged, w_scr)

    own = lambda i, ix, tl, se: (0, ix[1])
    out_shape = [jax.ShapeDtypeStruct((span, 2 * HD), BF if k else F32) for k in chunks]
    in_specs = [pl.BlockSpec((rows, width), own)] * 2 + [spec(stats.shape)] + [spec((span, HD))] * (2 * n)
    out_specs = [spec((span, 2 * HD))] * n
    scratch = [pltpu.VMEM((span, HD), F32)] * 2
    more = []
    if parts is not None:
        more.append(parts)
        in_specs.append(spec(parts.shape))
        out_shape.append(jax.ShapeDtypeStruct(parts.shape, BF))
        out_specs.append(spec(parts.shape))
        scratch.append(pltpu.VMEM((rows, HD), F32))
    return pl.pallas_call(
        body,
        out_shape=out_shape,
        grid_spec=pltpu.PrefetchScalarGridSpec(
            num_scalar_prefetch=3,
            grid=(1,),
            in_specs=in_specs,
            out_specs=out_specs,
            scratch_shapes=scratch,
        ),
        compiler_params=pltpu.CompilerParams(vmem_limit_bytes=20 << 20),
        name="grads" + "".join(map(str, chunks)),
        cost_estimate=cost(3 * n),
    )(idx, tiles, sees, queries, grad_out, stats, *[keys[k] for k in chunks], *[values[k] for k in chunks], *more)


def fetch_weights(key_weight, value_weight, token):
    rows = key_weight.shape[0]
    steps = 4
    chunk = rows // steps

    def body(k_hbm, v_hbm, _, k_out, v_out, sems):
        copies = []
        for s in range(steps):
            at = slice(s * chunk, (s + 1) * chunk)
            copies.append(pltpu.make_async_copy(k_hbm.at[at, :], k_out.at[at, :], sems.at[0, s]))
            copies.append(pltpu.make_async_copy(v_hbm.at[at, :], v_out.at[at, :], sems.at[1, s]))
        for copy in copies:
            copy.start()
        for copy in copies:
            copy.wait()

    hbm = pl.BlockSpec(memory_space=pltpu.HBM)
    vmem = pl.BlockSpec(memory_space=pltpu.VMEM)
    return pl.pallas_call(
        body,
        out_shape=(
            pltpu.VMEM(key_weight.shape, BF),
            pltpu.VMEM(value_weight.shape, BF),
        ),
        in_specs=[hbm, hbm, pl.BlockSpec(memory_space=pl.ANY)],
        out_specs=[vmem, vmem],
        scratch_shapes=[pltpu.SemaphoreType.DMA((2, steps))],
        compiler_params=pltpu.CompilerParams(vmem_limit_bytes=2 << 20),
        name="fetch",
        cost_estimate=cost(4),
    )(in_hbm(key_weight), in_hbm(value_weight), token)


def feature_grad(idx, own, oc, oh, ohc, key_weight, value_weight, mine, theirs):
    rows = own.shape[0]
    feat, cols = key_weight.shape
    steps = 5
    chunk = feat // steps
    half = mine.shape[1]

    def body(ix, a, b, c_, d_, wk, wv, m_ref, t_ref, out_hbm, attn, both, out, sems):
        h = ix[0]
        c = ix[1]

        def place(src, cc, s):
            at = pl.multiple_of(cc * half, half)
            return pltpu.make_async_copy(src, attn.at[:, pl.ds(at, half)], sems.at[1, s])

        def store(s):
            at = slice(s * chunk, (s + 1) * chunk)
            return pltpu.make_async_copy(out.at[s], out_hbm.at[:, at], sems.at[0, s])

        place(m_ref, c, 0).start()
        place(t_ref, 1 - c, 1).start()

        def put(hh, cc, x):
            at = pl.multiple_of((hh * 2 + cc) * HD, HD)
            both[0, :, pl.ds(at, HD)] = x[:, :HD]
            both[1, :, pl.ds(at, HD)] = x[:, HD:]

        put(h, c, a)
        put(h, 1 - c, b)
        put(1 - h, c, c_)
        put(1 - h, 1 - c, d_)
        for s in range(steps):
            at = slice(s * chunk, (s + 1) * chunk)
            out[s] = (dot_nt(both[0], wk[at, :]) + dot_nt(both[1], wv[at, :])).astype(BF)
            store(s).start()
        for s in range(steps):
            store(s).wait()
        place(m_ref, c, 0).wait()
        place(t_ref, 1 - c, 1).wait()

    piece = spec((rows, 2 * HD))
    hbm = pl.BlockSpec(memory_space=pltpu.HBM)
    vmem = pl.BlockSpec(memory_space=pltpu.VMEM)
    anywhere = pl.BlockSpec(memory_space=pl.ANY)
    return pl.pallas_call(
        body,
        out_shape=(
            jax.ShapeDtypeStruct((rows, feat), BF),
            jax.ShapeDtypeStruct((rows, 2 * half), BF),
        ),
        grid_spec=pltpu.PrefetchScalarGridSpec(
            num_scalar_prefetch=1,
            grid=(1,),
            in_specs=[piece] * 4 + [vmem] * 2 + [anywhere] * 2,
            out_specs=[hbm, hbm],
            scratch_shapes=[
                pltpu.VMEM((2, rows, cols), BF),
                pltpu.VMEM((steps, rows, chunk), BF),
                pltpu.SemaphoreType.DMA((2, steps)),
            ],
        ),
        compiler_params=pltpu.CompilerParams(vmem_limit_bytes=8 << 20),
        name="feats",
        cost_estimate=cost(4),
    )(idx, own, oc, oh, ohc, key_weight, value_weight, mine, theirs)


def solution(mesh):
    sizes = tuple(mesh.shape[a] for a in AXES)
    to_c = moved(sizes, lambda i, h, t: (i ^ 1, h, t))
    to_h = moved(sizes, lambda i, h, t: (i, 1 - h, t))
    to_hc = moved(sizes, lambda i, h, t: (i ^ 1, 1 - h, t))
    to_t = {k: moved(sizes, lambda i, h, t, k=k: (i, h, t ^ k)) for k in (1, 2, 3)}
    chips = [[m * 2 + c for m in range(8)] for c in range(2)]

    def swap8(x):
        return lax.all_to_all(x, "img", 0, 0, axis_index_groups=chips, tiled=True)

    def gathered(own):
        return [own] + [to_t[k](own) for k in (1, 2, 3)]

    def shards(image_feats, key_weight, value_weight, queries, grad_out, tile_image, text_sees):
        img = lax.axis_index("img")
        core = img % 2
        idx = jnp.stack([lax.axis_index("head"), core, lax.axis_index("txt"), img // 2]).astype(jnp.int32)
        own_k, c_k, h_k, hc_k, own_v, c_v, h_v, hc_v = project(
            idx, tile_image, image_feats, key_weight, value_weight
        )
        h_v, hc_v, c_v = to_h(h_v), to_hc(hc_v), to_c(c_v)
        h_k, hc_k, c_k = to_h(h_k), to_hc(hc_k), to_c(c_k)
        rows = h_v.shape[0]
        others = c_v[rows, : tile_image.shape[0]].astype(jnp.int32)
        tiles = jnp.stack([tile_image, others])

        def owned(own, h, c, hc):
            near = own + h.astype(F32)
            far = c[:rows].astype(F32) + hc.astype(F32)
            return jnp.concatenate([near.astype(BF), far.astype(BF)], axis=0)

        values = gathered(owned(own_v, h_v, c_v, hc_v))
        keys = gathered(owned(own_k, h_k, c_k, hc_k))
        parts, stats = forward(idx, tiles, text_sees, queries, grad_out, keys, values)
        stats = swap8(stats)
        parts = swap8(parts)

        keys = [in_hbm(x) for x in keys]
        values = [in_hbm(x) for x in values]

        def grads(chunks, *more):
            return backward(idx, tiles, text_sees, queries, grad_out, keys, values, stats, chunks, *more)

        second, first = grads((2, 1))
        third, total, merged = grads((3, 0), parts)
        far = [to_t[2](second), to_t[1](first), to_t[3](third)]
        mine = swap8(merged).reshape(queries.shape[0], -1)
        for x in far:
            total = total + x.astype(F32)
        total = total.astype(BF)
        rows = total.shape[0] // 2
        near, other = total[:rows], total[rows:]
        pieces = near, to_c(other), to_h(near), to_hc(other)
        key_near, value_near = fetch_weights(key_weight, value_weight, total)
        grad_feats, attn_out = feature_grad(idx, *pieces, key_near, value_near, mine, to_c(mine))
        return attn_out, grad_feats

    placed = (
        P(("img", "txt"), "head"),
        P("head", None),
        P("head", None),
        P("txt", "head"),
        P("txt", "head"),
        P("img"),
        P(),
    )
    return jax.shard_map(
        shards,
        mesh=mesh,
        in_specs=placed,
        out_specs=(P("txt", "head"), P(("img", "txt"), "head")),
        check_vma=False,
    )
```

```python
import math

import jax
import jax.numpy as jnp
from jax import lax
from jax.experimental import pallas as pl
from jax.experimental.pallas import tpu as pltpu
from jax.sharding import PartitionSpec as P

HD = 128
TILE = 128
TBLK = 128
BF = jnp.bfloat16
F32 = jnp.float32
SCALE = 1.0 / math.sqrt(HD)
C2 = SCALE * math.log2(math.e)
NEG = -1e30
TOP = 3e38
AXES = ("img", "head", "txt")
NT = (((1,), (1,)), ((), ()))


def dot_nt(a, b):
    return lax.dot_general(a, b, NT, preferred_element_type=F32)


def dot_nn(a, b):
    return jnp.dot(a, b, preferred_element_type=F32)


def moved(sizes, where):
    ni, nh, nt = sizes
    pairs = []
    for i in range(ni):
        for h in range(nh):
            for t in range(nt):
                a, b, c = where(i, h, t)
                pairs.append(((i * nh + h) * nt + t, (a * nh + b) * nt + c))
    return lambda x: lax.ppermute(x, AXES, pairs)


def cost(us):
    return pl.CostEstimate(flops=int(us * 1.1e9), transcendentals=0, bytes_accessed=1 << 16)


def spec(shape):
    zeros = (0,) * len(shape)
    return pl.BlockSpec(shape, lambda *_: zeros)


def in_hbm(x):
    return pltpu.with_memory_space_constraint(x, pltpu.HBM)


def project(idx, count, feats, key_weight, value_weight):
    rows, feat = feats.shape
    cols = key_weight.shape[1]
    steps = 5
    chunk = feat // steps

    def body(ix, x_hbm, wk_hbm, wv_hbm, k0, kc, kh, khc, v0, vc, vh, vhc, x, wk, wv, acc, sems):
        copies = []
        for s in range(steps):
            at = slice(s * chunk, (s + 1) * chunk)
            copies.append(
                (
                    pltpu.make_async_copy(x_hbm.at[:, at], x.at[s], sems.at[0, s]),
                    pltpu.make_async_copy(wk_hbm.at[at, :], wk.at[s], sems.at[1, s]),
                    pltpu.make_async_copy(wv_hbm.at[at, :], wv.at[s], sems.at[2, s]),
                )
            )
            for copy in copies[s]:
                copy.start()
        for s in range(steps):
            for copy in copies[s]:
                copy.wait()
            key = dot_nn(x[s], wk[s])
            value = dot_nn(x[s], wv[s])
            if s == 0:
                acc[0] = key
                acc[1] = value
            else:
                acc[0] += key
                acc[1] += value
        h = ix[0]
        c = ix[1]

        def piece(which, hh, cc):
            at = pl.multiple_of((hh * 2 + cc) * HD, HD)
            return acc[which, :, pl.ds(at, HD)]

        for which, refs in ((1, (v0, vh, vhc, vc)), (0, (k0, kh, khc, kc))):
            for ref, (hh, cc) in zip(refs, ((h, c), (1 - h, c), (1 - h, 1 - c), (h, 1 - c))):
                ref[:rows, :] = piece(which, hh, cc).astype(ref.dtype)
        lane = lax.broadcasted_iota(jnp.int32, (extra, HD), 1)
        ids = jnp.zeros((extra, HD), F32)
        for e in range(count):
            ids = jnp.where(lane == e, ix[4 + e].astype(F32), ids)
        vc[rows:, :] = ids.astype(BF)

    extra = 16
    key = jax.ShapeDtypeStruct((rows, HD), F32)
    value = jax.ShapeDtypeStruct((rows, HD), BF)
    marked = jax.ShapeDtypeStruct((rows + extra, HD), BF)
    outs = (key, key, key, key, key, marked, value, value)
    return pl.pallas_call(
        body,
        out_shape=outs,
        grid_spec=pltpu.PrefetchScalarGridSpec(
            num_scalar_prefetch=1,
            grid=(1,),
            in_specs=[pl.BlockSpec(memory_space=pltpu.HBM)] * 3,
            out_specs=[spec(o.shape) for o in outs],
            scratch_shapes=[
                pltpu.VMEM((steps, rows, chunk), BF),
                pltpu.VMEM((steps, chunk, cols), BF),
                pltpu.VMEM((steps, chunk, cols), BF),
                pltpu.VMEM((2, rows, cols), F32),
                pltpu.SemaphoreType.DMA((3, steps)),
            ],
        ),
        compiler_params=pltpu.CompilerParams(vmem_limit_bytes=24 << 20),
        name="project",
        cost_estimate=cost(4),
    )(idx, in_hbm(feats), in_hbm(key_weight), in_hbm(value_weight))


def tile_cap(ix, tiles, sees, block, chunk, tile):
    half, j = divmod(tile, 2)
    shard = jnp.bitwise_xor(ix[2], chunk)
    image = tiles[half, shard * 2 + j]
    row = ix[2] * 2 + block
    return jnp.where(sees[row, image] > 0, jnp.float32(TOP), jnp.float32(NEG))


def forward(idx, tiles, sees, queries, grad_out, keys, values):
    rows = queries.shape[0]
    heads = 8
    width = heads * HD
    span = keys[0].shape[0]
    n = len(keys)
    total = span * n
    share = rows // 8
    per = span // TILE

    def body(ix, tl, se, q, g, k0, k1, k2, k3, v0, v1, v2, v3, out, st_out, y_scr, va):
        ks = (k0, k1, k2, k3)
        vs = (v0, v1, v2, v3)
        for j in range(n):
            va[j * span : (j + 1) * span, :HD] = vs[j][...]
        va[:, HD:] = jnp.ones((total, HD), BF)
        caps = [
            [tile_cap(ix, tl, se, b, j, e) for j in range(n) for e in range(per)]
            for b in range(2)
        ]
        lane = lax.broadcasted_iota(jnp.int32, (rows, HD), 1)
        st = jnp.zeros((rows, HD), F32)
        for h in range(heads):
            cols = slice(h * HD, (h + 1) * HD)
            slot = h % 2
            qh = q[:, cols]
            best = [None, None]
            for j in range(n):
                s = dot_nt(qh, ks[j][...]) * C2
                for b in range(2):
                    for e in range(per):
                        y = jnp.minimum(
                            s[b * TBLK : (b + 1) * TBLK, e * TILE : (e + 1) * TILE],
                            caps[b][j * per + e],
                        )
                        at = j * span + e * TILE
                        y_scr[slot, b * TBLK : (b + 1) * TBLK, at : at + TILE] = y
                        best[b] = y if best[b] is None else jnp.maximum(best[b], y)
            m = jnp.max(jnp.concatenate(best, axis=0), axis=1, keepdims=True)
            p = jnp.exp2(y_scr[slot] - m).astype(BF)
            r = dot_nn(p, va[...])
            den = r[:, HD:]
            o = r[:, :HD] / den
            out[:, :, cols] = o.astype(BF).reshape(8, share, HD)
            lse = m + jnp.log2(den)
            delta = jnp.sum(o * g[:, cols].astype(F32), axis=1, keepdims=True)
            st = jnp.where(lane == h, lse, st)
            st = jnp.where(lane == heads + h, delta, st)
        flat = st.T[: 2 * heads, :]
        for i in range(8):
            st_out[i] = flat

    own = lambda i, ix, tl, se: (0, ix[1])
    return pl.pallas_call(
        body,
        out_shape=(
            jax.ShapeDtypeStruct((8, share, width), BF),
            jax.ShapeDtypeStruct((8, 2 * heads, rows), F32),
        ),
        grid_spec=pltpu.PrefetchScalarGridSpec(
            num_scalar_prefetch=3,
            grid=(1,),
            in_specs=[pl.BlockSpec((rows, width), own)] * 2 + [spec((span, HD))] * 8,
            out_specs=[spec((8, share, width)), spec((8, 2 * heads, rows))],
            scratch_shapes=[
                pltpu.VMEM((2, rows, total), F32),
                pltpu.VMEM((total, 2 * HD), BF),
            ],
        ),
        compiler_params=pltpu.CompilerParams(vmem_limit_bytes=24 << 20),
        name="fwd",
        cost_estimate=cost(7),
    )(idx, tiles, sees, queries, grad_out, *keys, *values)


def merge_weights(st, heads):
    stats = [st[i] for i in range(8)]
    top = stats[0][:heads]
    for x in stats[1:]:
        top = jnp.maximum(top, x[:heads])
    ws = [jnp.exp2(x[:heads] - top) for x in stats]
    total = ws[0]
    delta = ws[0] * stats[0][heads:]
    for w, x in zip(ws[1:], stats[1:]):
        total = total + w
        delta = delta + w * x[heads:]
    inv = 1.0 / total
    return top + jnp.log2(total), delta * inv, [w * inv for w in ws]


def merge_parts(ix, x, ws, out, w_scr):
    _, share, width = x.shape
    heads = width // HD
    rows = w_scr.shape[0]
    pad = [jnp.zeros((HD - 8 * heads, rows), F32)]
    w_scr[...] = jnp.concatenate(ws + pad, axis=0).T
    w = w_scr[pl.ds(pl.multiple_of(ix[3] * share, share), share), :]
    for h in range(heads):
        cols = slice(h * HD, (h + 1) * HD)
        acc = jnp.zeros((share, HD), F32)
        for i in range(8):
            acc += x[i, :, cols].astype(F32) * w[:, i * heads + h : i * heads + h + 1]
        v = acc.astype(BF)
        for i in range(8):
            out[i, :, cols] = v


def backward(idx, tiles, sees, queries, grad_out, keys, values, stats, chunks, parts=None):
    rows = queries.shape[0]
    heads = 8
    width = heads * HD
    span = keys[0].shape[0]
    per = span // TILE
    n = len(chunks)

    def body(ix, tl, se, q, g, st, *refs):
        k_refs, v_refs, refs = refs[:n], refs[n : 2 * n], refs[2 * n :]
        lse, delta, ws = merge_weights(st, heads)
        if parts is None:
            outs, (dk, dv) = refs[:n], refs[n:]
        else:
            x, outs, (merged, dk, dv, w_scr) = refs[0], refs[1 : n + 1], refs[n + 1 :]
        lane = lax.broadcasted_iota(jnp.int32, (1, rows), 1)
        for chunk, k_ref, v_ref, out in zip(chunks, k_refs, v_refs, outs):
            caps = [
                jnp.where(
                    lane < TBLK,
                    tile_cap(ix, tl, se, 0, chunk, e),
                    tile_cap(ix, tl, se, 1, chunk, e),
                )
                for e in range(per)
            ]
            kk = k_ref[...]
            vv = v_ref[...]
            for h in range(heads):
                cols = slice(h * HD, (h + 1) * HD)
                qh = q[:, cols]
                gh = g[:, cols]
                s = dot_nt(kk, qh) * C2
                d = dot_nt(vv, gh)
                lh = lse[h : h + 1, :]
                dh = delta[h : h + 1, :]
                ps = []
                ds = []
                for e in range(per):
                    at = slice(e * TILE, (e + 1) * TILE)
                    p = jnp.exp2(jnp.minimum(s[at, :], caps[e]) - lh)
                    ps.append(p.astype(BF))
                    ds.append((p * (d[at, :] - dh) * SCALE).astype(BF))
                pv = dot_nn(jnp.concatenate(ps, axis=0), gh)
                pk = dot_nn(jnp.concatenate(ds, axis=0), qh)
                if h == 0:
                    dv[...] = pv
                    dk[...] = pk
                else:
                    dv[...] += pv
                    dk[...] += pk
            out[:, :HD] = dk[...].astype(out.dtype)
            out[:, HD:] = dv[...].astype(out.dtype)
        if parts is not None:
            merge_parts(ix, x, ws, merged, w_scr)

    own = lambda i, ix, tl, se: (0, ix[1])
    out_shape = [jax.ShapeDtypeStruct((span, 2 * HD), BF if k else F32) for k in chunks]
    in_specs = [pl.BlockSpec((rows, width), own)] * 2 + [spec(stats.shape)] + [spec((span, HD))] * (2 * n)
    out_specs = [spec((span, 2 * HD))] * n
    scratch = [pltpu.VMEM((span, HD), F32)] * 2
    more = []
    if parts is not None:
        more.append(parts)
        in_specs.append(spec(parts.shape))
        out_shape.append(jax.ShapeDtypeStruct(parts.shape, BF))
        out_specs.append(spec(parts.shape))
        scratch.append(pltpu.VMEM((rows, HD), F32))
    return pl.pallas_call(
        body,
        out_shape=out_shape,
        grid_spec=pltpu.PrefetchScalarGridSpec(
            num_scalar_prefetch=3,
            grid=(1,),
            in_specs=in_specs,
            out_specs=out_specs,
            scratch_shapes=scratch,
        ),
        compiler_params=pltpu.CompilerParams(vmem_limit_bytes=20 << 20),
        name="grads" + "".join(map(str, chunks)),
        cost_estimate=cost(3 * n),
    )(idx, tiles, sees, queries, grad_out, stats, *[keys[k] for k in chunks], *[values[k] for k in chunks], *more)


def fetch_weights(key_weight, value_weight, token):
    rows = key_weight.shape[0]
    steps = 4
    chunk = rows // steps

    def body(k_hbm, v_hbm, _, k_out, v_out, sems):
        copies = []
        for s in range(steps):
            at = slice(s * chunk, (s + 1) * chunk)
            copies.append(pltpu.make_async_copy(k_hbm.at[at, :], k_out.at[at, :], sems.at[0, s]))
            copies.append(pltpu.make_async_copy(v_hbm.at[at, :], v_out.at[at, :], sems.at[1, s]))
        for copy in copies:
            copy.start()
        for copy in copies:
            copy.wait()

    hbm = pl.BlockSpec(memory_space=pltpu.HBM)
    vmem = pl.BlockSpec(memory_space=pltpu.VMEM)
    return pl.pallas_call(
        body,
        out_shape=(
            pltpu.VMEM(key_weight.shape, BF),
            pltpu.VMEM(value_weight.shape, BF),
        ),
        in_specs=[hbm, hbm, pl.BlockSpec(memory_space=pl.ANY)],
        out_specs=[vmem, vmem],
        scratch_shapes=[pltpu.SemaphoreType.DMA((2, steps))],
        compiler_params=pltpu.CompilerParams(vmem_limit_bytes=2 << 20),
        name="fetch",
        cost_estimate=cost(4),
    )(in_hbm(key_weight), in_hbm(value_weight), token)


def feature_grad(idx, own, oc, oh, ohc, key_weight, value_weight, mine):
    rows = own.shape[0]
    feat, cols = key_weight.shape
    steps = 5
    chunk = feat // steps
    half = mine.shape[1]

    def body(ix, a, b, c_, d_, wk, wv, m_ref, out_hbm, attn, both, out, sems):
        h = ix[0]
        c = ix[1]

        mine_at = attn.at[:, pl.ds(pl.multiple_of(c * half, half), half)]
        place = pltpu.make_async_copy(m_ref, mine_at, sems.at[1, 0])

        def store(s):
            at = slice(s * chunk, (s + 1) * chunk)
            return pltpu.make_async_copy(out.at[s], out_hbm.at[:, at], sems.at[0, s])

        place.start()

        def put(hh, cc, x):
            at = pl.multiple_of((hh * 2 + cc) * HD, HD)
            both[0, :, pl.ds(at, HD)] = x[:, :HD]
            both[1, :, pl.ds(at, HD)] = x[:, HD:]

        put(h, c, a)
        put(h, 1 - c, b)
        put(1 - h, c, c_)
        put(1 - h, 1 - c, d_)
        for s in range(steps):
            at = slice(s * chunk, (s + 1) * chunk)
            out[s] = (dot_nt(both[0], wk[at, :]) + dot_nt(both[1], wv[at, :])).astype(BF)
            store(s).start()
        for s in range(steps):
            store(s).wait()
        place.wait()

    piece = spec((rows, 2 * HD))
    hbm = pl.BlockSpec(memory_space=pltpu.HBM)
    vmem = pl.BlockSpec(memory_space=pltpu.VMEM)
    anywhere = pl.BlockSpec(memory_space=pl.ANY)
    return pl.pallas_call(
        body,
        out_shape=(
            jax.ShapeDtypeStruct((rows, feat), BF),
            jax.ShapeDtypeStruct((rows, 2 * half), BF),
        ),
        grid_spec=pltpu.PrefetchScalarGridSpec(
            num_scalar_prefetch=1,
            grid=(1,),
            in_specs=[piece] * 4 + [vmem] * 2 + [anywhere],
            out_specs=[hbm, hbm],
            scratch_shapes=[
                pltpu.VMEM((2, rows, cols), BF),
                pltpu.VMEM((steps, rows, chunk), BF),
                pltpu.SemaphoreType.DMA((2, steps)),
            ],
        ),
        compiler_params=pltpu.CompilerParams(vmem_limit_bytes=8 << 20),
        name="feats",
        cost_estimate=cost(4),
    )(idx, own, oc, oh, ohc, key_weight, value_weight, mine)


def add_theirs(idx, attn, theirs):
    half = theirs.shape[1]

    def body(ix, _, t_ref, out, sem):
        at = pl.multiple_of((1 - ix[1]) * half, half)
        copy = pltpu.make_async_copy(t_ref, out.at[:, pl.ds(at, half)], sem)
        copy.start()
        copy.wait()

    hbm = pl.BlockSpec(memory_space=pltpu.HBM)
    return pl.pallas_call(
        body,
        out_shape=jax.ShapeDtypeStruct(attn.shape, BF),
        grid_spec=pltpu.PrefetchScalarGridSpec(
            num_scalar_prefetch=1,
            grid=(1,),
            in_specs=[hbm, pl.BlockSpec(memory_space=pl.ANY)],
            out_specs=hbm,
            scratch_shapes=[pltpu.SemaphoreType.DMA],
        ),
        input_output_aliases={1: 0},
        compiler_params=pltpu.CompilerParams(vmem_limit_bytes=1 << 20),
        name="theirs",
    )(idx, attn, theirs)


def solution(mesh):
    sizes = tuple(mesh.shape[a] for a in AXES)
    to_c = moved(sizes, lambda i, h, t: (i ^ 1, h, t))
    to_h = moved(sizes, lambda i, h, t: (i, 1 - h, t))
    to_hc = moved(sizes, lambda i, h, t: (i ^ 1, 1 - h, t))
    to_t = {k: moved(sizes, lambda i, h, t, k=k: (i, h, t ^ k)) for k in (1, 2, 3)}
    chips = [[m * 2 + c for m in range(8)] for c in range(2)]

    def swap8(x):
        return lax.all_to_all(x, "img", 0, 0, axis_index_groups=chips, tiled=True)

    def gathered(own):
        return [own] + [to_t[k](own) for k in (1, 2, 3)]

    def shards(image_feats, key_weight, value_weight, queries, grad_out, tile_image, text_sees):
        img = lax.axis_index("img")
        core = img % 2
        idx = jnp.stack([lax.axis_index("head"), core, lax.axis_index("txt"), img // 2]).astype(jnp.int32)
        idx = jnp.concatenate([idx, tile_image])
        own_k, c_k, h_k, hc_k, own_v, c_v, h_v, hc_v = project(
            idx, tile_image.shape[0], image_feats, key_weight, value_weight
        )
        h_v, hc_v, c_v = to_h(h_v), to_hc(hc_v), to_c(c_v)
        h_k, hc_k, c_k = to_h(h_k), to_hc(hc_k), to_c(c_k)
        rows = h_v.shape[0]
        others = c_v[rows, : tile_image.shape[0]].astype(jnp.int32)
        tiles = jnp.stack([tile_image, others])

        def owned(own, h, c, hc):
            near = own + h.astype(F32)
            far = c[:rows].astype(F32) + hc.astype(F32)
            return jnp.concatenate([near.astype(BF), far.astype(BF)], axis=0)

        values = gathered(owned(own_v, h_v, c_v, hc_v))
        keys = gathered(owned(own_k, h_k, c_k, hc_k))
        parts, stats = forward(idx, tiles, text_sees, queries, grad_out, keys, values)
        stats = swap8(stats)
        parts = swap8(parts)

        keys = [in_hbm(x) for x in keys]
        values = [in_hbm(x) for x in values]

        def grads(chunks, *more):
            return backward(idx, tiles, text_sees, queries, grad_out, keys, values, stats, chunks, *more)

        second, first = grads((2, 1))
        third, total, merged = grads((3, 0), parts)
        far = [to_t[2](second), to_t[1](first), to_t[3](third)]
        mine = swap8(merged).reshape(queries.shape[0], -1)
        for x in far:
            total = total + x.astype(F32)
        total = total.astype(BF)
        rows = total.shape[0] // 2
        near, other = total[:rows], total[rows:]
        side, ahead, across = to_c(other), to_h(near), to_hc(other)
        key_near, value_near = fetch_weights(key_weight, value_weight, total)
        mine, side = lax.optimization_barrier((mine, side))
        theirs = to_c(mine)
        grad_feats, attn_out = feature_grad(
            idx, near, side, ahead, across, key_near, value_near, mine
        )
        attn_out = add_theirs(idx, attn_out, theirs)
        return attn_out, grad_feats

    placed = (
        P(("img", "txt"), "head"),
        P("head", None),
        P("head", None),
        P("txt", "head"),
        P("txt", "head"),
        P("img"),
        P(),
    )
    return jax.shard_map(
        shards,
        mesh=mesh,
        in_specs=placed,
        out_specs=(P("txt", "head"), P(("img", "txt"), "head")),
        check_vma=False,
    )
```

```python
import math

import jax
import jax.numpy as jnp
from jax import lax
from jax.experimental import pallas as pl
from jax.experimental.pallas import tpu as pltpu
from jax.sharding import PartitionSpec as P

HD = 128
TILE = 128
TBLK = 128
BF = jnp.bfloat16
F32 = jnp.float32
SCALE = 1.0 / math.sqrt(HD)
C2 = SCALE * math.log2(math.e)
NEG = -1e30
TOP = 3e38
AXES = ("img", "head", "txt")
NT = (((1,), (1,)), ((), ()))


def dot_nt(a, b):
    return lax.dot_general(a, b, NT, preferred_element_type=F32)


def dot_nn(a, b):
    return jnp.dot(a, b, preferred_element_type=F32)


def moved(sizes, where):
    ni, nh, nt = sizes
    pairs = []
    for i in range(ni):
        for h in range(nh):
            for t in range(nt):
                a, b, c = where(i, h, t)
                pairs.append(((i * nh + h) * nt + t, (a * nh + b) * nt + c))
    return lambda x: lax.ppermute(x, AXES, pairs)


def cost(us):
    return pl.CostEstimate(flops=int(us * 1.1e9), transcendentals=0, bytes_accessed=1 << 16)


def spec(shape):
    zeros = (0,) * len(shape)
    return pl.BlockSpec(shape, lambda *_: zeros)


def in_hbm(x):
    return pltpu.with_memory_space_constraint(x, pltpu.HBM)


def project(idx, count, feats, key_weight, value_weight):
    rows, feat = feats.shape
    cols = key_weight.shape[1]
    steps = 5
    chunk = feat // steps

    def body(ix, x_hbm, wk_hbm, wv_hbm, k0, kc, kh, khc, v0, vc, vh, vhc, x, wk, wv, acc, sems):
        copies = []
        for s in range(steps):
            at = slice(s * chunk, (s + 1) * chunk)
            copies.append(
                (
                    pltpu.make_async_copy(x_hbm.at[:, at], x.at[s], sems.at[0, s]),
                    pltpu.make_async_copy(wk_hbm.at[at, :], wk.at[s], sems.at[1, s]),
                    pltpu.make_async_copy(wv_hbm.at[at, :], wv.at[s], sems.at[2, s]),
                )
            )
            for copy in copies[s]:
                copy.start()
        for s in range(steps):
            for copy in copies[s]:
                copy.wait()
            key = dot_nn(x[s], wk[s])
            value = dot_nn(x[s], wv[s])
            if s == 0:
                acc[0] = key
                acc[1] = value
            else:
                acc[0] += key
                acc[1] += value
        h = ix[0]
        c = ix[1]

        def piece(which, hh, cc):
            at = pl.multiple_of((hh * 2 + cc) * HD, HD)
            return acc[which, :, pl.ds(at, HD)]

        for which, refs in ((1, (v0, vh, vhc, vc)), (0, (k0, kh, khc, kc))):
            for ref, (hh, cc) in zip(refs, ((h, c), (1 - h, c), (1 - h, 1 - c), (h, 1 - c))):
                ref[:rows, :] = piece(which, hh, cc).astype(ref.dtype)
        lane = lax.broadcasted_iota(jnp.int32, (extra, HD), 1)
        ids = jnp.zeros((extra, HD), F32)
        for e in range(count):
            ids = jnp.where(lane == e, ix[4 + e].astype(F32), ids)
        vc[rows:, :] = ids.astype(BF)

    extra = 16
    key = jax.ShapeDtypeStruct((rows, HD), F32)
    value = jax.ShapeDtypeStruct((rows, HD), BF)
    marked = jax.ShapeDtypeStruct((rows + extra, HD), BF)
    outs = (key, key, key, key, key, marked, value, value)
    return pl.pallas_call(
        body,
        out_shape=outs,
        grid_spec=pltpu.PrefetchScalarGridSpec(
            num_scalar_prefetch=1,
            grid=(1,),
            in_specs=[pl.BlockSpec(memory_space=pltpu.HBM)] * 3,
            out_specs=[spec(o.shape) for o in outs],
            scratch_shapes=[
                pltpu.VMEM((steps, rows, chunk), BF),
                pltpu.VMEM((steps, chunk, cols), BF),
                pltpu.VMEM((steps, chunk, cols), BF),
                pltpu.VMEM((2, rows, cols), F32),
                pltpu.SemaphoreType.DMA((3, steps)),
            ],
        ),
        compiler_params=pltpu.CompilerParams(vmem_limit_bytes=24 << 20),
        name="project",
        cost_estimate=cost(4),
    )(idx, in_hbm(feats), in_hbm(key_weight), in_hbm(value_weight))


def tile_cap(ix, tiles, sees, block, chunk, tile):
    half, j = divmod(tile, 2)
    shard = jnp.bitwise_xor(ix[2], chunk)
    image = tiles[half, shard * 2 + j]
    row = ix[2] * 2 + block
    return jnp.where(sees[row, image] > 0, jnp.float32(TOP), jnp.float32(NEG))


def forward(idx, tiles, sees, queries, grad_out, keys, values):
    rows = queries.shape[0]
    heads = 8
    width = heads * HD
    span = keys[0].shape[0]
    n = len(keys)
    total = span * n
    share = rows // 8
    per = span // TILE

    def body(ix, tl, se, q, g, k0, k1, k2, k3, v0, v1, v2, v3, out, st_out, y_scr, va):
        ks = (k0, k1, k2, k3)
        vs = (v0, v1, v2, v3)
        for j in range(n):
            va[j * span : (j + 1) * span, :HD] = vs[j][...]
        va[:, HD:] = jnp.ones((total, HD), BF)
        caps = [
            [tile_cap(ix, tl, se, b, j, e) for j in range(n) for e in range(per)]
            for b in range(2)
        ]
        lane = lax.broadcasted_iota(jnp.int32, (rows, HD), 1)
        st = jnp.zeros((rows, HD), F32)
        group = 2
        for h0 in range(0, heads, group):
            qh = jnp.concatenate([q[:, h * HD : (h + 1) * HD] for h in range(h0, h0 + group)], axis=0)
            best = [None] * (2 * group)
            slot = (h0 // group) % 2
            for j in range(n):
                s = dot_nt(qh, ks[j][...]) * C2
                for b in range(2 * group):
                    for e in range(per):
                        y = jnp.minimum(
                            s[b * TBLK : (b + 1) * TBLK, e * TILE : (e + 1) * TILE],
                            caps[b % 2][j * per + e],
                        )
                        at = j * span + e * TILE
                        y_scr[slot, b * TBLK : (b + 1) * TBLK, at : at + TILE] = y
                        best[b] = y if best[b] is None else jnp.maximum(best[b], y)
            m = jnp.max(jnp.concatenate(best, axis=0), axis=1, keepdims=True)
            p = jnp.exp2(y_scr[slot] - m).astype(BF)
            r = dot_nn(p, va[...])
            for k in range(group):
                h = h0 + k
                cols = slice(h * HD, (h + 1) * HD)
                mine = slice(k * rows, (k + 1) * rows)
                den = r[mine, HD:]
                o = r[mine, :HD] / den
                out[:, :, cols] = o.astype(BF).reshape(8, share, HD)
                lse = m[mine] + jnp.log2(den)
                delta = jnp.sum(o * g[:, cols].astype(F32), axis=1, keepdims=True)
                st = jnp.where(lane == h, lse, st)
                st = jnp.where(lane == heads + h, delta, st)
        flat = st.T[: 2 * heads, :]
        for i in range(8):
            st_out[i] = flat

    own = lambda i, ix, tl, se: (0, ix[1])
    return pl.pallas_call(
        body,
        out_shape=(
            jax.ShapeDtypeStruct((8, share, width), BF),
            jax.ShapeDtypeStruct((8, 2 * heads, rows), F32),
        ),
        grid_spec=pltpu.PrefetchScalarGridSpec(
            num_scalar_prefetch=3,
            grid=(1,),
            in_specs=[pl.BlockSpec((rows, width), own)] * 2 + [spec((span, HD))] * 8,
            out_specs=[spec((8, share, width)), spec((8, 2 * heads, rows))],
            scratch_shapes=[
                pltpu.VMEM((2, 2 * rows, total), F32),
                pltpu.VMEM((total, 2 * HD), BF),
            ],
        ),
        compiler_params=pltpu.CompilerParams(vmem_limit_bytes=40 << 20),
        name="fwd",
        cost_estimate=cost(7),
    )(idx, tiles, sees, queries, grad_out, *keys, *values)


def merge_weights(st, heads):
    stats = [st[i] for i in range(8)]
    top = stats[0][:heads]
    for x in stats[1:]:
        top = jnp.maximum(top, x[:heads])
    ws = [jnp.exp2(x[:heads] - top) for x in stats]
    total = ws[0]
    delta = ws[0] * stats[0][heads:]
    for w, x in zip(ws[1:], stats[1:]):
        total = total + w
        delta = delta + w * x[heads:]
    inv = 1.0 / total
    return top + jnp.log2(total), delta * inv, [w * inv for w in ws]


def merge_parts(ix, x, ws, out, w_scr):
    _, share, width = x.shape
    heads = width // HD
    rows = w_scr.shape[0]
    pad = [jnp.zeros((HD - 8 * heads, rows), F32)]
    w_scr[...] = jnp.concatenate(ws + pad, axis=0).T
    w = w_scr[pl.ds(pl.multiple_of(ix[3] * share, share), share), :]
    for h in range(heads):
        cols = slice(h * HD, (h + 1) * HD)
        acc = jnp.zeros((share, HD), F32)
        for i in range(8):
            acc += x[i, :, cols].astype(F32) * w[:, i * heads + h : i * heads + h + 1]
        v = acc.astype(BF)
        for i in range(8):
            out[i, :, cols] = v


def backward(idx, tiles, sees, queries, grad_out, keys, values, stats, chunks, parts=None):
    rows = queries.shape[0]
    heads = 8
    width = heads * HD
    span = keys[0].shape[0]
    per = span // TILE
    n = len(chunks)

    def body(ix, tl, se, q, g, st, *refs):
        k_refs, v_refs, refs = refs[:n], refs[n : 2 * n], refs[2 * n :]
        lse, delta, ws = merge_weights(st, heads)
        if parts is None:
            outs, (dk, dv) = refs[:n], refs[n:]
        else:
            x, outs, (merged, dk, dv, w_scr) = refs[0], refs[1 : n + 1], refs[n + 1 :]
        lane = lax.broadcasted_iota(jnp.int32, (1, rows), 1)
        for chunk, k_ref, v_ref, out in zip(chunks, k_refs, v_refs, outs):
            caps = [
                jnp.where(
                    lane < TBLK,
                    tile_cap(ix, tl, se, 0, chunk, e),
                    tile_cap(ix, tl, se, 1, chunk, e),
                )
                for e in range(per)
            ]
            kk = k_ref[...]
            vv = v_ref[...]
            group = 2
            for h0 in range(0, heads, group):
                hs = range(h0, h0 + group)
                qh = jnp.concatenate([q[:, h * HD : (h + 1) * HD] for h in hs], axis=0)
                gh = jnp.concatenate([g[:, h * HD : (h + 1) * HD] for h in hs], axis=0)
                s = dot_nt(kk, qh) * C2
                d = dot_nt(vv, gh)
                dh = jnp.concatenate([delta[h : h + 1, :] for h in hs], axis=1)
                ps = []
                ds = []
                for e in range(per):
                    at = slice(e * TILE, (e + 1) * TILE)
                    lh = jnp.concatenate([jnp.where(caps[e] > 0, lse[h : h + 1, :], -NEG) for h in hs], axis=1)
                    p = jnp.exp2(s[at, :] - lh)
                    ps.append(p.astype(BF))
                    ds.append((p * (d[at, :] - dh) * SCALE).astype(BF))
                pv = dot_nn(jnp.concatenate(ps, axis=0), gh)
                pk = dot_nn(jnp.concatenate(ds, axis=0), qh)
                if h0 == 0:
                    dv[...] = pv
                    dk[...] = pk
                else:
                    dv[...] += pv
                    dk[...] += pk
            out[:, :HD] = dk[...].astype(out.dtype)
            out[:, HD:] = dv[...].astype(out.dtype)
        if parts is not None:
            merge_parts(ix, x, ws, merged, w_scr)

    own = lambda i, ix, tl, se: (0, ix[1])
    out_shape = [jax.ShapeDtypeStruct((span, 2 * HD), BF if k else F32) for k in chunks]
    in_specs = [pl.BlockSpec((rows, width), own)] * 2 + [spec(stats.shape)] + [spec((span, HD))] * (2 * n)
    out_specs = [spec((span, 2 * HD))] * n
    scratch = [pltpu.VMEM((span, HD), F32)] * 2
    more = []
    if parts is not None:
        more.append(parts)
        in_specs.append(spec(parts.shape))
        out_shape.append(jax.ShapeDtypeStruct(parts.shape, BF))
        out_specs.append(spec(parts.shape))
        scratch.append(pltpu.VMEM((rows, HD), F32))
    return pl.pallas_call(
        body,
        out_shape=out_shape,
        grid_spec=pltpu.PrefetchScalarGridSpec(
            num_scalar_prefetch=3,
            grid=(1,),
            in_specs=in_specs,
            out_specs=out_specs,
            scratch_shapes=scratch,
        ),
        compiler_params=pltpu.CompilerParams(vmem_limit_bytes=32 << 20),
        name="grads" + "".join(map(str, chunks)),
        cost_estimate=cost(3 * n),
    )(idx, tiles, sees, queries, grad_out, stats, *[keys[k] for k in chunks], *[values[k] for k in chunks], *more)


def fetch_weights(key_weight, value_weight, token):
    rows = key_weight.shape[0]
    steps = 4
    chunk = rows // steps

    def body(k_hbm, v_hbm, _, k_out, v_out, sems):
        copies = []
        for s in range(steps):
            at = slice(s * chunk, (s + 1) * chunk)
            copies.append(pltpu.make_async_copy(k_hbm.at[at, :], k_out.at[at, :], sems.at[0, s]))
            copies.append(pltpu.make_async_copy(v_hbm.at[at, :], v_out.at[at, :], sems.at[1, s]))
        for copy in copies:
            copy.start()
        for copy in copies:
            copy.wait()

    hbm = pl.BlockSpec(memory_space=pltpu.HBM)
    vmem = pl.BlockSpec(memory_space=pltpu.VMEM)
    return pl.pallas_call(
        body,
        out_shape=(
            pltpu.VMEM(key_weight.shape, BF),
            pltpu.VMEM(value_weight.shape, BF),
        ),
        in_specs=[hbm, hbm, pl.BlockSpec(memory_space=pl.ANY)],
        out_specs=[vmem, vmem],
        scratch_shapes=[pltpu.SemaphoreType.DMA((2, steps))],
        compiler_params=pltpu.CompilerParams(vmem_limit_bytes=2 << 20),
        name="fetch",
        cost_estimate=cost(4),
    )(in_hbm(key_weight), in_hbm(value_weight), token)


def feature_grad(idx, own, oc, oh, ohc, key_weight, value_weight, mine):
    rows = own.shape[0]
    feat, cols = key_weight.shape
    steps = 5
    chunk = feat // steps
    half = mine.shape[1]

    def body(ix, a, b, c_, d_, wk, wv, m_ref, out_hbm, attn, both, out, sems):
        h = ix[0]
        c = ix[1]

        mine_at = attn.at[:, pl.ds(pl.multiple_of(c * half, half), half)]
        place = pltpu.make_async_copy(m_ref, mine_at, sems.at[1, 0])

        def store(s):
            at = slice(s * chunk, (s + 1) * chunk)
            return pltpu.make_async_copy(out.at[s], out_hbm.at[:, at], sems.at[0, s])

        place.start()

        def put(hh, cc, x):
            at = pl.multiple_of((hh * 2 + cc) * HD, HD)
            both[0, :, pl.ds(at, HD)] = x[:, :HD]
            both[1, :, pl.ds(at, HD)] = x[:, HD:]

        put(h, c, a)
        put(h, 1 - c, b)
        put(1 - h, c, c_)
        put(1 - h, 1 - c, d_)
        for s in range(steps):
            at = slice(s * chunk, (s + 1) * chunk)
            out[s] = (dot_nt(both[0], wk[at, :]) + dot_nt(both[1], wv[at, :])).astype(BF)
            store(s).start()
        for s in range(steps):
            store(s).wait()
        place.wait()

    piece = spec((rows, 2 * HD))
    hbm = pl.BlockSpec(memory_space=pltpu.HBM)
    vmem = pl.BlockSpec(memory_space=pltpu.VMEM)
    anywhere = pl.BlockSpec(memory_space=pl.ANY)
    return pl.pallas_call(
        body,
        out_shape=(
            jax.ShapeDtypeStruct((rows, feat), BF),
            jax.ShapeDtypeStruct((rows, 2 * half), BF),
        ),
        grid_spec=pltpu.PrefetchScalarGridSpec(
            num_scalar_prefetch=1,
            grid=(1,),
            in_specs=[piece] * 4 + [vmem] * 2 + [anywhere],
            out_specs=[hbm, hbm],
            scratch_shapes=[
                pltpu.VMEM((2, rows, cols), BF),
                pltpu.VMEM((steps, rows, chunk), BF),
                pltpu.SemaphoreType.DMA((2, steps)),
            ],
        ),
        compiler_params=pltpu.CompilerParams(vmem_limit_bytes=8 << 20),
        name="feats",
        cost_estimate=cost(4),
    )(idx, own, oc, oh, ohc, key_weight, value_weight, mine)


def add_theirs(idx, attn, theirs):
    half = theirs.shape[1]

    def body(ix, _, t_ref, out, sem):
        at = pl.multiple_of((1 - ix[1]) * half, half)
        copy = pltpu.make_async_copy(t_ref, out.at[:, pl.ds(at, half)], sem)
        copy.start()
        copy.wait()

    hbm = pl.BlockSpec(memory_space=pltpu.HBM)
    return pl.pallas_call(
        body,
        out_shape=jax.ShapeDtypeStruct(attn.shape, BF),
        grid_spec=pltpu.PrefetchScalarGridSpec(
            num_scalar_prefetch=1,
            grid=(1,),
            in_specs=[hbm, pl.BlockSpec(memory_space=pl.ANY)],
            out_specs=hbm,
            scratch_shapes=[pltpu.SemaphoreType.DMA],
        ),
        input_output_aliases={1: 0},
        compiler_params=pltpu.CompilerParams(vmem_limit_bytes=1 << 20),
        name="theirs",
    )(idx, attn, theirs)


def solution(mesh):
    sizes = tuple(mesh.shape[a] for a in AXES)
    to_c = moved(sizes, lambda i, h, t: (i ^ 1, h, t))
    to_h = moved(sizes, lambda i, h, t: (i, 1 - h, t))
    to_hc = moved(sizes, lambda i, h, t: (i ^ 1, 1 - h, t))
    to_t = {k: moved(sizes, lambda i, h, t, k=k: (i, h, t ^ k)) for k in (1, 2, 3)}
    chips = [[m * 2 + c for m in range(8)] for c in range(2)]

    def swap8(x):
        return lax.all_to_all(x, "img", 0, 0, axis_index_groups=chips, tiled=True)

    def gathered(own):
        return [own] + [to_t[k](own) for k in (1, 2, 3)]

    def shards(image_feats, key_weight, value_weight, queries, grad_out, tile_image, text_sees):
        img = lax.axis_index("img")
        core = img % 2
        idx = jnp.stack([lax.axis_index("head"), core, lax.axis_index("txt"), img // 2]).astype(jnp.int32)
        idx = jnp.concatenate([idx, tile_image])
        own_k, c_k, h_k, hc_k, own_v, c_v, h_v, hc_v = project(
            idx, tile_image.shape[0], image_feats, key_weight, value_weight
        )
        h_v, hc_v, c_v = to_h(h_v), to_hc(hc_v), to_c(c_v)
        h_k, hc_k, c_k = to_h(h_k), to_hc(hc_k), to_c(c_k)
        rows = h_v.shape[0]
        others = c_v[rows, : tile_image.shape[0]].astype(jnp.int32)
        tiles = jnp.stack([tile_image, others])

        def owned(own, h, c, hc):
            near = own + h.astype(F32)
            far = c[:rows].astype(F32) + hc.astype(F32)
            return jnp.concatenate([near.astype(BF), far.astype(BF)], axis=0)

        values = gathered(owned(own_v, h_v, c_v, hc_v))
        keys = gathered(owned(own_k, h_k, c_k, hc_k))
        parts, stats = forward(idx, tiles, text_sees, queries, grad_out, keys, values)
        stats = swap8(stats)
        parts = swap8(parts)

        keys = [in_hbm(x) for x in keys]
        values = [in_hbm(x) for x in values]

        def grads(chunks, *more):
            return backward(idx, tiles, text_sees, queries, grad_out, keys, values, stats, chunks, *more)

        second, first = grads((2, 1))
        third, total, merged = grads((3, 0), parts)
        far = [to_t[2](second), to_t[1](first), to_t[3](third)]
        mine = swap8(merged).reshape(queries.shape[0], -1)
        for x in far:
            total = total + x.astype(F32)
        total = total.astype(BF)
        rows = total.shape[0] // 2
        near, other = total[:rows], total[rows:]
        side, ahead, across = to_c(other), to_h(near), to_hc(other)
        key_near, value_near = fetch_weights(key_weight, value_weight, total)
        mine, side = lax.optimization_barrier((mine, side))
        theirs = to_c(mine)
        grad_feats, attn_out = feature_grad(
            idx, near, side, ahead, across, key_near, value_near, mine
        )
        attn_out = add_theirs(idx, attn_out, theirs)
        return attn_out, grad_feats

    placed = (
        P(("img", "txt"), "head"),
        P("head", None),
        P("head", None),
        P("txt", "head"),
        P("txt", "head"),
        P("img"),
        P(),
    )
    return jax.shard_map(
        shards,
        mesh=mesh,
        in_specs=placed,
        out_specs=(P("txt", "head"), P(("img", "txt"), "head")),
        check_vma=False,
    )
```

```python
import math

import jax
import jax.numpy as jnp
from jax import lax
from jax.experimental import pallas as pl
from jax.experimental.pallas import tpu as pltpu
from jax.sharding import PartitionSpec as P

HD = 128
TILE = 128
TBLK = 128
BF = jnp.bfloat16
F32 = jnp.float32
SCALE = 1.0 / math.sqrt(HD)
C2 = SCALE * math.log2(math.e)
NEG = -1e30
TOP = 3e38
AXES = ("img", "head", "txt")
NT = (((1,), (1,)), ((), ()))


def dot_nt(a, b):
    return lax.dot_general(a, b, NT, preferred_element_type=F32)


def dot_nn(a, b):
    return jnp.dot(a, b, preferred_element_type=F32)


def moved(sizes, where):
    ni, nh, nt = sizes
    pairs = []
    for i in range(ni):
        for h in range(nh):
            for t in range(nt):
                a, b, c = where(i, h, t)
                pairs.append(((i * nh + h) * nt + t, (a * nh + b) * nt + c))
    return lambda x: lax.ppermute(x, AXES, pairs)


def cost(us):
    return pl.CostEstimate(flops=int(us * 1.1e9), transcendentals=0, bytes_accessed=1 << 16)


def spec(shape):
    zeros = (0,) * len(shape)
    return pl.BlockSpec(shape, lambda *_: zeros)


def in_hbm(x):
    return pltpu.with_memory_space_constraint(x, pltpu.HBM)


def project(idx, count, feats, key_weight, value_weight):
    rows, feat = feats.shape
    cols = key_weight.shape[1]
    steps = 5
    chunk = feat // steps

    def body(ix, x_hbm, wk_hbm, wv_hbm, k0, kc, kh, khc, v0, vc, vh, vhc, x, wk, wv, acc, sems):
        copies = []
        for s in range(steps):
            at = slice(s * chunk, (s + 1) * chunk)
            copies.append(
                (
                    pltpu.make_async_copy(x_hbm.at[:, at], x.at[s], sems.at[0, s]),
                    pltpu.make_async_copy(wk_hbm.at[at, :], wk.at[s], sems.at[1, s]),
                    pltpu.make_async_copy(wv_hbm.at[at, :], wv.at[s], sems.at[2, s]),
                )
            )
            for copy in copies[s]:
                copy.start()
        for s in range(steps):
            for copy in copies[s]:
                copy.wait()
            key = dot_nn(x[s], wk[s])
            value = dot_nn(x[s], wv[s])
            if s == 0:
                acc[0] = key
                acc[1] = value
            else:
                acc[0] += key
                acc[1] += value
        h = ix[0]
        c = ix[1]

        def piece(which, hh, cc):
            at = pl.multiple_of((hh * 2 + cc) * HD, HD)
            return acc[which, :, pl.ds(at, HD)]

        for which, refs in ((1, (v0, vh, vhc, vc)), (0, (k0, kh, khc, kc))):
            for ref, (hh, cc) in zip(refs, ((h, c), (1 - h, c), (1 - h, 1 - c), (h, 1 - c))):
                ref[:rows, :] = piece(which, hh, cc).astype(ref.dtype)
        lane = lax.broadcasted_iota(jnp.int32, (extra, HD), 1)
        ids = jnp.zeros((extra, HD), F32)
        for e in range(count):
            ids = jnp.where(lane == e, ix[4 + e].astype(F32), ids)
        vc[rows:, :] = ids.astype(BF)

    extra = 16
    key = jax.ShapeDtypeStruct((rows, HD), F32)
    value = jax.ShapeDtypeStruct((rows, HD), BF)
    marked = jax.ShapeDtypeStruct((rows + extra, HD), BF)
    outs = (key, key, key, key, key, marked, value, value)
    return pl.pallas_call(
        body,
        out_shape=outs,
        grid_spec=pltpu.PrefetchScalarGridSpec(
            num_scalar_prefetch=1,
            grid=(1,),
            in_specs=[pl.BlockSpec(memory_space=pltpu.HBM)] * 3,
            out_specs=[spec(o.shape) for o in outs],
            scratch_shapes=[
                pltpu.VMEM((steps, rows, chunk), BF),
                pltpu.VMEM((steps, chunk, cols), BF),
                pltpu.VMEM((steps, chunk, cols), BF),
                pltpu.VMEM((2, rows, cols), F32),
                pltpu.SemaphoreType.DMA((3, steps)),
            ],
        ),
        compiler_params=pltpu.CompilerParams(vmem_limit_bytes=24 << 20),
        name="project",
        cost_estimate=cost(4),
    )(idx, in_hbm(feats), in_hbm(key_weight), in_hbm(value_weight))


def tile_cap(ix, tiles, sees, block, chunk, tile):
    half, j = divmod(tile, 2)
    shard = jnp.bitwise_xor(ix[2], chunk)
    image = tiles[half, shard * 2 + j]
    row = ix[2] * 2 + block
    return jnp.where(sees[row, image] > 0, jnp.float32(TOP), jnp.float32(NEG))


def forward(idx, tiles, sees, queries, grad_out, keys, values):
    rows = queries.shape[0]
    heads = 8
    width = heads * HD
    span = keys[0].shape[0]
    n = len(keys)
    total = span * n
    share = rows // 8
    per = span // TILE

    def body(ix, tl, se, q, g, k3, k2, k1, k0, v3, v2, v1, v0, out, st_out, y_scr, va):
        ks = (k0, k1, k2, k3)
        vs = (v0, v1, v2, v3)
        for j in range(n):
            va[j * span : (j + 1) * span, :HD] = vs[j][...]
        va[:, HD:] = jnp.ones((total, HD), BF)
        caps = [
            [tile_cap(ix, tl, se, b, j, e) for j in range(n) for e in range(per)]
            for b in range(2)
        ]
        lane = lax.broadcasted_iota(jnp.int32, (rows, HD), 1)
        st = jnp.zeros((rows, HD), F32)
        for h in range(heads):
            cols = slice(h * HD, (h + 1) * HD)
            slot = h % 2
            qh = q[:, cols]
            best = [None, None]
            for j in range(n):
                s = dot_nt(qh, ks[j][...]) * C2
                for b in range(2):
                    for e in range(per):
                        y = jnp.minimum(
                            s[b * TBLK : (b + 1) * TBLK, e * TILE : (e + 1) * TILE],
                            caps[b][j * per + e],
                        )
                        at = j * span + e * TILE
                        y_scr[slot, b * TBLK : (b + 1) * TBLK, at : at + TILE] = y
                        best[b] = y if best[b] is None else jnp.maximum(best[b], y)
            m = jnp.max(jnp.concatenate(best, axis=0), axis=1, keepdims=True)
            p = jnp.exp2(y_scr[slot] - m).astype(BF)
            r = dot_nn(p, va[...])
            den = r[:, HD:]
            o = r[:, :HD] / den
            out[:, :, cols] = o.astype(BF).reshape(8, share, HD)
            lse = m + jnp.log2(den)
            delta = jnp.sum(o * g[:, cols].astype(F32), axis=1, keepdims=True)
            st = jnp.where(lane == h, lse, st)
            st = jnp.where(lane == heads + h, delta, st)
        flat = st.T[: 2 * heads, :]
        for i in range(8):
            st_out[i] = flat

    own = lambda i, ix, tl, se: (0, ix[1])
    return pl.pallas_call(
        body,
        out_shape=(
            jax.ShapeDtypeStruct((8, share, width), BF),
            jax.ShapeDtypeStruct((8, 2 * heads, rows), F32),
        ),
        grid_spec=pltpu.PrefetchScalarGridSpec(
            num_scalar_prefetch=3,
            grid=(1,),
            in_specs=[pl.BlockSpec((rows, width), own)] * 2 + [spec((span, HD))] * 8,
            out_specs=[spec((8, share, width)), spec((8, 2 * heads, rows))],
            scratch_shapes=[
                pltpu.VMEM((2, rows, total), F32),
                pltpu.VMEM((total, 2 * HD), BF),
            ],
        ),
        compiler_params=pltpu.CompilerParams(vmem_limit_bytes=24 << 20),
        name="fwd",
        cost_estimate=cost(7),
    )(idx, tiles, sees, queries, grad_out, *keys[::-1], *values[::-1])


def merge_weights(st, heads):
    stats = [st[i] for i in range(8)]
    top = stats[0][:heads]
    for x in stats[1:]:
        top = jnp.maximum(top, x[:heads])
    ws = [jnp.exp2(x[:heads] - top) for x in stats]
    total = ws[0]
    delta = ws[0] * stats[0][heads:]
    for w, x in zip(ws[1:], stats[1:]):
        total = total + w
        delta = delta + w * x[heads:]
    inv = 1.0 / total
    return top + jnp.log2(total), delta * inv, [w * inv for w in ws]


def merge_parts(ix, x, ws, out, w_scr):
    _, share, width = x.shape
    heads = width // HD
    rows = w_scr.shape[0]
    pad = [jnp.zeros((HD - 8 * heads, rows), F32)]
    w_scr[...] = jnp.concatenate(ws + pad, axis=0).T
    w = w_scr[pl.ds(pl.multiple_of(ix[3] * share, share), share), :]
    for h in range(heads):
        cols = slice(h * HD, (h + 1) * HD)
        acc = jnp.zeros((share, HD), F32)
        for i in range(8):
            acc += x[i, :, cols].astype(F32) * w[:, i * heads + h : i * heads + h + 1]
        v = acc.astype(BF)
        for i in range(8):
            out[i, :, cols] = v


def backward(idx, tiles, sees, queries, grad_out, keys, values, stats, chunks, parts=None):
    rows = queries.shape[0]
    heads = 8
    width = heads * HD
    span = keys[0].shape[0]
    per = span // TILE
    n = len(chunks)

    def body(ix, tl, se, q, g, st, *refs):
        k_refs, v_refs, refs = refs[:n], refs[n : 2 * n], refs[2 * n :]
        lse, delta, ws = merge_weights(st, heads)
        if parts is None:
            outs, (dk, dv) = refs[:n], refs[n:]
        else:
            x, outs, (merged, dk, dv, w_scr) = refs[0], refs[1 : n + 1], refs[n + 1 :]
        lane = lax.broadcasted_iota(jnp.int32, (1, rows), 1)
        for chunk, k_ref, v_ref, out in zip(chunks, k_refs, v_refs, outs):
            caps = [
                jnp.where(
                    lane < TBLK,
                    tile_cap(ix, tl, se, 0, chunk, e),
                    tile_cap(ix, tl, se, 1, chunk, e),
                )
                for e in range(per)
            ]
            kk = k_ref[...]
            vv = v_ref[...]
            for h in range(heads):
                cols = slice(h * HD, (h + 1) * HD)
                qh = q[:, cols]
                gh = g[:, cols]
                s = dot_nt(kk, qh) * C2
                d = dot_nt(vv, gh)
                lh = lse[h : h + 1, :]
                dh = delta[h : h + 1, :]
                ps = []
                ds = []
                for e in range(per):
                    at = slice(e * TILE, (e + 1) * TILE)
                    p = jnp.exp2(jnp.minimum(s[at, :], caps[e]) - lh)
                    ps.append(p.astype(BF))
                    ds.append((p * (d[at, :] - dh) * SCALE).astype(BF))
                pv = dot_nn(jnp.concatenate(ps, axis=0), gh)
                pk = dot_nn(jnp.concatenate(ds, axis=0), qh)
                if h == 0:
                    dv[...] = pv
                    dk[...] = pk
                else:
                    dv[...] += pv
                    dk[...] += pk
            out[:, :HD] = dk[...].astype(out.dtype)
            out[:, HD:] = dv[...].astype(out.dtype)
        if parts is not None:
            merge_parts(ix, x, ws, merged, w_scr)

    own = lambda i, ix, tl, se: (0, ix[1])
    out_shape = [jax.ShapeDtypeStruct((span, 2 * HD), BF if k else F32) for k in chunks]
    in_specs = [pl.BlockSpec((rows, width), own)] * 2 + [spec(stats.shape)] + [spec((span, HD))] * (2 * n)
    out_specs = [spec((span, 2 * HD))] * n
    scratch = [pltpu.VMEM((span, HD), F32)] * 2
    more = []
    if parts is not None:
        more.append(parts)
        in_specs.append(spec(parts.shape))
        out_shape.append(jax.ShapeDtypeStruct(parts.shape, BF))
        out_specs.append(spec(parts.shape))
        scratch.append(pltpu.VMEM((rows, HD), F32))
    return pl.pallas_call(
        body,
        out_shape=out_shape,
        grid_spec=pltpu.PrefetchScalarGridSpec(
            num_scalar_prefetch=3,
            grid=(1,),
            in_specs=in_specs,
            out_specs=out_specs,
            scratch_shapes=scratch,
        ),
        compiler_params=pltpu.CompilerParams(vmem_limit_bytes=20 << 20),
        name="grads" + "".join(map(str, chunks)),
        cost_estimate=cost(3 * n),
    )(idx, tiles, sees, queries, grad_out, stats, *[keys[k] for k in chunks], *[values[k] for k in chunks], *more)


def fetch_weights(key_weight, value_weight, token):
    rows = key_weight.shape[0]
    steps = 4
    chunk = rows // steps

    def body(k_hbm, v_hbm, _, k_out, v_out, sems):
        copies = []
        for s in range(steps):
            at = slice(s * chunk, (s + 1) * chunk)
            copies.append(pltpu.make_async_copy(k_hbm.at[at, :], k_out.at[at, :], sems.at[0, s]))
            copies.append(pltpu.make_async_copy(v_hbm.at[at, :], v_out.at[at, :], sems.at[1, s]))
        for copy in copies:
            copy.start()
        for copy in copies:
            copy.wait()

    hbm = pl.BlockSpec(memory_space=pltpu.HBM)
    vmem = pl.BlockSpec(memory_space=pltpu.VMEM)
    return pl.pallas_call(
        body,
        out_shape=(
            pltpu.VMEM(key_weight.shape, BF),
            pltpu.VMEM(value_weight.shape, BF),
        ),
        in_specs=[hbm, hbm, pl.BlockSpec(memory_space=pl.ANY)],
        out_specs=[vmem, vmem],
        scratch_shapes=[pltpu.SemaphoreType.DMA((2, steps))],
        compiler_params=pltpu.CompilerParams(vmem_limit_bytes=2 << 20),
        name="fetch",
        cost_estimate=cost(4),
    )(in_hbm(key_weight), in_hbm(value_weight), token)


def feature_grad(idx, own, oc, oh, ohc, key_weight, value_weight, mine):
    rows = own.shape[0]
    feat, cols = key_weight.shape
    steps = 5
    chunk = feat // steps
    half = mine.shape[1]

    def body(ix, a, b, c_, d_, wk, wv, m_ref, out_hbm, attn, both, out, sems):
        h = ix[0]
        c = ix[1]

        mine_at = attn.at[:, pl.ds(pl.multiple_of(c * half, half), half)]
        place = pltpu.make_async_copy(m_ref, mine_at, sems.at[1, 0])

        def store(s):
            at = slice(s * chunk, (s + 1) * chunk)
            return pltpu.make_async_copy(out.at[s], out_hbm.at[:, at], sems.at[0, s])

        place.start()

        def put(hh, cc, x):
            at = pl.multiple_of((hh * 2 + cc) * HD, HD)
            both[0, :, pl.ds(at, HD)] = x[:, :HD]
            both[1, :, pl.ds(at, HD)] = x[:, HD:]

        put(h, c, a)
        put(h, 1 - c, b)
        put(1 - h, c, c_)
        put(1 - h, 1 - c, d_)
        for s in range(steps):
            at = slice(s * chunk, (s + 1) * chunk)
            out[s] = (dot_nt(both[0], wk[at, :]) + dot_nt(both[1], wv[at, :])).astype(BF)
            store(s).start()
        for s in range(steps):
            store(s).wait()
        place.wait()

    piece = spec((rows, 2 * HD))
    hbm = pl.BlockSpec(memory_space=pltpu.HBM)
    vmem = pl.BlockSpec(memory_space=pltpu.VMEM)
    anywhere = pl.BlockSpec(memory_space=pl.ANY)
    return pl.pallas_call(
        body,
        out_shape=(
            jax.ShapeDtypeStruct((rows, feat), BF),
            jax.ShapeDtypeStruct((rows, 2 * half), BF),
        ),
        grid_spec=pltpu.PrefetchScalarGridSpec(
            num_scalar_prefetch=1,
            grid=(1,),
            in_specs=[piece] * 4 + [vmem] * 2 + [anywhere],
            out_specs=[hbm, hbm],
            scratch_shapes=[
                pltpu.VMEM((2, rows, cols), BF),
                pltpu.VMEM((steps, rows, chunk), BF),
                pltpu.SemaphoreType.DMA((2, steps)),
            ],
        ),
        compiler_params=pltpu.CompilerParams(vmem_limit_bytes=8 << 20),
        name="feats",
        cost_estimate=cost(4),
    )(idx, own, oc, oh, ohc, key_weight, value_weight, mine)


def add_theirs(idx, attn, theirs):
    half = theirs.shape[1]

    def body(ix, _, t_ref, out, sem):
        at = pl.multiple_of((1 - ix[1]) * half, half)
        copy = pltpu.make_async_copy(t_ref, out.at[:, pl.ds(at, half)], sem)
        copy.start()
        copy.wait()

    hbm = pl.BlockSpec(memory_space=pltpu.HBM)
    return pl.pallas_call(
        body,
        out_shape=jax.ShapeDtypeStruct(attn.shape, BF),
        grid_spec=pltpu.PrefetchScalarGridSpec(
            num_scalar_prefetch=1,
            grid=(1,),
            in_specs=[hbm, pl.BlockSpec(memory_space=pl.ANY)],
            out_specs=hbm,
            scratch_shapes=[pltpu.SemaphoreType.DMA],
        ),
        input_output_aliases={1: 0},
        compiler_params=pltpu.CompilerParams(vmem_limit_bytes=1 << 20),
        name="theirs",
    )(idx, attn, theirs)


def solution(mesh):
    sizes = tuple(mesh.shape[a] for a in AXES)
    to_c = moved(sizes, lambda i, h, t: (i ^ 1, h, t))
    to_h = moved(sizes, lambda i, h, t: (i, 1 - h, t))
    to_hc = moved(sizes, lambda i, h, t: (i ^ 1, 1 - h, t))
    to_t = {k: moved(sizes, lambda i, h, t, k=k: (i, h, t ^ k)) for k in (1, 2, 3)}
    chips = [[m * 2 + c for m in range(8)] for c in range(2)]

    def swap8(x):
        return lax.all_to_all(x, "img", 0, 0, axis_index_groups=chips, tiled=True)

    def gathered(own):
        return [own] + [to_t[k](own) for k in (1, 2, 3)]

    def shards(image_feats, key_weight, value_weight, queries, grad_out, tile_image, text_sees):
        img = lax.axis_index("img")
        core = img % 2
        idx = jnp.stack([lax.axis_index("head"), core, lax.axis_index("txt"), img // 2]).astype(jnp.int32)
        idx = jnp.concatenate([idx, tile_image])
        own_k, c_k, h_k, hc_k, own_v, c_v, h_v, hc_v = project(
            idx, tile_image.shape[0], image_feats, key_weight, value_weight
        )
        h_v, hc_v, c_v = to_h(h_v), to_hc(hc_v), to_c(c_v)
        h_k, hc_k, c_k = to_h(h_k), to_hc(hc_k), to_c(c_k)
        rows = h_v.shape[0]
        others = c_v[rows, : tile_image.shape[0]].astype(jnp.int32)
        tiles = jnp.stack([tile_image, others])

        def owned(own, h, c, hc):
            near = own + h.astype(F32)
            far = c[:rows].astype(F32) + hc.astype(F32)
            return jnp.concatenate([near.astype(BF), far.astype(BF)], axis=0)

        values = gathered(owned(own_v, h_v, c_v, hc_v))
        keys = gathered(owned(own_k, h_k, c_k, hc_k))
        parts, stats = forward(idx, tiles, text_sees, queries, grad_out, keys, values)
        stats = swap8(stats)
        parts = swap8(parts)

        keys = [in_hbm(x) for x in keys]
        values = [in_hbm(x) for x in values]

        def grads(chunks, *more):
            return backward(idx, tiles, text_sees, queries, grad_out, keys, values, stats, chunks, *more)

        second, first = grads((2, 1))
        third, total, merged = grads((3, 0), parts)
        far = [to_t[2](second), to_t[1](first), to_t[3](third)]
        mine = swap8(merged).reshape(queries.shape[0], -1)
        for x in far:
            total = total + x.astype(F32)
        total = total.astype(BF)
        rows = total.shape[0] // 2
        near, other = total[:rows], total[rows:]
        side, ahead, across = to_c(other), to_h(near), to_hc(other)
        key_near, value_near = fetch_weights(key_weight, value_weight, total)
        mine, side = lax.optimization_barrier((mine, side))
        theirs = to_c(mine)
        grad_feats, attn_out = feature_grad(
            idx, near, side, ahead, across, key_near, value_near, mine
        )
        attn_out = add_theirs(idx, attn_out, theirs)
        return attn_out, grad_feats

    placed = (
        P(("img", "txt"), "head"),
        P("head", None),
        P("head", None),
        P("txt", "head"),
        P("txt", "head"),
        P("img"),
        P(),
    )
    return jax.shard_map(
        shards,
        mesh=mesh,
        in_specs=placed,
        out_specs=(P("txt", "head"), P(("img", "txt"), "head")),
        check_vma=False,
    )
```

```python
import math

import jax
import jax.numpy as jnp
from jax import lax
from jax.experimental import pallas as pl
from jax.experimental.pallas import tpu as pltpu
from jax.sharding import PartitionSpec as P

HD = 128
TILE = 128
TBLK = 128
BF = jnp.bfloat16
F32 = jnp.float32
SCALE = 1.0 / math.sqrt(HD)
C2 = SCALE * math.log2(math.e)
NEG = -1e30
TOP = 3e38
AXES = ("img", "head", "txt")
NT = (((1,), (1,)), ((), ()))


def dot_nt(a, b):
    return lax.dot_general(a, b, NT, preferred_element_type=F32)


def dot_nn(a, b):
    return jnp.dot(a, b, preferred_element_type=F32)


def moved(sizes, where):
    ni, nh, nt = sizes
    pairs = []
    for i in range(ni):
        for h in range(nh):
            for t in range(nt):
                a, b, c = where(i, h, t)
                pairs.append(((i * nh + h) * nt + t, (a * nh + b) * nt + c))
    return lambda x: lax.ppermute(x, AXES, pairs)


def cost(us):
    return pl.CostEstimate(flops=int(us * 1.1e9), transcendentals=0, bytes_accessed=1 << 16)


def spec(shape):
    zeros = (0,) * len(shape)
    return pl.BlockSpec(shape, lambda *_: zeros)


def in_hbm(x):
    return pltpu.with_memory_space_constraint(x, pltpu.HBM)


def project(idx, count, feats, key_weight, value_weight):
    rows, feat = feats.shape
    cols = key_weight.shape[1]
    steps = 5
    chunk = feat // steps

    def body(ix, x_hbm, wk_hbm, wv_hbm, k0, kc, kh, khc, v0, vc, vh, vhc, x, wk, wv, acc, sems):
        copies = []
        for s in range(steps):
            at = slice(s * chunk, (s + 1) * chunk)
            copies.append(
                (
                    pltpu.make_async_copy(x_hbm.at[:, at], x.at[s], sems.at[0, s]),
                    pltpu.make_async_copy(wk_hbm.at[at, :], wk.at[s], sems.at[1, s]),
                    pltpu.make_async_copy(wv_hbm.at[at, :], wv.at[s], sems.at[2, s]),
                )
            )
            for copy in copies[s]:
                copy.start()
        for s in range(steps):
            for copy in copies[s]:
                copy.wait()
            key = dot_nn(x[s], wk[s])
            value = dot_nn(x[s], wv[s])
            if s == 0:
                acc[0] = key
                acc[1] = value
            else:
                acc[0] += key
                acc[1] += value
        h = ix[0]
        c = ix[1]

        def piece(which, hh, cc):
            at = pl.multiple_of((hh * 2 + cc) * HD, HD)
            return acc[which, :, pl.ds(at, HD)]

        for which, refs in ((1, (v0, vh, vhc, vc)), (0, (k0, kh, khc, kc))):
            for ref, (hh, cc) in zip(refs, ((h, c), (1 - h, c), (1 - h, 1 - c), (h, 1 - c))):
                ref[:rows, :] = piece(which, hh, cc).astype(ref.dtype)
        lane = lax.broadcasted_iota(jnp.int32, (extra, HD), 1)
        ids = jnp.zeros((extra, HD), F32)
        for e in range(count):
            ids = jnp.where(lane == e, ix[4 + e].astype(F32), ids)
        vc[rows:, :] = ids.astype(BF)

    extra = 16
    key = jax.ShapeDtypeStruct((rows, HD), F32)
    value = jax.ShapeDtypeStruct((rows, HD), BF)
    marked = jax.ShapeDtypeStruct((rows + extra, HD), BF)
    outs = (key, key, key, key, key, marked, value, value)
    return pl.pallas_call(
        body,
        out_shape=outs,
        grid_spec=pltpu.PrefetchScalarGridSpec(
            num_scalar_prefetch=1,
            grid=(1,),
            in_specs=[pl.BlockSpec(memory_space=pltpu.HBM)] * 3,
            out_specs=[spec(o.shape) for o in outs],
            scratch_shapes=[
                pltpu.VMEM((steps, rows, chunk), BF),
                pltpu.VMEM((steps, chunk, cols), BF),
                pltpu.VMEM((steps, chunk, cols), BF),
                pltpu.VMEM((2, rows, cols), F32),
                pltpu.SemaphoreType.DMA((3, steps)),
            ],
        ),
        compiler_params=pltpu.CompilerParams(vmem_limit_bytes=24 << 20),
        name="project",
        cost_estimate=cost(4),
    )(idx, in_hbm(feats), in_hbm(key_weight), in_hbm(value_weight))


def tile_cap(ix, tiles, sees, block, chunk, tile):
    half, j = divmod(tile, 2)
    shard = jnp.bitwise_xor(ix[2], chunk)
    image = tiles[half, shard * 2 + j]
    row = ix[2] * 2 + block
    return jnp.where(sees[row, image] > 0, jnp.float32(TOP), jnp.float32(NEG))


def forward(idx, tiles, sees, queries, grad_out, keys, values):
    rows = queries.shape[0]
    heads = 8
    width = heads * HD
    span = keys[0].shape[0]
    n = len(keys)
    total = span * n
    share = rows // 8
    per = span // TILE

    def body(ix, tl, se, q, g, k3, k2, k1, k0, v3, v2, v1, v0, out, st_out, y_scr, va):
        ks = (k0, k1, k2, k3)
        vs = (v0, v1, v2, v3)
        for j in range(n):
            va[j * span : (j + 1) * span, :HD] = vs[j][...]
        va[:, HD:] = jnp.ones((total, HD), BF)
        caps = [
            [tile_cap(ix, tl, se, b, j, e) for j in range(n) for e in range(per)]
            for b in range(2)
        ]
        lane = lax.broadcasted_iota(jnp.int32, (rows, HD), 1)
        st = jnp.zeros((rows, HD), F32)
        for h in range(heads):
            cols = slice(h * HD, (h + 1) * HD)
            slot = h % 2
            qh = q[:, cols]
            best = [None, None]
            for j in range(n):
                s = dot_nt(qh, ks[j][...]) * C2
                for b in range(2):
                    for e in range(per):
                        y = jnp.minimum(
                            s[b * TBLK : (b + 1) * TBLK, e * TILE : (e + 1) * TILE],
                            caps[b][j * per + e],
                        )
                        at = j * span + e * TILE
                        y_scr[slot, b * TBLK : (b + 1) * TBLK, at : at + TILE] = y
                        best[b] = y if best[b] is None else jnp.maximum(best[b], y)
            m = jnp.max(jnp.concatenate(best, axis=0), axis=1, keepdims=True)
            p = jnp.exp2(y_scr[slot] - m).astype(BF)
            r = dot_nn(p, va[...])
            den = r[:, HD:]
            o = r[:, :HD] / den
            out[:, :, cols] = o.astype(BF).reshape(8, share, HD)
            lse = m + jnp.log2(den)
            delta = jnp.sum(o * g[:, cols].astype(F32), axis=1, keepdims=True)
            st = jnp.where(lane == h, lse, st)
            st = jnp.where(lane == heads + h, delta, st)
        flat = st.T[: 2 * heads, :]
        for i in range(8):
            st_out[i] = flat

    own = lambda i, ix, tl, se: (0, ix[1])
    return pl.pallas_call(
        body,
        out_shape=(
            jax.ShapeDtypeStruct((8, share, width), BF),
            jax.ShapeDtypeStruct((8, 2 * heads, rows), F32),
        ),
        grid_spec=pltpu.PrefetchScalarGridSpec(
            num_scalar_prefetch=3,
            grid=(1,),
            in_specs=[pl.BlockSpec((rows, width), own)] * 2 + [spec((span, HD))] * 8,
            out_specs=[spec((8, share, width)), spec((8, 2 * heads, rows))],
            scratch_shapes=[
                pltpu.VMEM((2, rows, total), F32),
                pltpu.VMEM((total, 2 * HD), BF),
            ],
        ),
        compiler_params=pltpu.CompilerParams(vmem_limit_bytes=24 << 20),
        name="fwd",
        cost_estimate=cost(7),
    )(idx, tiles, sees, queries, grad_out, *keys[::-1], *values[::-1])


def merge_weights(st, heads):
    stats = [st[i] for i in range(8)]
    top = stats[0][:heads]
    for x in stats[1:]:
        top = jnp.maximum(top, x[:heads])
    ws = [jnp.exp2(x[:heads] - top) for x in stats]
    total = ws[0]
    delta = ws[0] * stats[0][heads:]
    for w, x in zip(ws[1:], stats[1:]):
        total = total + w
        delta = delta + w * x[heads:]
    inv = 1.0 / total
    return top + jnp.log2(total), delta * inv, [w * inv for w in ws]


def merge_parts(ix, x, ws, out, w_scr):
    _, share, width = x.shape
    heads = width // HD
    rows = w_scr.shape[0]
    pad = [jnp.zeros((HD - 8 * heads, rows), F32)]
    w_scr[...] = jnp.concatenate(ws + pad, axis=0).T
    w = w_scr[pl.ds(pl.multiple_of(ix[3] * share, share), share), :]
    for h in range(heads):
        cols = slice(h * HD, (h + 1) * HD)
        acc = jnp.zeros((share, HD), F32)
        for i in range(8):
            acc += x[i, :, cols].astype(F32) * w[:, i * heads + h : i * heads + h + 1]
        v = acc.astype(BF)
        for i in range(8):
            out[i, :, cols] = v


def backward(idx, tiles, sees, queries, grad_out, keys, values, stats, chunks, parts=None, after=None):
    rows = queries.shape[0]
    heads = 8
    width = heads * HD
    span = keys[0].shape[0]
    per = span // TILE
    n = len(chunks)

    def body(ix, tl, se, q, g, st, *refs):
        k_refs, v_refs, refs = refs[:n], refs[n : 2 * n], refs[2 * n :]
        lse, delta, ws = merge_weights(st, heads)
        if parts is None:
            outs, (dk, dv) = refs[:n], refs[n:]
        else:
            x, outs, (merged, dk, dv, w_scr) = refs[0], refs[2 : n + 2], refs[n + 2 :]
        lane = lax.broadcasted_iota(jnp.int32, (1, rows), 1)
        for chunk, k_ref, v_ref, out in zip(chunks, k_refs, v_refs, outs):
            caps = [
                jnp.where(
                    lane < TBLK,
                    tile_cap(ix, tl, se, 0, chunk, e),
                    tile_cap(ix, tl, se, 1, chunk, e),
                )
                for e in range(per)
            ]
            kk = k_ref[...]
            vv = v_ref[...]
            for h in range(heads):
                cols = slice(h * HD, (h + 1) * HD)
                qh = q[:, cols]
                gh = g[:, cols]
                s = dot_nt(kk, qh) * C2
                d = dot_nt(vv, gh)
                lh = lse[h : h + 1, :]
                dh = delta[h : h + 1, :]
                ps = []
                ds = []
                for e in range(per):
                    at = slice(e * TILE, (e + 1) * TILE)
                    p = jnp.exp2(jnp.minimum(s[at, :], caps[e]) - lh)
                    ps.append(p.astype(BF))
                    ds.append((p * (d[at, :] - dh) * SCALE).astype(BF))
                pv = dot_nn(jnp.concatenate(ps, axis=0), gh)
                pk = dot_nn(jnp.concatenate(ds, axis=0), qh)
                if h == 0:
                    dv[...] = pv
                    dk[...] = pk
                else:
                    dv[...] += pv
                    dk[...] += pk
            out[:, :HD] = dk[...].astype(out.dtype)
            out[:, HD:] = dv[...].astype(out.dtype)
        if parts is not None:
            merge_parts(ix, x, ws, merged, w_scr)

    own = lambda i, ix, tl, se: (0, ix[1])
    out_shape = [jax.ShapeDtypeStruct((span, 2 * HD), BF if k else F32) for k in chunks]
    in_specs = [pl.BlockSpec((rows, width), own)] * 2 + [spec(stats.shape)] + [spec((span, HD))] * (2 * n)
    out_specs = [spec((span, 2 * HD))] * n
    scratch = [pltpu.VMEM((span, HD), F32)] * 2
    more = []
    if parts is not None:
        more += [parts, after]
        in_specs += [spec(parts.shape), pl.BlockSpec(memory_space=pl.ANY)]
        out_shape.append(jax.ShapeDtypeStruct(parts.shape, BF))
        out_specs.append(spec(parts.shape))
        scratch.append(pltpu.VMEM((rows, HD), F32))
    return pl.pallas_call(
        body,
        out_shape=out_shape,
        grid_spec=pltpu.PrefetchScalarGridSpec(
            num_scalar_prefetch=3,
            grid=(1,),
            in_specs=in_specs,
            out_specs=out_specs,
            scratch_shapes=scratch,
        ),
        compiler_params=pltpu.CompilerParams(vmem_limit_bytes=20 << 20),
        name="grads" + "".join(map(str, chunks)),
        cost_estimate=cost(3 * n),
    )(idx, tiles, sees, queries, grad_out, stats, *[keys[k] for k in chunks], *[values[k] for k in chunks], *more)


def fetch_weights(key_weight, value_weight, token):
    rows = key_weight.shape[0]
    steps = 4
    chunk = rows // steps

    def body(k_hbm, v_hbm, _, k_out, v_out, sems):
        copies = []
        for s in range(steps):
            at = slice(s * chunk, (s + 1) * chunk)
            copies.append(pltpu.make_async_copy(k_hbm.at[at, :], k_out.at[at, :], sems.at[0, s]))
            copies.append(pltpu.make_async_copy(v_hbm.at[at, :], v_out.at[at, :], sems.at[1, s]))
        for copy in copies:
            copy.start()
        for copy in copies:
            copy.wait()

    hbm = pl.BlockSpec(memory_space=pltpu.HBM)
    vmem = pl.BlockSpec(memory_space=pltpu.VMEM)
    return pl.pallas_call(
        body,
        out_shape=(
            pltpu.VMEM(key_weight.shape, BF),
            pltpu.VMEM(value_weight.shape, BF),
        ),
        in_specs=[hbm, hbm, pl.BlockSpec(memory_space=pl.ANY)],
        out_specs=[vmem, vmem],
        scratch_shapes=[pltpu.SemaphoreType.DMA((2, steps))],
        compiler_params=pltpu.CompilerParams(vmem_limit_bytes=2 << 20),
        name="fetch",
        cost_estimate=cost(4),
    )(in_hbm(key_weight), in_hbm(value_weight), token)


def feature_grad(idx, own, oc, oh, ohc, key_weight, value_weight, mine):
    rows = own.shape[0]
    feat, cols = key_weight.shape
    steps = 5
    chunk = feat // steps
    half = mine.shape[1]

    def body(ix, a, b, c_, d_, wk, wv, m_ref, out_hbm, attn, both, out, sems):
        h = ix[0]
        c = ix[1]

        mine_at = attn.at[:, pl.ds(pl.multiple_of(c * half, half), half)]
        place = pltpu.make_async_copy(m_ref, mine_at, sems.at[1, 0])

        def store(s):
            at = slice(s * chunk, (s + 1) * chunk)
            return pltpu.make_async_copy(out.at[s], out_hbm.at[:, at], sems.at[0, s])

        place.start()

        def put(hh, cc, x):
            at = pl.multiple_of((hh * 2 + cc) * HD, HD)
            both[0, :, pl.ds(at, HD)] = x[:, :HD]
            both[1, :, pl.ds(at, HD)] = x[:, HD:]

        put(h, c, a)
        put(h, 1 - c, b)
        put(1 - h, c, c_)
        put(1 - h, 1 - c, d_)
        for s in range(steps):
            at = slice(s * chunk, (s + 1) * chunk)
            out[s] = (dot_nt(both[0], wk[at, :]) + dot_nt(both[1], wv[at, :])).astype(BF)
            store(s).start()
        for s in range(steps):
            store(s).wait()
        place.wait()

    piece = spec((rows, 2 * HD))
    hbm = pl.BlockSpec(memory_space=pltpu.HBM)
    vmem = pl.BlockSpec(memory_space=pltpu.VMEM)
    anywhere = pl.BlockSpec(memory_space=pl.ANY)
    return pl.pallas_call(
        body,
        out_shape=(
            jax.ShapeDtypeStruct((rows, feat), BF),
            jax.ShapeDtypeStruct((rows, 2 * half), BF),
        ),
        grid_spec=pltpu.PrefetchScalarGridSpec(
            num_scalar_prefetch=1,
            grid=(1,),
            in_specs=[piece] * 4 + [vmem] * 2 + [anywhere],
            out_specs=[hbm, hbm],
            scratch_shapes=[
                pltpu.VMEM((2, rows, cols), BF),
                pltpu.VMEM((steps, rows, chunk), BF),
                pltpu.SemaphoreType.DMA((2, steps)),
            ],
        ),
        compiler_params=pltpu.CompilerParams(vmem_limit_bytes=8 << 20),
        name="feats",
        cost_estimate=cost(4),
    )(idx, own, oc, oh, ohc, key_weight, value_weight, mine)


def add_theirs(idx, attn, theirs):
    half = theirs.shape[1]

    def body(ix, _, t_ref, out, sem):
        at = pl.multiple_of((1 - ix[1]) * half, half)
        copy = pltpu.make_async_copy(t_ref, out.at[:, pl.ds(at, half)], sem)
        copy.start()
        copy.wait()

    hbm = pl.BlockSpec(memory_space=pltpu.HBM)
    return pl.pallas_call(
        body,
        out_shape=jax.ShapeDtypeStruct(attn.shape, BF),
        grid_spec=pltpu.PrefetchScalarGridSpec(
            num_scalar_prefetch=1,
            grid=(1,),
            in_specs=[hbm, pl.BlockSpec(memory_space=pl.ANY)],
            out_specs=hbm,
            scratch_shapes=[pltpu.SemaphoreType.DMA],
        ),
        input_output_aliases={1: 0},
        compiler_params=pltpu.CompilerParams(vmem_limit_bytes=1 << 20),
        name="theirs",
    )(idx, attn, theirs)


def solution(mesh):
    sizes = tuple(mesh.shape[a] for a in AXES)
    to_c = moved(sizes, lambda i, h, t: (i ^ 1, h, t))
    to_h = moved(sizes, lambda i, h, t: (i, 1 - h, t))
    to_hc = moved(sizes, lambda i, h, t: (i ^ 1, 1 - h, t))
    to_t = {k: moved(sizes, lambda i, h, t, k=k: (i, h, t ^ k)) for k in (1, 2, 3)}
    chips = [[m * 2 + c for m in range(8)] for c in range(2)]

    def swap8(x):
        return lax.all_to_all(x, "img", 0, 0, axis_index_groups=chips, tiled=True)

    def gathered(own):
        return [own] + [to_t[k](own) for k in (1, 2, 3)]

    def shards(image_feats, key_weight, value_weight, queries, grad_out, tile_image, text_sees):
        img = lax.axis_index("img")
        core = img % 2
        idx = jnp.stack([lax.axis_index("head"), core, lax.axis_index("txt"), img // 2]).astype(jnp.int32)
        idx = jnp.concatenate([idx, tile_image])
        own_k, c_k, h_k, hc_k, own_v, c_v, h_v, hc_v = project(
            idx, tile_image.shape[0], image_feats, key_weight, value_weight
        )
        h_v, hc_v, c_v = to_h(h_v), to_hc(hc_v), to_c(c_v)
        h_k, hc_k, c_k = to_h(h_k), to_hc(hc_k), to_c(c_k)
        rows = h_v.shape[0]
        others = c_v[rows, : tile_image.shape[0]].astype(jnp.int32)
        tiles = jnp.stack([tile_image, others])

        def owned(own, h, c, hc):
            near = own + h.astype(F32)
            far = c[:rows].astype(F32) + hc.astype(F32)
            return jnp.concatenate([near.astype(BF), far.astype(BF)], axis=0)

        values = gathered(owned(own_v, h_v, c_v, hc_v))
        keys = gathered(owned(own_k, h_k, c_k, hc_k))
        parts, stats = forward(idx, tiles, text_sees, queries, grad_out, keys, values)
        stats = swap8(stats)
        parts = swap8(parts)

        keys = [in_hbm(x) for x in keys]
        values = [in_hbm(x) for x in values]

        def grads(chunks, *more):
            return backward(idx, tiles, text_sees, queries, grad_out, keys, values, stats, chunks, *more)

        second, first = grads((2, 1))
        (third,) = grads((3,))
        total, merged = grads((0,), parts, third)
        far = [to_t[2](second), to_t[1](first), to_t[3](third)]
        mine = swap8(merged).reshape(queries.shape[0], -1)
        for x in far:
            total = total + x.astype(F32)
        total = total.astype(BF)
        rows = total.shape[0] // 2
        near, other = total[:rows], total[rows:]
        side, ahead, across = to_c(other), to_h(near), to_hc(other)
        key_near, value_near = fetch_weights(key_weight, value_weight, total)
        mine, side = lax.optimization_barrier((mine, side))
        theirs = to_c(mine)
        grad_feats, attn_out = feature_grad(
            idx, near, side, ahead, across, key_near, value_near, mine
        )
        attn_out = add_theirs(idx, attn_out, theirs)
        return attn_out, grad_feats

    placed = (
        P(("img", "txt"), "head"),
        P("head", None),
        P("head", None),
        P("txt", "head"),
        P("txt", "head"),
        P("img"),
        P(),
    )
    return jax.shard_map(
        shards,
        mesh=mesh,
        in_specs=placed,
        out_specs=(P("txt", "head"), P(("img", "txt"), "head")),
        check_vma=False,
    )
```

```python
import math

import jax
import jax.numpy as jnp
from jax import lax
from jax.experimental import pallas as pl
from jax.experimental.pallas import tpu as pltpu
from jax.sharding import PartitionSpec as P

HD = 128
TILE = 128
TBLK = 128
BF = jnp.bfloat16
F32 = jnp.float32
SCALE = 1.0 / math.sqrt(HD)
C2 = SCALE * math.log2(math.e)
NEG = -1e30
TOP = 3e38
AXES = ("img", "head", "txt")
NT = (((1,), (1,)), ((), ()))


def dot_nt(a, b):
    return lax.dot_general(a, b, NT, preferred_element_type=F32)


def dot_nn(a, b):
    return jnp.dot(a, b, preferred_element_type=F32)


def moved(sizes, where):
    ni, nh, nt = sizes
    pairs = []
    for i in range(ni):
        for h in range(nh):
            for t in range(nt):
                a, b, c = where(i, h, t)
                pairs.append(((i * nh + h) * nt + t, (a * nh + b) * nt + c))
    return lambda x: lax.ppermute(x, AXES, pairs)


def cost(us):
    return pl.CostEstimate(flops=int(us * 1.1e9), transcendentals=0, bytes_accessed=1 << 16)


def spec(shape):
    zeros = (0,) * len(shape)
    return pl.BlockSpec(shape, lambda *_: zeros)


def in_hbm(x):
    return pltpu.with_memory_space_constraint(x, pltpu.HBM)


def project(idx, count, feats, key_weight, value_weight):
    rows, feat = feats.shape
    cols = key_weight.shape[1]
    steps = 5
    chunk = feat // steps

    def body(ix, x_hbm, wk_hbm, wv_hbm, k0, kc, kh, khc, v0, vc, vh, vhc, x, wk, wv, acc, sems):
        copies = []
        for s in range(steps):
            at = slice(s * chunk, (s + 1) * chunk)
            copies.append(
                (
                    pltpu.make_async_copy(x_hbm.at[:, at], x.at[s], sems.at[0, s]),
                    pltpu.make_async_copy(wk_hbm.at[at, :], wk.at[s], sems.at[1, s]),
                    pltpu.make_async_copy(wv_hbm.at[at, :], wv.at[s], sems.at[2, s]),
                )
            )
            for copy in copies[s]:
                copy.start()
        for s in range(steps):
            for copy in copies[s]:
                copy.wait()
            key = dot_nn(x[s], wk[s])
            value = dot_nn(x[s], wv[s])
            if s == 0:
                acc[0] = key
                acc[1] = value
            else:
                acc[0] += key
                acc[1] += value
        h = ix[0]
        c = ix[1]

        def piece(which, hh, cc):
            at = pl.multiple_of((hh * 2 + cc) * HD, HD)
            return acc[which, :, pl.ds(at, HD)]

        for which, refs in ((1, (v0, vh, vhc, vc)), (0, (k0, kh, khc, kc))):
            for ref, (hh, cc) in zip(refs, ((h, c), (1 - h, c), (1 - h, 1 - c), (h, 1 - c))):
                ref[:rows, :] = piece(which, hh, cc).astype(ref.dtype)
        lane = lax.broadcasted_iota(jnp.int32, (extra, HD), 1)
        ids = jnp.zeros((extra, HD), F32)
        for e in range(count):
            ids = jnp.where(lane == e, ix[4 + e].astype(F32), ids)
        vc[rows:, :] = ids.astype(BF)

    extra = 16
    key = jax.ShapeDtypeStruct((rows, HD), F32)
    value = jax.ShapeDtypeStruct((rows, HD), BF)
    marked = jax.ShapeDtypeStruct((rows + extra, HD), BF)
    outs = (key, key, key, key, key, marked, value, value)
    return pl.pallas_call(
        body,
        out_shape=outs,
        grid_spec=pltpu.PrefetchScalarGridSpec(
            num_scalar_prefetch=1,
            grid=(1,),
            in_specs=[pl.BlockSpec(memory_space=pltpu.HBM)] * 3,
            out_specs=[spec(o.shape) for o in outs],
            scratch_shapes=[
                pltpu.VMEM((steps, rows, chunk), BF),
                pltpu.VMEM((steps, chunk, cols), BF),
                pltpu.VMEM((steps, chunk, cols), BF),
                pltpu.VMEM((2, rows, cols), F32),
                pltpu.SemaphoreType.DMA((3, steps)),
            ],
        ),
        compiler_params=pltpu.CompilerParams(vmem_limit_bytes=24 << 20),
        name="project",
        cost_estimate=cost(4),
    )(idx, in_hbm(feats), in_hbm(key_weight), in_hbm(value_weight))


def tile_cap(ix, tiles, sees, block, chunk, tile):
    half, j = divmod(tile, 2)
    shard = jnp.bitwise_xor(ix[2], chunk)
    image = tiles[half, shard * 2 + j]
    row = ix[2] * 2 + block
    return jnp.where(sees[row, image] > 0, jnp.float32(TOP), jnp.float32(NEG))


def forward(idx, tiles, sees, queries, grad_out, keys, values):
    rows = queries.shape[0]
    heads = 8
    width = heads * HD
    span = keys[0].shape[0]
    n = len(keys)
    total = span * n
    share = rows // 8
    per = span // TILE

    def body(ix, tl, se, q, g, k3, k2, k1, k0, v3, v2, v1, v0, out, st_out, y_scr, va):
        ks = (k0, k1, k2, k3)
        vs = (v0, v1, v2, v3)
        for j in range(n):
            va[j * span : (j + 1) * span, :HD] = vs[j][...]
        va[:, HD:] = jnp.ones((total, HD), BF)
        caps = [
            [tile_cap(ix, tl, se, b, j, e) for j in range(n) for e in range(per)]
            for b in range(2)
        ]
        lane = lax.broadcasted_iota(jnp.int32, (rows, HD), 1)
        st = jnp.zeros((rows, HD), F32)
        for h in range(heads):
            cols = slice(h * HD, (h + 1) * HD)
            slot = h % 2
            qh = q[:, cols]
            best = [None, None]
            for j in range(n):
                s = dot_nt(qh, ks[j][...]) * C2
                for b in range(2):
                    for e in range(per):
                        y = jnp.minimum(
                            s[b * TBLK : (b + 1) * TBLK, e * TILE : (e + 1) * TILE],
                            caps[b][j * per + e],
                        )
                        at = j * span + e * TILE
                        y_scr[slot, b * TBLK : (b + 1) * TBLK, at : at + TILE] = y
                        best[b] = y if best[b] is None else jnp.maximum(best[b], y)
            m = jnp.max(jnp.concatenate(best, axis=0), axis=1, keepdims=True)
            p = jnp.exp2(y_scr[slot] - m).astype(BF)
            r = dot_nn(p, va[...])
            den = r[:, HD:]
            o = r[:, :HD] / den
            out[:, :, cols] = o.astype(BF).reshape(8, share, HD)
            lse = m + jnp.log2(den)
            delta = jnp.sum(o * g[:, cols].astype(F32), axis=1, keepdims=True)
            st = jnp.where(lane == h, lse, st)
            st = jnp.where(lane == heads + h, delta, st)
        flat = st.T[: 2 * heads, :]
        for i in range(8):
            st_out[i] = flat

    own = lambda i, ix, tl, se: (0, ix[1])
    return pl.pallas_call(
        body,
        out_shape=(
            jax.ShapeDtypeStruct((8, share, width), BF),
            jax.ShapeDtypeStruct((8, 2 * heads, rows), F32),
        ),
        grid_spec=pltpu.PrefetchScalarGridSpec(
            num_scalar_prefetch=3,
            grid=(1,),
            in_specs=[pl.BlockSpec((rows, width), own)] * 2 + [spec((span, HD))] * 8,
            out_specs=[spec((8, share, width)), spec((8, 2 * heads, rows))],
            scratch_shapes=[
                pltpu.VMEM((2, rows, total), F32),
                pltpu.VMEM((total, 2 * HD), BF),
            ],
        ),
        compiler_params=pltpu.CompilerParams(vmem_limit_bytes=24 << 20),
        name="fwd",
        cost_estimate=cost(7),
    )(idx, tiles, sees, queries, grad_out, *keys[::-1], *values[::-1])


def merge_weights(st, heads):
    stats = [st[i] for i in range(8)]
    top = stats[0][:heads]
    for x in stats[1:]:
        top = jnp.maximum(top, x[:heads])
    ws = [jnp.exp2(x[:heads] - top) for x in stats]
    total = ws[0]
    delta = ws[0] * stats[0][heads:]
    for w, x in zip(ws[1:], stats[1:]):
        total = total + w
        delta = delta + w * x[heads:]
    inv = 1.0 / total
    return top + jnp.log2(total), delta * inv, [w * inv for w in ws]


def merge_parts(ix, x, ws, out, w_scr):
    _, share, width = x.shape
    heads = width // HD
    rows = w_scr.shape[0]
    pad = [jnp.zeros((HD - 8 * heads, rows), F32)]
    w_scr[...] = jnp.concatenate(ws + pad, axis=0).T
    w = w_scr[pl.ds(pl.multiple_of(ix[3] * share, share), share), :]
    for h in range(heads):
        cols = slice(h * HD, (h + 1) * HD)
        acc = jnp.zeros((share, HD), F32)
        for i in range(8):
            acc += x[i, :, cols].astype(F32) * w[:, i * heads + h : i * heads + h + 1]
        v = acc.astype(BF)
        for i in range(8):
            out[i, :, cols] = v


def backward(idx, tiles, sees, queries, grad_out, keys, values, stats, chunks, parts=None):
    rows = queries.shape[0]
    heads = 8
    width = heads * HD
    span = keys[0].shape[0]
    per = span // TILE
    n = len(chunks)

    def body(ix, tl, se, q, g, st, *refs):
        k_refs, v_refs, refs = refs[:n], refs[n : 2 * n], refs[2 * n :]
        lse, delta, ws = merge_weights(st, heads)
        if parts is None:
            outs, (dk, dv) = refs[:n], refs[n:]
        else:
            x, outs, (merged, dk, dv, w_scr) = refs[0], refs[1 : n + 1], refs[n + 1 :]
        lane = lax.broadcasted_iota(jnp.int32, (1, rows), 1)
        for chunk, k_ref, v_ref, out in zip(chunks, k_refs, v_refs, outs):
            caps = [
                jnp.where(
                    lane < TBLK,
                    tile_cap(ix, tl, se, 0, chunk, e),
                    tile_cap(ix, tl, se, 1, chunk, e),
                )
                for e in range(per)
            ]
            kk = k_ref[...]
            vv = v_ref[...]
            for h in range(heads):
                cols = slice(h * HD, (h + 1) * HD)
                qh = q[:, cols]
                gh = g[:, cols]
                s = dot_nt(kk, qh) * C2
                d = dot_nt(vv, gh)
                lh = lse[h : h + 1, :]
                dh = delta[h : h + 1, :]
                ps = []
                ds = []
                for e in range(per):
                    at = slice(e * TILE, (e + 1) * TILE)
                    p = jnp.exp2(s[at, :] - jnp.where(caps[e] > 0, lh, -NEG))
                    ps.append(p.astype(BF))
                    ds.append((p * (d[at, :] - dh) * SCALE).astype(BF))
                pv = dot_nn(jnp.concatenate(ps, axis=0), gh)
                pk = dot_nn(jnp.concatenate(ds, axis=0), qh)
                if h == 0:
                    dv[...] = pv
                    dk[...] = pk
                else:
                    dv[...] += pv
                    dk[...] += pk
            out[:, :HD] = dk[...].astype(out.dtype)
            out[:, HD:] = dv[...].astype(out.dtype)
        if parts is not None:
            merge_parts(ix, x, ws, merged, w_scr)

    own = lambda i, ix, tl, se: (0, ix[1])
    out_shape = [jax.ShapeDtypeStruct((span, 2 * HD), BF if k else F32) for k in chunks]
    in_specs = [pl.BlockSpec((rows, width), own)] * 2 + [spec(stats.shape)] + [spec((span, HD))] * (2 * n)
    out_specs = [spec((span, 2 * HD))] * n
    scratch = [pltpu.VMEM((span, HD), F32)] * 2
    more = []
    if parts is not None:
        more.append(parts)
        in_specs.append(spec(parts.shape))
        out_shape.append(jax.ShapeDtypeStruct(parts.shape, BF))
        out_specs.append(spec(parts.shape))
        scratch.append(pltpu.VMEM((rows, HD), F32))
    return pl.pallas_call(
        body,
        out_shape=out_shape,
        grid_spec=pltpu.PrefetchScalarGridSpec(
            num_scalar_prefetch=3,
            grid=(1,),
            in_specs=in_specs,
            out_specs=out_specs,
            scratch_shapes=scratch,
        ),
        compiler_params=pltpu.CompilerParams(vmem_limit_bytes=20 << 20),
        name="grads" + "".join(map(str, chunks)),
        cost_estimate=cost(3 * n),
    )(idx, tiles, sees, queries, grad_out, stats, *[keys[k] for k in chunks], *[values[k] for k in chunks], *more)


def fetch_weights(key_weight, value_weight, token):
    rows = key_weight.shape[0]
    steps = 4
    chunk = rows // steps

    def body(k_hbm, v_hbm, _, k_out, v_out, sems):
        copies = []
        for s in range(steps):
            at = slice(s * chunk, (s + 1) * chunk)
            copies.append(pltpu.make_async_copy(k_hbm.at[at, :], k_out.at[at, :], sems.at[0, s]))
            copies.append(pltpu.make_async_copy(v_hbm.at[at, :], v_out.at[at, :], sems.at[1, s]))
        for copy in copies:
            copy.start()
        for copy in copies:
            copy.wait()

    hbm = pl.BlockSpec(memory_space=pltpu.HBM)
    vmem = pl.BlockSpec(memory_space=pltpu.VMEM)
    return pl.pallas_call(
        body,
        out_shape=(
            pltpu.VMEM(key_weight.shape, BF),
            pltpu.VMEM(value_weight.shape, BF),
        ),
        in_specs=[hbm, hbm, pl.BlockSpec(memory_space=pl.ANY)],
        out_specs=[vmem, vmem],
        scratch_shapes=[pltpu.SemaphoreType.DMA((2, steps))],
        compiler_params=pltpu.CompilerParams(vmem_limit_bytes=2 << 20),
        name="fetch",
        cost_estimate=cost(4),
    )(in_hbm(key_weight), in_hbm(value_weight), token)


def feature_grad(idx, own, oc, oh, ohc, key_weight, value_weight, mine):
    rows = own.shape[0]
    feat, cols = key_weight.shape
    steps = 5
    chunk = feat // steps
    half = mine.shape[1]

    def body(ix, a, b, c_, d_, wk, wv, m_ref, out_hbm, attn, both, out, sems):
        h = ix[0]
        c = ix[1]

        mine_at = attn.at[:, pl.ds(pl.multiple_of(c * half, half), half)]
        place = pltpu.make_async_copy(m_ref, mine_at, sems.at[1, 0])

        def store(s):
            at = slice(s * chunk, (s + 1) * chunk)
            return pltpu.make_async_copy(out.at[s], out_hbm.at[:, at], sems.at[0, s])

        place.start()

        def put(hh, cc, x):
            at = pl.multiple_of((hh * 2 + cc) * HD, HD)
            both[0, :, pl.ds(at, HD)] = x[:, :HD]
            both[1, :, pl.ds(at, HD)] = x[:, HD:]

        put(h, c, a)
        put(h, 1 - c, b)
        put(1 - h, c, c_)
        put(1 - h, 1 - c, d_)
        for s in range(steps):
            at = slice(s * chunk, (s + 1) * chunk)
            out[s] = (dot_nt(both[0], wk[at, :]) + dot_nt(both[1], wv[at, :])).astype(BF)
            store(s).start()
        for s in range(steps):
            store(s).wait()
        place.wait()

    piece = spec((rows, 2 * HD))
    hbm = pl.BlockSpec(memory_space=pltpu.HBM)
    vmem = pl.BlockSpec(memory_space=pltpu.VMEM)
    anywhere = pl.BlockSpec(memory_space=pl.ANY)
    return pl.pallas_call(
        body,
        out_shape=(
            jax.ShapeDtypeStruct((rows, feat), BF),
            jax.ShapeDtypeStruct((rows, 2 * half), BF),
        ),
        grid_spec=pltpu.PrefetchScalarGridSpec(
            num_scalar_prefetch=1,
            grid=(1,),
            in_specs=[piece] * 4 + [vmem] * 2 + [anywhere],
            out_specs=[hbm, hbm],
            scratch_shapes=[
                pltpu.VMEM((2, rows, cols), BF),
                pltpu.VMEM((steps, rows, chunk), BF),
                pltpu.SemaphoreType.DMA((2, steps)),
            ],
        ),
        compiler_params=pltpu.CompilerParams(vmem_limit_bytes=8 << 20),
        name="feats",
        cost_estimate=cost(4),
    )(idx, own, oc, oh, ohc, key_weight, value_weight, mine)


def add_theirs(idx, attn, theirs):
    half = theirs.shape[1]

    rows = theirs.shape[0]
    parts = 4

    def body(ix, _, t_ref, out, sems):
        at = pl.ds(pl.multiple_of((1 - ix[1]) * half, half), half)
        copies = []
        for k in range(parts):
            some = slice(k * rows // parts, (k + 1) * rows // parts)
            copies.append(pltpu.make_async_copy(t_ref.at[some, :], out.at[some, at], sems.at[k]))
        for copy in copies:
            copy.start()
        for copy in copies:
            copy.wait()

    hbm = pl.BlockSpec(memory_space=pltpu.HBM)
    return pl.pallas_call(
        body,
        out_shape=jax.ShapeDtypeStruct(attn.shape, BF),
        grid_spec=pltpu.PrefetchScalarGridSpec(
            num_scalar_prefetch=1,
            grid=(1,),
            in_specs=[hbm, pl.BlockSpec(memory_space=pl.ANY)],
            out_specs=hbm,
            scratch_shapes=[pltpu.SemaphoreType.DMA((parts,))],
        ),
        input_output_aliases={1: 0},
        compiler_params=pltpu.CompilerParams(vmem_limit_bytes=1 << 20),
        name="theirs",
    )(idx, attn, theirs)


def solution(mesh):
    sizes = tuple(mesh.shape[a] for a in AXES)
    to_c = moved(sizes, lambda i, h, t: (i ^ 1, h, t))
    to_h = moved(sizes, lambda i, h, t: (i, 1 - h, t))
    to_hc = moved(sizes, lambda i, h, t: (i ^ 1, 1 - h, t))
    to_t = {k: moved(sizes, lambda i, h, t, k=k: (i, h, t ^ k)) for k in (1, 2, 3)}
    chips = [[m * 2 + c for m in range(8)] for c in range(2)]

    def swap8(x):
        return lax.all_to_all(x, "img", 0, 0, axis_index_groups=chips, tiled=True)

    def gathered(own):
        return [own] + [to_t[k](own) for k in (1, 2, 3)]

    def shards(image_feats, key_weight, value_weight, queries, grad_out, tile_image, text_sees):
        img = lax.axis_index("img")
        core = img % 2
        idx = jnp.stack([lax.axis_index("head"), core, lax.axis_index("txt"), img // 2]).astype(jnp.int32)
        idx = jnp.concatenate([idx, tile_image])
        own_k, c_k, h_k, hc_k, own_v, c_v, h_v, hc_v = project(
            idx, tile_image.shape[0], image_feats, key_weight, value_weight
        )
        h_v, hc_v, c_v = to_h(h_v), to_hc(hc_v), to_c(c_v)
        h_k, hc_k, c_k = to_h(h_k), to_hc(hc_k), to_c(c_k)
        rows = h_v.shape[0]
        others = c_v[rows, : tile_image.shape[0]].astype(jnp.int32)
        tiles = jnp.stack([tile_image, others])

        def owned(own, h, c, hc):
            near = own + h.astype(F32)
            far = c[:rows].astype(F32) + hc.astype(F32)
            return jnp.concatenate([near.astype(BF), far.astype(BF)], axis=0)

        values = gathered(owned(own_v, h_v, c_v, hc_v))
        keys = gathered(owned(own_k, h_k, c_k, hc_k))
        parts, stats = forward(idx, tiles, text_sees, queries, grad_out, keys, values)
        stats = swap8(stats)
        parts = swap8(parts)

        keys = [in_hbm(x) for x in keys]
        values = [in_hbm(x) for x in values]

        def grads(chunks, *more):
            return backward(idx, tiles, text_sees, queries, grad_out, keys, values, stats, chunks, *more)

        second, first = grads((2, 1))
        third, total, merged = grads((3, 0), parts)
        far = [to_t[2](second), to_t[1](first), to_t[3](third)]
        mine = swap8(merged).reshape(queries.shape[0], -1)
        for x in far:
            total = total + x.astype(F32)
        total = total.astype(BF)
        rows = total.shape[0] // 2
        near, other = total[:rows], total[rows:]
        side, ahead, across = to_c(other), to_h(near), to_hc(other)
        key_near, value_near = fetch_weights(key_weight, value_weight, total)
        mine, side = lax.optimization_barrier((mine, side))
        theirs = to_c(mine)
        grad_feats, attn_out = feature_grad(
            idx, near, side, ahead, across, key_near, value_near, mine
        )
        attn_out = add_theirs(idx, attn_out, theirs)
        return attn_out, grad_feats

    placed = (
        P(("img", "txt"), "head"),
        P("head", None),
        P("head", None),
        P("txt", "head"),
        P("txt", "head"),
        P("img"),
        P(),
    )
    return jax.shard_map(
        shards,
        mesh=mesh,
        in_specs=placed,
        out_specs=(P("txt", "head"), P(("img", "txt"), "head")),
        check_vma=False,
    )
```

```python
import math

import jax
import jax.numpy as jnp
from jax import lax
from jax.experimental import pallas as pl
from jax.experimental.pallas import tpu as pltpu
from jax.sharding import PartitionSpec as P

HD = 128
TILE = 128
TBLK = 128
BF = jnp.bfloat16
F32 = jnp.float32
SCALE = 1.0 / math.sqrt(HD)
C2 = SCALE * math.log2(math.e)
NEG = -1e30
TOP = 3e38
AXES = ("img", "head", "txt")
NT = (((1,), (1,)), ((), ()))


def dot_nt(a, b):
    return lax.dot_general(a, b, NT, preferred_element_type=F32)


def dot_nn(a, b):
    return jnp.dot(a, b, preferred_element_type=F32)


def moved(sizes, where):
    ni, nh, nt = sizes
    pairs = []
    for i in range(ni):
        for h in range(nh):
            for t in range(nt):
                a, b, c = where(i, h, t)
                pairs.append(((i * nh + h) * nt + t, (a * nh + b) * nt + c))
    return lambda x: lax.ppermute(x, AXES, pairs)


def cost(us):
    return pl.CostEstimate(flops=int(us * 1.1e9), transcendentals=0, bytes_accessed=1 << 16)


def spec(shape):
    zeros = (0,) * len(shape)
    return pl.BlockSpec(shape, lambda *_: zeros)


def in_hbm(x):
    return pltpu.with_memory_space_constraint(x, pltpu.HBM)


def project(idx, count, feats, key_weight, value_weight):
    rows, feat = feats.shape
    cols = key_weight.shape[1]
    steps = 5
    chunk = feat // steps

    def body(ix, x_hbm, wk_hbm, wv_hbm, k0, kc, kh, khc, v0, vc, vh, vhc, x, wk, wv, acc, sems):
        copies = []
        for s in range(steps):
            at = slice(s * chunk, (s + 1) * chunk)
            copies.append(
                (
                    pltpu.make_async_copy(x_hbm.at[:, at], x.at[s], sems.at[0, s]),
                    pltpu.make_async_copy(wk_hbm.at[at, :], wk.at[s], sems.at[1, s]),
                    pltpu.make_async_copy(wv_hbm.at[at, :], wv.at[s], sems.at[2, s]),
                )
            )
            for copy in copies[s]:
                copy.start()
        for s in range(steps):
            for copy in copies[s]:
                copy.wait()
            key = dot_nn(x[s], wk[s])
            value = dot_nn(x[s], wv[s])
            if s == 0:
                acc[0] = key
                acc[1] = value
            else:
                acc[0] += key
                acc[1] += value
        h = ix[0]
        c = ix[1]

        def piece(which, hh, cc):
            at = pl.multiple_of((hh * 2 + cc) * HD, HD)
            return acc[which, :, pl.ds(at, HD)]

        for which, refs in ((1, (v0, vh, vhc, vc)), (0, (k0, kh, khc, kc))):
            for ref, (hh, cc) in zip(refs, ((h, c), (1 - h, c), (1 - h, 1 - c), (h, 1 - c))):
                ref[:rows, :] = piece(which, hh, cc).astype(ref.dtype)
        lane = lax.broadcasted_iota(jnp.int32, (extra, HD), 1)
        ids = jnp.zeros((extra, HD), F32)
        for e in range(count):
            ids = jnp.where(lane == e, ix[4 + e].astype(F32), ids)
        vc[rows:, :] = ids.astype(BF)

    extra = 16
    key = jax.ShapeDtypeStruct((rows, HD), F32)
    value = jax.ShapeDtypeStruct((rows, HD), BF)
    marked = jax.ShapeDtypeStruct((rows + extra, HD), BF)
    outs = (key, key, key, key, key, marked, value, value)
    return pl.pallas_call(
        body,
        out_shape=outs,
        grid_spec=pltpu.PrefetchScalarGridSpec(
            num_scalar_prefetch=1,
            grid=(1,),
            in_specs=[pl.BlockSpec(memory_space=pltpu.HBM)] * 3,
            out_specs=[spec(o.shape) for o in outs],
            scratch_shapes=[
                pltpu.VMEM((steps, rows, chunk), BF),
                pltpu.VMEM((steps, chunk, cols), BF),
                pltpu.VMEM((steps, chunk, cols), BF),
                pltpu.VMEM((2, rows, cols), F32),
                pltpu.SemaphoreType.DMA((3, steps)),
            ],
        ),
        compiler_params=pltpu.CompilerParams(vmem_limit_bytes=24 << 20),
        name="project",
        cost_estimate=cost(4),
    )(idx, in_hbm(feats), in_hbm(key_weight), in_hbm(value_weight))


def tile_cap(ix, tiles, sees, block, chunk, tile):
    half, j = divmod(tile, 2)
    shard = jnp.bitwise_xor(ix[2], chunk)
    image = tiles[half, shard * 2 + j]
    row = ix[2] * 2 + block
    return jnp.where(sees[row, image] > 0, jnp.float32(TOP), jnp.float32(NEG))


def forward(idx, tiles, sees, queries, grad_out, keys, values):
    rows = queries.shape[0]
    heads = 8
    width = heads * HD
    span = keys[0].shape[0]
    n = len(keys)
    total = span * n
    share = rows // 8
    per = span // TILE

    def body(ix, tl, se, q, g, k3, k2, k1, k0, v0, v1, v2, v3, out, st_out, y_scr, va):
        ks = (k0, k1, k2, k3)
        vs = (v0, v1, v2, v3)
        for j in range(n):
            va[j * span : (j + 1) * span, :HD] = vs[j][...]
        va[:, HD:] = jnp.ones((total, HD), BF)
        caps = [
            [tile_cap(ix, tl, se, b, j, e) for j in range(n) for e in range(per)]
            for b in range(2)
        ]
        lane = lax.broadcasted_iota(jnp.int32, (rows, HD), 1)
        st = jnp.zeros((rows, HD), F32)
        for h in range(heads):
            cols = slice(h * HD, (h + 1) * HD)
            slot = h % 2
            qh = q[:, cols]
            best = [None, None]
            for j in range(n):
                s = dot_nt(qh, ks[j][...]) * C2
                for b in range(2):
                    for e in range(per):
                        y = jnp.minimum(
                            s[b * TBLK : (b + 1) * TBLK, e * TILE : (e + 1) * TILE],
                            caps[b][j * per + e],
                        )
                        at = j * span + e * TILE
                        y_scr[slot, b * TBLK : (b + 1) * TBLK, at : at + TILE] = y
                        best[b] = y if best[b] is None else jnp.maximum(best[b], y)
            m = jnp.max(jnp.concatenate(best, axis=0), axis=1, keepdims=True)
            p = jnp.exp2(y_scr[slot] - m).astype(BF)
            r = dot_nn(p, va[...])
            den = r[:, HD:]
            o = r[:, :HD] / den
            out[:, :, cols] = o.astype(BF).reshape(8, share, HD)
            lse = m + jnp.log2(den)
            delta = jnp.sum(o * g[:, cols].astype(F32), axis=1, keepdims=True)
            st = jnp.where(lane == h, lse, st)
            st = jnp.where(lane == heads + h, delta, st)
        flat = st.T[: 2 * heads, :]
        for i in range(8):
            st_out[i] = flat

    own = lambda i, ix, tl, se: (0, ix[1])
    return pl.pallas_call(
        body,
        out_shape=(
            jax.ShapeDtypeStruct((8, share, width), BF),
            jax.ShapeDtypeStruct((8, 2 * heads, rows), F32),
        ),
        grid_spec=pltpu.PrefetchScalarGridSpec(
            num_scalar_prefetch=3,
            grid=(1,),
            in_specs=[pl.BlockSpec((rows, width), own)] * 2 + [spec((span, HD))] * 8,
            out_specs=[spec((8, share, width)), spec((8, 2 * heads, rows))],
            scratch_shapes=[
                pltpu.VMEM((2, rows, total), F32),
                pltpu.VMEM((total, 2 * HD), BF),
            ],
        ),
        compiler_params=pltpu.CompilerParams(vmem_limit_bytes=24 << 20),
        name="fwd",
        cost_estimate=cost(7),
    )(idx, tiles, sees, queries, grad_out, *keys[::-1], *values)


def merge_weights(st, heads):
    stats = [st[i] for i in range(8)]
    top = stats[0][:heads]
    for x in stats[1:]:
        top = jnp.maximum(top, x[:heads])
    ws = [jnp.exp2(x[:heads] - top) for x in stats]
    total = ws[0]
    delta = ws[0] * stats[0][heads:]
    for w, x in zip(ws[1:], stats[1:]):
        total = total + w
        delta = delta + w * x[heads:]
    inv = 1.0 / total
    return top + jnp.log2(total), delta * inv, [w * inv for w in ws]


def merge_parts(ix, x, ws, out, w_scr):
    _, share, width = x.shape
    heads = width // HD
    rows = w_scr.shape[0]
    pad = [jnp.zeros((HD - 8 * heads, rows), F32)]
    w_scr[...] = jnp.concatenate(ws + pad, axis=0).T
    w = w_scr[pl.ds(pl.multiple_of(ix[3] * share, share), share), :]
    for h in range(heads):
        cols = slice(h * HD, (h + 1) * HD)
        acc = jnp.zeros((share, HD), F32)
        for i in range(8):
            acc += x[i, :, cols].astype(F32) * w[:, i * heads + h : i * heads + h + 1]
        v = acc.astype(BF)
        for i in range(8):
            out[i, :, cols] = v


def backward(idx, tiles, sees, queries, grad_out, keys, values, stats, chunks, parts=None):
    rows = queries.shape[0]
    heads = 8
    width = heads * HD
    span = keys[0].shape[0]
    per = span // TILE
    n = len(chunks)

    def body(ix, tl, se, q, g, st, *refs):
        k_refs, v_refs, refs = refs[:n], refs[n : 2 * n], refs[2 * n :]
        lse, delta, ws = merge_weights(st, heads)
        if parts is None:
            outs, (dk, dv) = refs[:n], refs[n:]
        else:
            x, outs, (merged, dk, dv, w_scr) = refs[0], refs[1 : n + 1], refs[n + 1 :]
        lane = lax.broadcasted_iota(jnp.int32, (1, rows), 1)
        for chunk, k_ref, v_ref, out in zip(chunks, k_refs, v_refs, outs):
            caps = [
                jnp.where(
                    lane < TBLK,
                    tile_cap(ix, tl, se, 0, chunk, e),
                    tile_cap(ix, tl, se, 1, chunk, e),
                )
                for e in range(per)
            ]
            kk = k_ref[...]
            vv = v_ref[...]
            for h in range(heads):
                cols = slice(h * HD, (h + 1) * HD)
                qh = q[:, cols]
                gh = g[:, cols]
                s = dot_nt(kk, qh) * C2
                d = dot_nt(vv, gh)
                lh = lse[h : h + 1, :]
                dh = delta[h : h + 1, :]
                ps = []
                ds = []
                for e in range(per):
                    at = slice(e * TILE, (e + 1) * TILE)
                    p = jnp.exp2(jnp.minimum(s[at, :], caps[e]) - lh)
                    ps.append(p.astype(BF))
                    ds.append((p * (d[at, :] - dh) * SCALE).astype(BF))
                pv = dot_nn(jnp.concatenate(ps, axis=0), gh)
                pk = dot_nn(jnp.concatenate(ds, axis=0), qh)
                if h == 0:
                    dv[...] = pv
                    dk[...] = pk
                else:
                    dv[...] += pv
                    dk[...] += pk
            out[:, :HD] = dk[...].astype(out.dtype)
            out[:, HD:] = dv[...].astype(out.dtype)
        if parts is not None:
            merge_parts(ix, x, ws, merged, w_scr)

    own = lambda i, ix, tl, se: (0, ix[1])
    out_shape = [jax.ShapeDtypeStruct((span, 2 * HD), BF if k else F32) for k in chunks]
    in_specs = [pl.BlockSpec((rows, width), own)] * 2 + [spec(stats.shape)] + [spec((span, HD))] * (2 * n)
    out_specs = [spec((span, 2 * HD))] * n
    scratch = [pltpu.VMEM((span, HD), F32)] * 2
    more = []
    if parts is not None:
        more.append(parts)
        in_specs.append(spec(parts.shape))
        out_shape.append(jax.ShapeDtypeStruct(parts.shape, BF))
        out_specs.append(spec(parts.shape))
        scratch.append(pltpu.VMEM((rows, HD), F32))
    return pl.pallas_call(
        body,
        out_shape=out_shape,
        grid_spec=pltpu.PrefetchScalarGridSpec(
            num_scalar_prefetch=3,
            grid=(1,),
            in_specs=in_specs,
            out_specs=out_specs,
            scratch_shapes=scratch,
        ),
        compiler_params=pltpu.CompilerParams(vmem_limit_bytes=20 << 20),
        name="grads" + "".join(map(str, chunks)),
        cost_estimate=cost(3 * n),
    )(idx, tiles, sees, queries, grad_out, stats, *[keys[k] for k in chunks], *[values[k] for k in chunks], *more)


def fetch_weights(key_weight, value_weight, token):
    rows = key_weight.shape[0]
    steps = 4
    chunk = rows // steps

    def body(k_hbm, v_hbm, _, k_out, v_out, sems):
        copies = []
        for s in range(steps):
            at = slice(s * chunk, (s + 1) * chunk)
            copies.append(pltpu.make_async_copy(k_hbm.at[at, :], k_out.at[at, :], sems.at[0, s]))
            copies.append(pltpu.make_async_copy(v_hbm.at[at, :], v_out.at[at, :], sems.at[1, s]))
        for copy in copies:
            copy.start()
        for copy in copies:
            copy.wait()

    hbm = pl.BlockSpec(memory_space=pltpu.HBM)
    vmem = pl.BlockSpec(memory_space=pltpu.VMEM)
    return pl.pallas_call(
        body,
        out_shape=(
            pltpu.VMEM(key_weight.shape, BF),
            pltpu.VMEM(value_weight.shape, BF),
        ),
        in_specs=[hbm, hbm, pl.BlockSpec(memory_space=pl.ANY)],
        out_specs=[vmem, vmem],
        scratch_shapes=[pltpu.SemaphoreType.DMA((2, steps))],
        compiler_params=pltpu.CompilerParams(vmem_limit_bytes=2 << 20),
        name="fetch",
        cost_estimate=cost(4),
    )(in_hbm(key_weight), in_hbm(value_weight), token)


def feature_grad(idx, own, oc, oh, ohc, key_weight, value_weight, mine):
    rows = own.shape[0]
    feat, cols = key_weight.shape
    steps = 5
    chunk = feat // steps
    half = mine.shape[1]

    def body(ix, a, b, c_, d_, wk, wv, m_ref, out_hbm, attn, both, out, sems):
        h = ix[0]
        c = ix[1]

        mine_at = attn.at[:, pl.ds(pl.multiple_of(c * half, half), half)]
        place = pltpu.make_async_copy(m_ref, mine_at, sems.at[1, 0])

        def store(s):
            at = slice(s * chunk, (s + 1) * chunk)
            return pltpu.make_async_copy(out.at[s], out_hbm.at[:, at], sems.at[0, s])

        place.start()

        def put(hh, cc, x):
            at = pl.multiple_of((hh * 2 + cc) * HD, HD)
            both[0, :, pl.ds(at, HD)] = x[:, :HD]
            both[1, :, pl.ds(at, HD)] = x[:, HD:]

        put(h, c, a)
        put(h, 1 - c, b)
        put(1 - h, c, c_)
        put(1 - h, 1 - c, d_)
        for s in range(steps):
            at = slice(s * chunk, (s + 1) * chunk)
            out[s] = (dot_nt(both[0], wk[at, :]) + dot_nt(both[1], wv[at, :])).astype(BF)
            store(s).start()
        for s in range(steps):
            store(s).wait()
        place.wait()

    piece = spec((rows, 2 * HD))
    hbm = pl.BlockSpec(memory_space=pltpu.HBM)
    vmem = pl.BlockSpec(memory_space=pltpu.VMEM)
    anywhere = pl.BlockSpec(memory_space=pl.ANY)
    return pl.pallas_call(
        body,
        out_shape=(
            jax.ShapeDtypeStruct((rows, feat), BF),
            jax.ShapeDtypeStruct((rows, 2 * half), BF),
        ),
        grid_spec=pltpu.PrefetchScalarGridSpec(
            num_scalar_prefetch=1,
            grid=(1,),
            in_specs=[piece] * 4 + [vmem] * 2 + [anywhere],
            out_specs=[hbm, hbm],
            scratch_shapes=[
                pltpu.VMEM((2, rows, cols), BF),
                pltpu.VMEM((steps, rows, chunk), BF),
                pltpu.SemaphoreType.DMA((2, steps)),
            ],
        ),
        compiler_params=pltpu.CompilerParams(vmem_limit_bytes=8 << 20),
        name="feats",
        cost_estimate=cost(4),
    )(idx, own, oc, oh, ohc, key_weight, value_weight, mine)


def add_theirs(idx, attn, theirs):
    half = theirs.shape[1]

    def body(ix, _, t_ref, out, sem):
        at = pl.multiple_of((1 - ix[1]) * half, half)
        copy = pltpu.make_async_copy(t_ref, out.at[:, pl.ds(at, half)], sem)
        copy.start()
        copy.wait()

    hbm = pl.BlockSpec(memory_space=pltpu.HBM)
    return pl.pallas_call(
        body,
        out_shape=jax.ShapeDtypeStruct(attn.shape, BF),
        grid_spec=pltpu.PrefetchScalarGridSpec(
            num_scalar_prefetch=1,
            grid=(1,),
            in_specs=[hbm, pl.BlockSpec(memory_space=pl.ANY)],
            out_specs=hbm,
            scratch_shapes=[pltpu.SemaphoreType.DMA],
        ),
        input_output_aliases={1: 0},
        compiler_params=pltpu.CompilerParams(vmem_limit_bytes=1 << 20),
        name="theirs",
    )(idx, attn, theirs)


def solution(mesh):
    sizes = tuple(mesh.shape[a] for a in AXES)
    to_c = moved(sizes, lambda i, h, t: (i ^ 1, h, t))
    to_h = moved(sizes, lambda i, h, t: (i, 1 - h, t))
    to_hc = moved(sizes, lambda i, h, t: (i ^ 1, 1 - h, t))
    to_t = {k: moved(sizes, lambda i, h, t, k=k: (i, h, t ^ k)) for k in (1, 2, 3)}
    chips = [[m * 2 + c for m in range(8)] for c in range(2)]

    def swap8(x):
        return lax.all_to_all(x, "img", 0, 0, axis_index_groups=chips, tiled=True)

    def gathered(own):
        return [own] + [to_t[k](own) for k in (1, 2, 3)]

    def shards(image_feats, key_weight, value_weight, queries, grad_out, tile_image, text_sees):
        img = lax.axis_index("img")
        core = img % 2
        idx = jnp.stack([lax.axis_index("head"), core, lax.axis_index("txt"), img // 2]).astype(jnp.int32)
        idx = jnp.concatenate([idx, tile_image])
        own_k, c_k, h_k, hc_k, own_v, c_v, h_v, hc_v = project(
            idx, tile_image.shape[0], image_feats, key_weight, value_weight
        )
        h_v, hc_v, c_v = to_h(h_v), to_hc(hc_v), to_c(c_v)
        h_k, hc_k, c_k = to_h(h_k), to_hc(hc_k), to_c(c_k)
        rows = h_v.shape[0]
        others = c_v[rows, : tile_image.shape[0]].astype(jnp.int32)
        tiles = jnp.stack([tile_image, others])

        def owned(own, h, c, hc):
            near = own + h.astype(F32)
            far = c[:rows].astype(F32) + hc.astype(F32)
            return jnp.concatenate([near.astype(BF), far.astype(BF)], axis=0)

        values = gathered(owned(own_v, h_v, c_v, hc_v))
        keys = gathered(owned(own_k, h_k, c_k, hc_k))
        parts, stats = forward(idx, tiles, text_sees, queries, grad_out, keys, values)
        stats = swap8(stats)
        parts = swap8(parts)

        keys = [in_hbm(x) for x in keys]
        values = [in_hbm(x) for x in values]

        def grads(chunks, *more):
            return backward(idx, tiles, text_sees, queries, grad_out, keys, values, stats, chunks, *more)

        second, first = grads((2, 1))
        third, total, merged = grads((3, 0), parts)
        far = [to_t[2](second), to_t[1](first), to_t[3](third)]
        mine = swap8(merged).reshape(queries.shape[0], -1)
        for x in far:
            total = total + x.astype(F32)
        total = total.astype(BF)
        rows = total.shape[0] // 2
        near, other = total[:rows], total[rows:]
        side, ahead, across = to_c(other), to_h(near), to_hc(other)
        key_near, value_near = fetch_weights(key_weight, value_weight, total)
        mine, side = lax.optimization_barrier((mine, side))
        theirs = to_c(mine)
        grad_feats, attn_out = feature_grad(
            idx, near, side, ahead, across, key_near, value_near, mine
        )
        attn_out = add_theirs(idx, attn_out, theirs)
        return attn_out, grad_feats

    placed = (
        P(("img", "txt"), "head"),
        P("head", None),
        P("head", None),
        P("txt", "head"),
        P("txt", "head"),
        P("img"),
        P(),
    )
    return jax.shard_map(
        shards,
        mesh=mesh,
        in_specs=placed,
        out_specs=(P("txt", "head"), P(("img", "txt"), "head")),
        check_vma=False,
    )
```
